32 devices in a mesh: slab: 8 (over y, x, core), cross: 4 (over z).
Axes of the slice: x: 2, y: 2, z: 4, core: 2. Of those that a mesh axis runs over, the one named last changes fastest.
Arguments:
- positions: float32 [3, 4096], P(None, ('slab', 'cross')), as said below
- velocities: float32 [3, 4096], P(None, ('slab', 'cross')), may hold values from -3 to 3
- inverse_mass: float32 [4096], P(('slab', 'cross')), may hold values from 0.0625 to 1
- species: int32 [4096], P(('slab', 'cross')), may hold values from 0 to 7
- type_table: float32 [8, 128], replicated, may hold values from -5 to 5
- neighbours: int32 [4096, 16], P(('slab', 'cross')), may hold values from 0 to 639, as said below
- slot_count: int32 [4096], P(('slab', 'cross')), may hold values from 0 to 16, as said below
- atom_count: int32 [32], P(('slab', 'cross')), may hold values from 96 to 128
- pair_bins: int32 [4096, 16], P(('slab', 'cross')), may hold values from 0 to 127
- send_list: int32 [16, 8, 32], P('slab', 'cross'), may hold values from 0 to 127, as said below
- target: float32 [128], replicated, may hold values from 0 to 0.5
- encoder: float32 [128, 128], replicated, may hold values from -0.5 to 0.5
- spreader: float32 [128, 256], replicated, may hold values from -0.5 to 0.5
- filters: float32 [20, 256], replicated, may hold values from -1.25 to 1.25
- rotator: float32 [128, 128], replicated, may hold values from -0.5 to 0.5
- reflector: float32 [128, 128], replicated, may hold values from -0.5 to 0.5
- combiner: float32 [256, 128], replicated, may hold values from -0.375 to 0.375
- splitter: float32 [128, 256], replicated, may hold values from -0.5 to 0.5
- readout: float32 [128, 128], replicated, may hold values from -0.5 to 0.5
- collector: float32 [128], replicated, may hold values from -0.5 to 0.5
Outputs:
- next_positions: float32 [3, 4096], P(None, ('slab', 'cross'))
- position_adjoint: float32 [3, 4096], P(None, ('slab', 'cross'))
- encoder_grad: float32 [128, 128], P('cross')
- spreader_grad: float32 [128, 256], P('cross')
- filters_grad: float32 [20, 256], P(None, 'cross')
- rotator_grad: float32 [128, 128], P('cross')
- reflector_grad: float32 [128, 128], P('cross')
- combiner_grad: float32 [256, 128], P('cross')
- splitter_grad: float32 [128, 256], P('cross')
- readout_grad: float32 [128, 128], P('cross')
- collector_grad: float32 [128], P('cross')
The draws below stay inside these ranges and needn't reach their ends.
Inputs may be any that keep to these rules, and one draw needn't show every extreme that they name: `neighbours`: rows of the device's pool; a live slot never names the atom itself, a dead atom, or a block (p, q) with p and q both in 1..2; live slots come before dead ones. `slot_count`: 0 for atoms at or beyond the device's atom_count. The four blocks send_list[2 s + a, 2 c + b], a and b in 0..1, of device (s, c) list each of its 128 atom rows exactly once. `positions`: A device's atoms lie in its local box of 10 by 10 by 1.6 * 8 Angstrom.
All inputs are finite; a program needn't handle non-finite values.
Results may differ from the reference program's by a relative error of at most 0.0003.
Values sent between devices are 32-bit elements; how exact they have to be, the bound alone decides.
No kernel may reach another device: no remote copies, remote signals or barrier semaphores. Data moves between devices by JAX's collectives and lax.ppermute only.
A program may use at most 128 MiB of HBM per device.

```python
import math
import jax
import jax.numpy as jnp
import numpy as np
from jax import lax

FEAT = 128
RBF = 20
TYPES = 8
SLOTS = 16
BINS = 128
A_DEV = 128
GHOST = 32
DEPTH_SITES = 8
ATOMS = 4096
N_SLAB = 8
N_CROSS = 4


def candidate_table():
    entries = []
    for slab_step in (-1, 0, 1):
        for cross_step in (-1, 0, 1):
            for depth_step in range(-3, 4):
                if slab_step != 0 or cross_step != 0 or depth_step != 0:
                    entries.append((slab_step, cross_step, depth_step))
    entries.append((-2, 0, 0))
    entries.append((2, 0, 0))
    return np.array(entries, dtype=np.int64)


def static_layout():
    depth_sites = A_DEV // 16
    ghost_rows = A_DEV // 4
    sites = np.arange(A_DEV)
    site_slab = sites // (4 * depth_sites)
    site_cross = sites // depth_sites % 4
    site_depth = sites % depth_sites
    steps_table = candidate_table()
    moved_slab = site_slab[:, None] + steps_table[None, :, 0]
    moved_cross = site_cross[:, None] + steps_table[None, :, 1]
    moved_depth = (site_depth[:, None] + steps_table[None, :, 2]) % depth_sites
    slab_move = moved_slab // 4
    cross_move = moved_cross // 4
    inner_slab = moved_slab - 4 * slab_move
    inner_cross = moved_cross - 4 * cross_move
    target_site = (inner_slab * 4 + inner_cross) * depth_sites + moved_depth
    block_row = np.where(slab_move < 0, 0, np.where(slab_move > 0, 3, 1 + inner_slab // 2))
    block_col = np.where(cross_move < 0, 0, np.where(cross_move > 0, 3, 1 + inner_cross // 2))
    within = (inner_slab % 2 * 2 + inner_cross % 2) * depth_sites + moved_depth
    pool_slot = A_DEV + (block_row * 4 + block_col) * ghost_rows + within
    at_home = (slab_move == 0) & (cross_move == 0)
    squares = 625 * (steps_table[:, 0] ** 2 + steps_table[:, 1] ** 2) + 256 * steps_table[:, 2] ** 2
    base_bins = squares * BINS // 3600
    slot_ids = np.arange(ghost_rows)
    inner_a = slot_ids // (2 * depth_sites)
    inner_b = slot_ids // depth_sites % 2
    slot_depth = slot_ids % depth_sites
    quad_sites = np.zeros((2, 2, ghost_rows), dtype=np.int64)
    for half_a in range(2):
        for half_b in range(2):
            quad_sites[half_a, half_b] = ((2 * half_a + inner_a) * 4 + 2 * half_b + inner_b) * depth_sites + slot_depth
    coords = np.stack([(site_slab + 0.5) * 2.5, (site_cross + 0.5) * 2.5, (site_depth + 0.5) * 1.6]).astype(np.float32)
    return (slab_move, cross_move, target_site, pool_slot, at_home, base_bins, quad_sites, coords)


def shuffle_sites(subkey):
    return jax.random.permutation(subkey, A_DEV).astype(jnp.int32)


def lattice(key):
    base = jax.random.fold_in(key, 4242)
    devices = N_SLAB * N_CROSS
    slab_move, cross_move, target_site, pool_slot, at_home, base_bins, quad_sites, coords = static_layout()
    device_keys = jax.random.split(jax.random.fold_in(base, 1), devices)
    site_atom = jax.vmap(shuffle_sites)(device_keys)
    atom_site = jnp.argsort(site_atom, axis=1).astype(jnp.int32)
    counts = (A_DEV - jax.random.randint(jax.random.fold_in(base, 2), (devices,), 0, A_DEV // 4 + 1)).astype(jnp.int32)
    counts = counts.at[0].set(A_DEV).at[1].set(A_DEV - A_DEV // 4)
    device_ids = jnp.arange(devices, dtype=jnp.int32)
    slab_pos = device_ids // N_CROSS
    cross_pos = device_ids % N_CROSS
    source = (slab_pos[:, None, None] + jnp.asarray(slab_move, jnp.int32)[None]) % N_SLAB * N_CROSS + (cross_pos[:, None, None] + jnp.asarray(cross_move, jnp.int32)[None]) % N_CROSS
    source_atom = site_atom[source, jnp.asarray(target_site, jnp.int32)[None]]
    alive = (source_atom < counts[source]).astype(jnp.int32)
    pool_index = jnp.where(jnp.asarray(at_home)[None], source_atom, jnp.asarray(pool_slot, jnp.int32)[None])
    self_live = site_atom < counts[:, None]
    scores = jax.random.randint(jax.random.fold_in(base, 3), (devices, A_DEV, 64), 0, 2 ** 20)
    sort_keys = (1 - alive) * 2 ** 27 + scores * 64 + jnp.arange(64, dtype=jnp.int32)
    order = jnp.argsort(sort_keys, axis=-1)[:, :, :SLOTS]
    chosen = jnp.take_along_axis(pool_index, order, axis=-1)
    jitter = jax.random.randint(jax.random.fold_in(base, 4), (devices, A_DEV, 64), -1, 2)
    all_bins = jnp.clip(jnp.asarray(base_bins, jnp.int32)[None, None, :] + jitter, 0, BINS - 1)
    chosen_bins = jnp.take_along_axis(all_bins, order, axis=-1)
    live_total = jnp.sum(alive, axis=-1)
    slot_site = jnp.where(self_live, jnp.minimum(live_total, SLOTS), 0)
    lists = jnp.take_along_axis(chosen, atom_site[:, :, None], axis=1).reshape(devices * A_DEV, SLOTS)
    bins = jnp.take_along_axis(chosen_bins, atom_site[:, :, None], axis=1).reshape(devices * A_DEV, SLOTS)
    slots_used = jnp.take_along_axis(slot_site, atom_site, axis=1).reshape(devices * A_DEV)
    sends = site_atom[:, jnp.asarray(quad_sites, jnp.int32)]
    sends = sends.reshape(N_SLAB, N_CROSS, 2, 2, A_DEV // 4).transpose(0, 2, 1, 3, 4).reshape(2 * N_SLAB, 2 * N_CROSS, A_DEV // 4)
    return (lists.astype(jnp.int32), slots_used.astype(jnp.int32), counts, bins.astype(jnp.int32), sends.astype(jnp.int32), atom_site, coords)


def draw_neighbours(key, part):
    return lattice(key)[0]


def draw_slot_count(key, part):
    return lattice(key)[1]


def draw_atom_count(key, part):
    return lattice(key)[2]


def draw_pair_bins(key, part):
    return lattice(key)[3]


def draw_send_list(key, part):
    return lattice(key)[4]


def draw_positions(key, part):
    pieces = lattice(key)
    atom_site = pieces[5]
    coords = jnp.asarray(pieces[6], jnp.float32)
    devices = N_SLAB * N_CROSS
    jitter_key = jax.random.fold_in(key, 77)
    jitter = jnp.clip(0.12 * jax.random.normal(jitter_key, (devices, 3, A_DEV), jnp.float32), -0.3, 0.3)
    site_coords = coords[None] + jitter
    atom_coords = jnp.take_along_axis(site_coords, atom_site[:, None, :], axis=2)
    return atom_coords.transpose(1, 0, 2).reshape(3, devices * A_DEV).astype(jnp.float32)


def set_ends(result, own_key, low, high):
    spot = [jax.random.randint(jax.random.fold_in(own_key, axis), (), 0, length) for axis, length in enumerate(result.shape)]
    longest = result.shape.index(max(result.shape))
    beside = spot[:longest] + [(spot[longest] + 1) % result.shape[longest]] + spot[longest + 1:]
    return result.at[tuple(spot)].set(low).at[tuple(beside)].set(high)


def shard_levels(rng, shape, cuts, smallest, high):
    def one(position, shards_of):
        steps = jax.random.uniform(jax.random.fold_in(jax.random.fold_in(rng, 6), position), (shards_of,), jnp.float32, smallest / len(cuts), high / len(cuts))
        return jnp.repeat(jnp.exp(steps), shape[position] // shards_of).reshape((-1,) + (1,) * (len(shape) - position - 1))

    loudness = one(*cuts[0])
    for cut in cuts[1:]:
        loudness = loudness * one(*cut)
    return loudness


def centred(stream_key, dims, spread, bound, shards=(), held_as=jnp.bfloat16):
    values = jax.random.normal(stream_key, dims, jnp.float32) * spread
    if len(shards) > 0:
        values = shard_levels(stream_key, dims, shards, -0.22, 0.18) * values
    return jnp.clip(values, min=-bound, max=bound).astype(held_as)


def setup_inputs(seed: int = 0) -> dict:
    keys = jax.random.split(jax.random.key(seed), 21)
    return {
        "positions": draw_positions(jax.random.fold_in(keys[20], 71), 0),
        "velocities": centred(keys[1], (3, ATOMS), 0.5, 3.0, ((1, 32),), jnp.float32),
        "inverse_mass": jnp.clip(jnp.exp(math.log(1.0) - 2.7725887 * jax.random.uniform(keys[2], (ATOMS,), jnp.float32) ** shard_levels(keys[2], (ATOMS,), ((0, 32),), -0.2, 0.2)), 0.0625, 1.0),
        "species": set_ends(jax.random.randint(keys[3], (ATOMS,), 0, TYPES), jax.random.fold_in(keys[3], 1), 0, TYPES - 1).astype(jnp.int32),
        "type_table": centred(keys[4], (TYPES, FEAT), 1.0, 5.0, (), jnp.float32),
        "neighbours": draw_neighbours(jax.random.fold_in(keys[20], 71), 0),
        "slot_count": draw_slot_count(jax.random.fold_in(keys[20], 71), 0),
        "atom_count": draw_atom_count(jax.random.fold_in(keys[20], 71), 0),
        "pair_bins": draw_pair_bins(jax.random.fold_in(keys[20], 71), 0),
        "send_list": draw_send_list(jax.random.fold_in(keys[20], 71), 0),
        "target": jnp.clip(jax.random.uniform(keys[10], (BINS,), jnp.float32, 0.0, 0.5), 0.0, 0.5),
        "encoder": centred(keys[11], (FEAT, FEAT), FEAT ** -0.5, 0.5, (), jnp.float32),
        "spreader": centred(keys[12], (FEAT, 2 * FEAT), FEAT ** -0.5, 0.5, (), jnp.float32),
        "filters": centred(keys[13], (RBF, 2 * FEAT), RBF ** -0.5, 1.25, (), jnp.float32),
        "rotator": centred(keys[14], (FEAT, FEAT), FEAT ** -0.5, 0.5, (), jnp.float32),
        "reflector": centred(keys[15], (FEAT, FEAT), FEAT ** -0.5, 0.5, (), jnp.float32),
        "combiner": centred(keys[16], (2 * FEAT, FEAT), (2 * FEAT) ** -0.5, 0.375, (), jnp.float32),
        "splitter": centred(keys[17], (FEAT, 2 * FEAT), FEAT ** -0.5, 0.5, (), jnp.float32),
        "readout": centred(keys[18], (FEAT, FEAT), FEAT ** -0.5, 0.5, (), jnp.float32),
        "collector": centred(keys[19], (FEAT,), FEAT ** -0.5, 0.5, (), jnp.float32),
    }


cutoff = 5.0
soften = 0.25
sigma_two = 0.18
slab_length = 10.0
cell_length = 10.0
time_step = 0.5
highest = lax.Precision.HIGHEST

def matmul(left, right):
    return jnp.dot(left, right, precision=highest, preferred_element_type=jnp.float32)

def geometry(own_coords, ghost_coords, neighbours, depth_length):
    atoms_here = neighbours.shape[0]
    slot_total = neighbours.shape[1]
    pool_coords = jnp.concatenate([own_coords, ghost_coords], axis=1)
    flat_lists = neighbours.reshape(atoms_here * slot_total)
    others = jnp.take(pool_coords, flat_lists, axis=1)
    owners = jnp.broadcast_to(own_coords[:, :, None], (3, atoms_here, slot_total)).reshape(3, atoms_here * slot_total)
    deltas = others - owners
    depth_part = deltas[2] - depth_length * jnp.floor(deltas[2] / depth_length + 0.5)
    deltas = jnp.stack([deltas[0], deltas[1], depth_part])
    radius = jnp.sqrt(lax.optimization_barrier(jnp.sum(deltas * deltas, axis=0)) + soften)
    return (deltas, radius)

def energy_local(weights, own_coords, ghost_coords, pool_features, neighbours, slot_mask, live_mask, depth_length):
    encoder, spreader, filters, rotator, reflector, combiner, splitter, readout, collector = weights
    atoms_here = own_coords.shape[1]
    slot_total = neighbours.shape[1]
    feature_width = pool_features.shape[1]
    deltas, radius = geometry(own_coords, ghost_coords, neighbours, depth_length)
    hidden = jax.nn.silu(matmul(pool_features, encoder))
    scalars = matmul(hidden, spreader)
    orders = jnp.arange(1, filters.shape[0] + 1, dtype=jnp.float32) * (jnp.pi / cutoff)
    radial_basis = jnp.sin(orders[:, None] * radius[None, :]) / radius[None, :]
    envelope = 0.5 * (jnp.cos(jnp.pi * jnp.minimum(radius, cutoff) / cutoff) + 1.0) * slot_mask.reshape(atoms_here * slot_total)
    filtered = jnp.einsum('rn,rc->nc', radial_basis, filters, precision=highest) * envelope[:, None]
    messages = (jnp.take(scalars, neighbours.reshape(atoms_here * slot_total), axis=0) * filtered).reshape(atoms_here, slot_total, 2 * feature_width)
    scalar_one = pool_features[:atoms_here] + lax.optimization_barrier(jnp.sum(messages[:, :, :feature_width], axis=1))
    units = (deltas / radius[None, :]).reshape(3, atoms_here, slot_total)
    vector_one = jnp.einsum('cak,akf->caf', units, messages[:, :, feature_width:], precision=highest)
    turned = jnp.einsum('caf,fg->cag', vector_one, rotator, precision=highest)
    mirrored = jnp.einsum('caf,fg->cag', vector_one, reflector, precision=highest)
    lengths = jnp.sqrt(lax.optimization_barrier(jnp.sum(mirrored * mirrored, axis=0)) + 1.0)
    joined = jnp.concatenate([scalar_one, lengths], axis=1)
    gate_values = matmul(jax.nn.silu(matmul(joined, combiner)), splitter)
    scalar_two = scalar_one + gate_values[:, :feature_width] + gate_values[:, feature_width:] * lax.optimization_barrier(jnp.sum(turned * mirrored, axis=0))
    energies = matmul(jax.nn.silu(matmul(scalar_two, readout)), collector[:, None])[:, 0]
    return jnp.sum(energies * live_mask)

def histogram_local(own_coords, ghost_coords, neighbours, slot_mask, pair_bins, depth_length, bin_total):
    atoms_here = neighbours.shape[0]
    slot_total = neighbours.shape[1]
    deltas, radius = geometry(own_coords, ghost_coords, neighbours, depth_length)
    flat_bins = pair_bins.reshape(atoms_here * slot_total)
    centre_of = 0.1 * jnp.sqrt(3600.0 * (flat_bins.astype(jnp.float32) + 0.5) / bin_total)
    kernel = jnp.exp(-(radius - centre_of) * (radius - centre_of) / sigma_two) * slot_mask.reshape(atoms_here * slot_total)
    return jax.ops.segment_sum(kernel, flat_bins, num_segments=bin_total)

def ghost_tables(send_list, slab_count, cross_count, atoms_here, ghost_rows):
    devices = slab_count * cross_count
    device_ids = jnp.arange(devices, dtype=jnp.int32)
    slab_pos = device_ids // cross_count
    cross_pos = device_ids % cross_count
    blocks = jnp.arange(16, dtype=jnp.int32)
    block_row = blocks // 4
    block_col = blocks % 4
    shift_row = (block_row == 3).astype(jnp.int32) - (block_row == 0).astype(jnp.int32)
    shift_col = (block_col == 3).astype(jnp.int32) - (block_col == 0).astype(jnp.int32)
    source_slab = (slab_pos[:, None] + shift_row[None, :]) % slab_count
    source_cross = (cross_pos[:, None] + shift_col[None, :]) % cross_count
    row_half = (block_row + 1) % 2
    col_half = (block_col + 1) % 2
    local_rows = send_list[2 * source_slab + row_half[None, :], 2 * source_cross + col_half[None, :]]
    global_rows = ((source_slab * cross_count + source_cross) * atoms_here)[:, :, None] + local_rows
    shifts = jnp.stack([shift_row.astype(jnp.float32) * slab_length, shift_col.astype(jnp.float32) * cell_length, jnp.zeros((16,), jnp.float32)])
    offsets = jnp.broadcast_to(shifts[:, :, None], (3, 16, ghost_rows)).reshape(3, 16 * ghost_rows)
    return (global_rows.reshape(devices, 16 * ghost_rows).astype(jnp.int32), offsets)

def reference(positions, velocities, inverse_mass, species, type_table, neighbours, slot_count, atom_count, pair_bins, send_list, target, encoder, spreader, filters, rotator, reflector, combiner, splitter, readout, collector):
    weights = (encoder, spreader, filters, rotator, reflector, combiner, splitter, readout, collector)
    atoms_here = A_DEV
    devices = N_SLAB * N_CROSS
    depth_length = 1.6 * DEPTH_SITES
    ghost_ids, offsets = ghost_tables(send_list, N_SLAB, N_CROSS, atoms_here, GHOST)
    features = matmul((species[:, None] == jnp.arange(TYPES, dtype=jnp.int32)).astype(jnp.float32), type_table)
    slot_mask_all = (jnp.arange(SLOTS, dtype=jnp.int32)[None, :] < slot_count[:, None]).astype(jnp.float32)
    device_list = jnp.arange(devices, dtype=jnp.int32)

    def device_pieces(coords, device):
        first_row = device * atoms_here
        own_coords = lax.dynamic_slice_in_dim(coords, first_row, atoms_here, 1)
        ghost_coords = jnp.take(coords, ghost_ids[device], axis=1) + offsets
        own_lists = lax.dynamic_slice_in_dim(neighbours, first_row, atoms_here, 0)
        own_masks = lax.dynamic_slice_in_dim(slot_mask_all, first_row, atoms_here, 0)
        return (first_row, own_coords, ghost_coords, own_lists, own_masks)

    def total_energy(coords, weight_set):

        def advance(running, device):
            first_row, own_coords, ghost_coords, own_lists, own_masks = device_pieces(coords, device)
            pool_features = jnp.concatenate([lax.dynamic_slice_in_dim(features, first_row, atoms_here, 0), jnp.take(features, ghost_ids[device], axis=0)], axis=0)
            live_mask = (jnp.arange(atoms_here, dtype=jnp.int32) < atom_count[device]).astype(jnp.float32)
            device_energy = energy_local(weight_set, own_coords, ghost_coords, pool_features, own_lists, own_masks, live_mask, depth_length)
            return (running + device_energy, None)
        summed, unused = lax.scan(jax.checkpoint(advance), jnp.zeros((), jnp.float32), device_list)
        return summed
    grad_energy = jax.grad(total_energy, argnums=0)
    forces = -grad_energy(positions, weights)
    kick_scale = 0.5 * time_step * time_step * inverse_mass
    next_positions = positions + time_step * velocities + kick_scale * forces

    def observable(coords):

        def advance(running, device):
            first_row, own_coords, ghost_coords, own_lists, own_masks = device_pieces(coords, device)
            own_bins = lax.dynamic_slice_in_dim(pair_bins, first_row, atoms_here, 0)
            counts = histogram_local(own_coords, ghost_coords, own_lists, own_masks, own_bins, depth_length, BINS)
            return (running + counts, None)
        histogram, unused = lax.scan(jax.checkpoint(advance), jnp.zeros((BINS,), jnp.float32), device_list)
        excess = histogram / ATOMS - target
        return jnp.sum(excess * excess)
    adjoint = jax.grad(observable)(next_positions)
    probe_weights = kick_scale * adjoint

    def directional(coords, weight_set):
        return jnp.sum(grad_energy(coords, weight_set) * probe_weights)
    coord_part, weight_part = jax.grad(directional, argnums=(0, 1))(positions, weights)
    position_adjoint = ATOMS * (adjoint - coord_part)
    return (next_positions, position_adjoint, -weight_part[0], -weight_part[1], -weight_part[2], -weight_part[3], -weight_part[4], -weight_part[5], -weight_part[6], -weight_part[7], -weight_part[8])
```

```python
import functools

import jax
import jax.numpy as jnp
from jax import lax
from jax.experimental import pallas as pl
from jax.experimental.pallas import tpu as pltpu
from jax.sharding import PartitionSpec as P

cutoff = 5.0
soften = 0.25
sigma_two = 0.18
slab_length = 10.0
cell_length = 10.0
time_step = 0.5
highest = lax.Precision.HIGHEST
f32 = jnp.float32
bf16 = jnp.bfloat16
pi = 3.141592653589793
omega = pi / cutoff

NN = ((1,), (0,))
NT = ((1,), (1,))
VM = pl.BlockSpec(memory_space=pltpu.VMEM)
SM = pl.BlockSpec(memory_space=pltpu.SMEM)


def call(body, outs, *args, specs=None, scratch=()):
    return pl.pallas_call(
        body,
        out_shape=[jax.ShapeDtypeStruct(s, d) for s, d in outs],
        in_specs=[VM] * len(args) if specs is None else specs,
        out_specs=[VM] * len(outs),
        scratch_shapes=list(scratch),
    )(*args)


def split(x):
    high = x.astype(bf16)
    return high, (x - high.astype(f32)).astype(bf16)


def dot1(a, b, dims):
    return lax.dot_general(a, b, (dims, ((), ())), preferred_element_type=f32)


def dot3(a, b, dims=NN):
    return dot1(a[0], b[0], dims) + (dot1(a[0], b[1], dims) + dot1(a[1], b[0], dims))


def cat(parts, axis):
    return jnp.concatenate(parts, axis=axis)


def iota(shape, dim):
    return lax.broadcasted_iota(jnp.int32, shape, dim)


def lane_take(row, index):
    return jnp.take_along_axis(jnp.broadcast_to(row, index.shape), index, axis=1)


def own_lanes(group, lanes):
    quarter = lanes // 4
    start = 2 * quarter * (1 - group // 2) + quarter * (1 - group % 2)
    return start, quarter


def pool_offsets(group, lanes):
    place = iota((1, lanes), 1)
    up, right = group // 2, group % 2
    half, quarter = lanes // 2, lanes // 4
    first = (place >= half) if up else (place < half)
    second_bit = place % half >= quarter
    second = second_bit if right else jnp.logical_not(second_bit)
    sign_u, sign_r = 2.0 * up - 1.0, 2.0 * right - 1.0
    return (
        jnp.where(first, sign_u * slab_length, 0.0).astype(f32),
        jnp.where(second, sign_r * cell_length, 0.0).astype(f32),
        None,
    )


def from_pool(rows, code, lanes):
    group = code // lanes
    lane = code % lanes
    out = lane_take(rows[0], lane)
    for j in range(1, 4):
        out = jnp.where(group == j, lane_take(rows[j], lane), out)
    return out


def pool_deltas(pool_rows, own_rows, code, lanes, depth):
    deltas = []
    for c in range(3):
        d = from_pool([pool_rows(j, c) for j in range(4)], code, lanes) - own_rows(c)
        if c == 2:
            d = d - depth * jnp.floor(d / depth + 0.5)
        deltas.append(d)
    radius = jnp.sqrt(deltas[0] * deltas[0] + deltas[1] * deltas[1] + deltas[2] * deltas[2] + soften)
    return deltas, radius


def one_hot_rows(index, slots, count):
    lanes = index.shape[1]
    place = iota((count, lanes), 0)
    return cat(
        [(place == index[k : k + 1, :]).astype(f32).astype(bf16) for k in range(slots)], 1
    )


def scatter_lanes(values, index, scratch, count):
    slots = index.shape[0]
    for row in range(16):
        value = values[row] if row < len(values) else None
        if value is None:
            value = jnp.zeros(index.shape, f32)
        scratch[pl.ds(row, slots, stride=16), :] = value
    highs, mids, lows = [], [], []
    for k in range(slots):
        x = scratch[16 * k : 16 * k + 16, :]
        high = x.astype(bf16)
        rest = x - high.astype(f32)
        mid = rest.astype(bf16)
        highs.append(high)
        mids.append(mid)
        lows.append((rest - mid.astype(f32)).astype(bf16))
    left = cat([cat(highs, 1), cat(mids, 1), cat(lows, 1)], 0)
    sums = dot1(left, one_hot_rows(index, slots, count), NT)
    return sums[0:16] + (sums[16:32] + sums[32:48])


def pool_partials(deltas_bar, code, send_index, out_ref, scratch, lanes):
    group = code // lanes
    lane = code % lanes
    values = []
    for j in range(4):
        for c in range(3):
            values.append(jnp.where(group == j, deltas_bar[c], 0.0))
        values.append(None)
    sums = scatter_lanes(values, lane, scratch, lanes)
    centres = [-jnp.sum(d, axis=0, keepdims=True) for d in deltas_bar]
    place = iota((1, lanes), 1)
    for j in range(4):
        start, width = own_lanes(j, lanes)
        own = jnp.logical_and(place >= start, place < start + width)
        out_ref[j, :, :] = jnp.zeros((8, lanes), f32)
        for c in range(3):
            mine = lane_take(jnp.broadcast_to(centres[c], (8, lanes)), jnp.broadcast_to(send_index(j), (8, lanes)))
            out_ref[j, c : c + 1, :] = sums[4 * j + c : 4 * j + c + 1, :] + jnp.where(
                own, mine[0:1, :], 0.0
            )


def offer_body(pos, vel, mass, species, send, out, rows):
    lanes = pos.shape[1]
    rows[0:3, :] = pos[...]
    rows[3:6, :] = vel[...]
    rows[6:7, :] = mass[...]
    rows[7:8, :] = species[...].astype(f32)
    place = iota((8, lanes), 1)
    for j in range(4):
        start, width = own_lanes(j, lanes)
        own = jnp.logical_and(place >= start, place < start + width)
        taken = jnp.take_along_axis(rows[...], jnp.broadcast_to(send[j : j + 1, :], (8, lanes)), axis=1)
        out[j, :, :] = jnp.where(own, taken, 0.0)


class Rows:
    def __init__(self, sizes):
        self.at = {}
        self.total = 0
        for name, size in sizes:
            self.at[name] = (self.total, size)
            self.total += size

    def get(self, ref, name):
        start, size = self.at[name]
        return ref[start : start + size, :]

    def put(self, ref, name, value):
        start, size = self.at[name]
        ref[start : start + size, :] = value


STRIDE = 32
USED = 24


def narrow_rows(feat):
    return Rows((("RQT", 2 * feat), ("C", 2 * feat), ("ST", 2 * feat), ("RT", feat), ("R", feat)))


def wide_rows(feat, types):
    return Rows((("BT", 2 * feat), ("B", STRIDE * types), ("RQ", feat), ("CT", feat), ("S", feat)))


def prep_body(
    near, slot_count, atom_count, send, species, table, encoder, spreader, filters,
    rotator, reflector, combiner, splitter, readout, collector,
    index, masks, feat_out, col_out, nh, nl, wh, wl, phi_out, types_out, filt_out,
):
    slots, lanes = near.shape
    types, feat = table.shape
    basis = filters.shape[0]
    quarter = lanes // 4
    lane_row = iota((16, lanes), 1).astype(f32)
    row_id = iota((16, lanes), 0)
    lefts, rights = [], []
    place = iota((lanes, lanes), 1)
    for j in range(4):
        start, width = own_lanes(j, lanes)
        own = jnp.logical_and(place >= start, place < start + width)
        same = jnp.logical_and(own, iota((lanes, lanes), 0) == send[j : j + 1, :])
        rights.append(same.astype(f32).astype(bf16))
        lefts.append(
            jnp.where(row_id == 0, lane_row, jnp.where(row_id == 1, float(j), 0.0)).astype(bf16)
        )
    found = dot1(cat(lefts, 1), cat(rights, 1), NT)
    inverse = (found[0:1, :] + lanes * found[1:2, :] + 0.5).astype(jnp.int32)
    near_v = near[...]
    ghost = near_v - lanes
    block = ghost // quarter
    p, q, g = block // 4, block % 4, ghost % quarter
    ghost_code = (2 * (p // 2) + q // 2) * lanes + 2 * quarter * (p % 2) + quarter * (q % 2) + g
    own_code = lane_take(inverse, jnp.minimum(near_v, lanes - 1))
    index[...] = jnp.zeros(index.shape, jnp.int32)
    index[0:slots, :] = jnp.where(near_v < lanes, own_code, ghost_code)
    index[slots : slots + 4, :] = send[...]
    index[slots + 4 : slots + 5, :] = inverse
    masks[...] = jnp.zeros(masks.shape, f32)
    masks[0:slots, :] = (iota((slots, lanes), 0) < slot_count[...]).astype(f32)
    masks[slots : slots + 1, :] = (iota((1, lanes), 1) < atom_count[0]).astype(f32)
    pre = jnp.dot(table[...], encoder[...], precision=highest, preferred_element_type=f32)
    gate = lax.logistic(pre)
    hidden = pre * gate
    phi = jnp.dot(hidden, spreader[...], precision=highest, preferred_element_type=f32)
    phi_out[...] = phi
    types_out[0:types, :] = hidden
    types_out[types : 2 * types, :] = gate * (1.0 + pre * (1.0 - gate))
    types_out[2 * types : 3 * types, :] = table[...]
    filt_out[...] = jnp.zeros(filt_out.shape, f32)
    filt_out[0:basis, :] = filters[...]
    filt = filt_out[...]
    table_pad = cat([table[...]] + [jnp.zeros((lanes - types, feat), f32)], 0)
    table_t = jnp.transpose(table_pad)
    feat_out[...] = jnp.take_along_axis(
        table_t, jnp.broadcast_to(species[...], (feat, lanes)), axis=1
    )
    col_out[...] = jnp.transpose(jnp.broadcast_to(collector[...], (lanes, feat)))

    narrow = narrow_rows(feat)
    wide = wide_rows(feat, types)

    def put(rows, high_ref, low_ref, name, value, row=0, col=0):
        high, low = split(value)
        start = rows.at[name][0] + row
        high_ref[start : start + value.shape[0], col : col + value.shape[1]] = high
        low_ref[start : start + value.shape[0], col : col + value.shape[1]] = low

    per_half = feat // STRIDE
    for half in range(2):
        cols = slice(half * feat, (half + 1) * feat)
        for chunk in range(types // per_half):
            block = cat(
                [
                    filt[:, cols] * phi[t : t + 1, cols]
                    for t in range(chunk * per_half, (chunk + 1) * per_half)
                ],
                0,
            )
            put(wide, wh, wl, "B", block, chunk * feat, half * feat)
            put(wide, wh, wl, "BT", jnp.transpose(block), half * feat, chunk * feat)
    put(wide, wh, wl, "RQ", rotator[...], 0, 0)
    put(wide, wh, wl, "RQ", reflector[...], 0, feat)
    put(narrow, nh, nl, "RQT", jnp.transpose(rotator[...]), 0)
    put(narrow, nh, nl, "RQT", jnp.transpose(reflector[...]), feat)
    put(narrow, nh, nl, "C", combiner[...])
    put(wide, wh, wl, "CT", jnp.transpose(combiner[0:feat, :]), 0, 0)
    put(wide, wh, wl, "CT", jnp.transpose(combiner[feat : 2 * feat, :]), 0, feat)
    put(wide, wh, wl, "S", splitter[...])
    put(narrow, nh, nl, "ST", jnp.transpose(splitter[:, 0:feat]), 0)
    put(narrow, nh, nl, "ST", jnp.transpose(splitter[:, feat : 2 * feat]), feat)
    put(narrow, nh, nl, "R", readout[...])
    put(narrow, nh, nl, "RT", jnp.transpose(readout[...]))


def saved_rows(feat, types, slots):
    k = STRIDE * types
    pair = ("e", "e1", "e2", "ir", "u0", "u1", "u2", "t")
    sizes = [("A%d" % q, k) for q in range(4)]
    sizes += [("%s%d" % (n, c), feat) for n in ("v", "vb") for c in range(3)]
    sizes += [("%s%d" % (n, c), 2 * feat) for n in ("uw", "uwb") for c in range(3)]
    sizes += [("joined", 2 * feat), ("ab", 2 * feat)]
    sizes += [
        (n, feat)
        for n in ("z", "dz", "d2z", "a2", "q", "n", "s2", "yb", "yc", "ldy", "s2b", "zb", "hb", "qb", "nbn", "s1b")
    ]
    sizes += [("sin", slots * USED), ("cos", slots * USED)]
    sizes += [(n, slots) for n in pair]
    sizes += [("%s%d" % (n, q), slots) for n in ("sa", "sb", "sd") for q in range(4)]
    return Rows(sizes)


def multiples(c1, s1, sin_ref, cos_ref, slots):
    lanes = c1.shape[1]
    powers = [(c1, s1)]
    for _ in range(4):
        c, s = powers[-1]
        powers.append((c * c - s * s, 2.0 * c * s))
    sub = iota((8, lanes), 0)
    bits = [(sub // 2**b) % 2 == 1 for b in range(3)]
    order = sub.astype(f32) + 1.0

    def times(x, y):
        return x[0] * y[0] - x[1] * y[1], x[0] * y[1] + x[1] * y[0]

    for k in range(slots):
        rows = [
            tuple(jnp.broadcast_to(part[k : k + 1, :], (8, lanes)) for part in power)
            for power in powers
        ]
        z = rows[0]
        for b in range(3):
            step = (jnp.where(bits[b], rows[b][0], 1.0), jnp.where(bits[b], rows[b][1], 0.0))
            z = times(z, step)
        for v in range(3):
            if v == 1:
                zv = times(z, rows[3])
            elif v == 2:
                zv = times(z, rows[4])
            else:
                zv = z
            start = k * USED + 8 * v
            sin_ref[start : start + 8, :] = zv[1]
            cos_ref[start : start + 8, :] = zv[0] * ((order + 8.0 * v) * omega)


def slot_sums(read_sin, read_cos, sin_coef, cos_coef, kinds, slots, types, put):
    lanes = kinds.shape[1]
    for q in range(4):
        sums = [None] * types
        for k in range(slots):
            value = read_sin(k) * sin_coef[q][k : k + 1, :]
            if cos_coef is not None:
                value = value + read_cos(k) * cos_coef[q][k : k + 1, :]
            kind = jnp.broadcast_to(kinds[k : k + 1, :], value.shape)
            for t in range(types):
                part = jnp.where(kind == t, value, 0.0)
                sums[t] = part if sums[t] is None else sums[t] + part
        rest = jnp.zeros((STRIDE - USED, lanes), f32)
        put(q, cat([x for t in range(types) for x in (sums[t], rest)], 0))


def slot_reads(values, kinds, read_sin, read_cos, slots, types, put, with_square):
    lanes = kinds.shape[1]
    sub = iota((USED, lanes), 0).astype(f32) + 1.0
    square = sub * sub * (omega * omega)
    for q in range(4):
        tables = [values(q)[STRIDE * t : STRIDE * t + USED, :] for t in range(types)]
        for k in range(slots):
            kind = jnp.broadcast_to(kinds[k : k + 1, :], (USED, lanes))
            picked = tables[0]
            for t in range(1, types):
                picked = jnp.where(kind == t, tables[t], picked)
            with_sin = read_sin(k) * picked
            put("sa", q, k, jnp.sum(with_sin, axis=0, keepdims=True))
            put("sb", q, k, jnp.sum(read_cos(k) * picked, axis=0, keepdims=True))
            if with_square:
                put("sd", q, k, jnp.sum(with_sin * square, axis=0, keepdims=True))


def triple(rows, ref, name):
    return cat([rows.get(ref, "%s%d" % (name, c)) for c in range(3)], 1)


def thirds(value):
    n = value.shape[1] // 3
    return [value[:, c * n : (c + 1) * n] for c in range(3)]


def force_body(types, depth, pool, pos, index, masks, features, colmat, nh, nl, wh, wl, out, save, scratch):
    lanes = pos.shape[1]
    slots = index.shape[0] - 8
    feat = features.shape[0]
    rows = saved_rows(feat, types, slots)
    narrow = narrow_rows(feat)
    wide = wide_rows(feat, types)
    code = index[0:slots, :]
    mask = masks[0:slots, :]
    live = masks[slots : slots + 1, :]

    def coords(j, c):
        shift = pool_offsets(j, lanes)[c]
        row = pool[j, c : c + 1, :]
        return row if shift is None else row + shift

    deltas, radius = pool_deltas(coords, lambda c: pos[c : c + 1, :], code, lanes, depth)
    kinds = from_pool([pool[j, 7:8, :] for j in range(4)], code, lanes)
    inside = jnp.where(radius < cutoff, mask, 0.0)
    theta = omega * jnp.minimum(radius, cutoff)
    c1, s1 = jnp.cos(theta), jnp.sin(theta)
    ir = 1.0 / radius
    env = 0.5 * (c1 + 1.0) * inside
    e = env * ir
    e1 = ((-0.5 * omega) * s1 * inside - e) * ir
    e2 = ((-0.5 * omega * omega) * c1 * inside - 2.0 * e1) * ir
    unit = [d * ir for d in deltas]
    for name, value in (("e", e), ("e1", e1), ("e2", e2), ("ir", ir), ("t", kinds)):
        rows.put(save, name, value)
    for c in range(3):
        rows.put(save, "u%d" % c, unit[c])
    sin_at, cos_at = rows.at["sin"][0], rows.at["cos"][0]
    multiples(c1, s1, save.at[sin_at : sin_at + slots * USED, :], save.at[cos_at : cos_at + slots * USED, :], slots)

    def read_sin(k):
        return save[sin_at + k * USED : sin_at + (k + 1) * USED, :]

    def read_cos(k):
        return save[cos_at + k * USED : cos_at + (k + 1) * USED, :]

    coefs = [e] + [e * u for u in unit]
    slot_sums(read_sin, read_cos, coefs, None, kinds, slots, types, lambda q, v: rows.put(save, "A%d" % q, v))

    def nw(name):
        return narrow.get(nh, name), narrow.get(nl, name)

    def wd(name, first=None, last=None, rsl=slice(None)):
        return tuple(wide.get(r, name)[rsl, first:last] for r in (wh, wl))

    a0 = split(rows.get(save, "A0"))
    av = split(cat([rows.get(save, "A%d" % q) for q in (1, 2, 3)], 1))
    s_one = features[...] + dot3(wd("BT", rsl=slice(0, feat)), a0)
    v = dot3(wd("BT", rsl=slice(feat, 2 * feat)), av)
    uw = dot3(nw("RQT"), split(v))
    turned, mirrored = thirds(uw[0:feat]), thirds(uw[feat : 2 * feat])
    q = turned[0] * mirrored[0] + turned[1] * mirrored[1] + turned[2] * mirrored[2]
    n = jnp.sqrt(mirrored[0] * mirrored[0] + mirrored[1] * mirrored[1] + mirrored[2] * mirrored[2] + 1.0)
    joined = cat([s_one, n], 0)
    h = dot3(wd("CT"), split(joined))
    gate = lax.logistic(h)
    z = h * gate
    dz = gate * (1.0 + h * (1.0 - gate))
    d2z = gate * (1.0 - gate) * (2.0 + h * (1.0 - 2.0 * gate))
    a = dot3(nw("ST"), split(z))
    a2 = a[feat : 2 * feat]
    s_two = s_one + a[0:feat] + a2 * q
    y = dot3(nw("RT"), split(s_two))
    gate = lax.logistic(y)
    dy = gate * (1.0 + y * (1.0 - gate))
    d2y = gate * (1.0 - gate) * (2.0 + y * (1.0 - 2.0 * gate))
    ldy = dy * live
    yb = colmat[...] * ldy
    s2b = dot3(nw("R"), split(yb))
    ab = cat([s2b, s2b * q], 0)
    qb = s2b * a2
    zb = dot3(wd("S"), split(ab))
    hb = zb * dz
    jb = dot3(nw("C"), split(hb))
    s1b = s2b + jb[0:feat]
    nbn = jb[feat : 2 * feat] / n
    uwb = cat(
        [
            cat([qb * mirrored[c] for c in range(3)], 1),
            cat([nbn * mirrored[c] + qb * turned[c] for c in range(3)], 1),
        ],
        0,
    )
    vb = dot3(wd("RQ"), split(uwb))
    for name, value in (
        ("joined", joined), ("ab", ab), ("z", z), ("dz", dz), ("d2z", d2z), ("a2", a2), ("q", q), ("n", n),
        ("s2", s_two), ("yb", yb), ("yc", colmat[...] * live * d2y), ("ldy", ldy), ("s2b", s2b), ("zb", zb),
        ("hb", hb), ("qb", qb), ("nbn", nbn), ("s1b", s1b),
    ):
        rows.put(save, name, value)
    for name, value in (("v", v), ("uw", uw), ("uwb", uwb), ("vb", vb)):
        for c, part in enumerate(thirds(value)):
            rows.put(save, "%s%d" % (name, c), part)
    ab0 = dot3(wd("B", 0, feat), split(s1b))
    abv = thirds(dot3(wd("B", feat, 2 * feat), split(vb)))

    def put(name, q, k, row):
        start = rows.at["%s%d" % (name, q)][0] + k
        save[start : start + 1, :] = row

    tables = [ab0] + abv
    slot_reads(lambda q: tables[q], kinds, read_sin, read_cos, slots, types, put, True)
    sa = [rows.get(save, "sa%d" % q) for q in range(4)]
    sb = [rows.get(save, "sb%d" % q) for q in range(4)]
    z_sum = unit[0] * sa[1] + unit[1] * sa[2] + unit[2] * sa[3]
    x_sum = sb[0] + unit[0] * sb[1] + unit[1] * sb[2] + unit[2] * sb[3]
    rb = e * x_sum + e1 * (sa[0] + z_sum) - ir * e * z_sum
    deltas_bar = [rb * unit[c] + e * ir * sa[c + 1] for c in range(3)]
    pool_partials(deltas_bar, code, lambda j: index[slots + j : slots + j + 1, :], out, scratch, lanes)


def centres_of(bins, bin_total):
    return 0.1 * jnp.sqrt(3600.0 * (bins.astype(f32) + 0.5) / bin_total)


def hist_body(depth, bin_total, pool, force, index, masks, bins, next_own, slopes, hist, moved, scratch):
    lanes = pool.shape[2]
    slots = index.shape[0] - 8
    code = index[0:slots, :]
    inverse = index[slots + 4 : slots + 5, :]
    mask = masks[0:slots, :]
    for j in range(4):
        kick = (0.5 * time_step * time_step) * pool[j, 6:7, :]
        moved[j, 0:3, :] = pool[j, 0:3, :] + time_step * pool[j, 3:6, :] - kick * force[j, 0:3, :]
    inverse8 = jnp.broadcast_to(inverse, (8, lanes))
    own = []
    for c in range(3):
        row = from_pool([moved[j, c : c + 1, :] for j in range(4)], inverse8, lanes)[0:1, :]
        next_own[c : c + 1, :] = row
        own.append(row)

    def coords(j, c):
        shift = pool_offsets(j, lanes)[c]
        row = moved[j, c : c + 1, :]
        return row if shift is None else row + shift

    deltas, radius = pool_deltas(coords, lambda c: own[c], code, lanes, depth)
    gap = radius - centres_of(bins[...], bin_total)
    kernel = jnp.exp(-gap * gap / sigma_two) * mask
    scale = kernel * gap * (-2.0 / sigma_two) / radius
    for c in range(3):
        slopes[c * slots : (c + 1) * slots, :] = scale * deltas[c]
    sums = scatter_lanes([kernel], bins[...], scratch, bin_total)
    hist[...] = jnp.broadcast_to(sums[0:1, :], hist.shape)


def adjoint_body(atoms_total, hists, target, slopes, index, bins, out, scratch):
    lanes = bins.shape[1]
    slots = bins.shape[0]
    code = index[0:slots, :]
    total = jnp.sum(hists[...], axis=0, keepdims=True)
    weights = 2.0 * (total / atoms_total - target[...]) / atoms_total
    picked = lane_take(weights, bins[...])
    deltas_bar = [picked * slopes[c * slots : (c + 1) * slots, :] for c in range(3)]
    pool_partials(deltas_bar, code, lambda j: index[slots + j : slots + j + 1, :], out, scratch, lanes)


def second_body(
    types, pool, adjoint, index, save, colmat, phi, filt, nh, nl, wh, wl,
    out, grads, tangents, scratch,
):
    lanes = pool.shape[2]
    slots = index.shape[0] - 8
    feat = colmat.shape[0]
    rows = saved_rows(feat, types, slots)
    narrow = narrow_rows(feat)
    wide = wide_rows(feat, types)
    code = index[0:slots, :]
    inverse8 = jnp.broadcast_to(index[slots + 4 : slots + 5, :], (8, lanes))

    def get(name):
        return rows.get(save, name)

    probe = [
        [(0.5 * time_step * time_step) * pool[j, 6:7, :] * adjoint[j, c : c + 1, :] for j in range(4)]
        for c in range(3)
    ]
    moves = [
        from_pool(probe[c], code, lanes) - from_pool(probe[c], inverse8, lanes)[0:1, :] for c in range(3)
    ]
    e, e1, e2, ir, kinds = get("e"), get("e1"), get("e2"), get("ir"), get("t")
    unit = [get("u%d" % c) for c in range(3)]
    dr = unit[0] * moves[0] + unit[1] * moves[1] + unit[2] * moves[2]
    du = [(moves[c] - unit[c] * dr) * ir for c in range(3)]
    de, de1, dir_ = e1 * dr, e2 * dr, -ir * ir * dr
    sin_at, cos_at = rows.at["sin"][0], rows.at["cos"][0]

    def read_sin(k):
        return save[sin_at + k * USED : sin_at + (k + 1) * USED, :]

    def read_cos(k):
        return save[cos_at + k * USED : cos_at + (k + 1) * USED, :]

    k_rows = STRIDE * types

    def put_sum(q, value):
        tangents[q * k_rows : (q + 1) * k_rows, :] = value

    sin_coef = [de] + [de * unit[c] + e * du[c] for c in range(3)]
    cos_coef = [e * dr] + [e * dr * unit[c] for c in range(3)]
    slot_sums(read_sin, read_cos, sin_coef, cos_coef, kinds, slots, types, put_sum)

    def nw(name):
        return narrow.get(nh, name), narrow.get(nl, name)

    def wd(name, first=None, last=None, rsl=slice(None)):
        return tuple(wide.get(r, name)[rsl, first:last] for r in (wh, wl))

    da_zero = tangents[0:k_rows, :]
    da_vec = cat([tangents[q * k_rows : (q + 1) * k_rows, :] for q in (1, 2, 3)], 1)
    ds1 = dot3(wd("BT", rsl=slice(0, feat)), split(da_zero))
    dv = dot3(wd("BT", rsl=slice(feat, 2 * feat)), split(da_vec))
    duw = dot3(nw("RQT"), split(dv))
    d_turn, d_mirr = thirds(duw[0:feat]), thirds(duw[feat : 2 * feat])
    turned = [get("uw%d" % c)[0:feat] for c in range(3)]
    mirrored = [get("uw%d" % c)[feat : 2 * feat] for c in range(3)]
    q, n, a2, dz, d2z = get("q"), get("n"), get("a2"), get("dz"), get("d2z")
    s2b, zb, qb, nbn = get("s2b"), get("zb"), get("qb"), get("nbn")
    dq = sum(d_turn[c] * mirrored[c] + turned[c] * d_mirr[c] for c in range(3))
    dn = sum(mirrored[c] * d_mirr[c] for c in range(3)) / n
    dj = cat([ds1, dn], 0)
    dh = dot3(wd("CT"), split(dj))
    dzt = dz * dh
    da = dot3(nw("ST"), split(dzt))
    da2 = da[feat : 2 * feat]
    ds2 = ds1 + da[0:feat] + da2 * q + a2 * dq
    dyt = dot3(nw("RT"), split(ds2))
    dyb = get("yc") * dyt
    ds2b = dot3(nw("R"), split(dyb))
    dab = cat([ds2b, ds2b * q + s2b * dq], 0)
    dqb = ds2b * a2 + s2b * da2
    dzb = dot3(wd("S"), split(dab))
    dhb = dzb * dz + zb * (d2z * dh)
    djb = dot3(nw("C"), split(dhb))
    ds1b = ds2b + djb[0:feat]
    dnbn = (djb[feat : 2 * feat] - nbn * dn) / n
    duwb = cat(
        [
            cat([dqb * mirrored[c] + qb * d_mirr[c] for c in range(3)], 1),
            cat(
                [
                    dnbn * mirrored[c] + nbn * d_mirr[c] + dqb * turned[c] + qb * d_turn[c]
                    for c in range(3)
                ],
                1,
            ),
        ],
        0,
    )
    dvb = dot3(wd("RQ"), split(duwb))

    def both(first, second, third, fourth):
        return -dot3(split(cat([first, second], 1)), split(cat([third, fourth], 1)), NT)

    parts = grads.shape[0]
    share = feat // parts
    rq = both(dv, triple(rows, save, "v"), triple(rows, save, "uwb"), duwb)
    cg = both(dj, get("joined"), get("hb"), dhb)
    sg = both(dzt, get("z"), get("ab"), dab)
    rg = both(ds2, get("s2"), get("yb"), dyb)
    bs = both(da_zero, get("A0"), get("s1b"), ds1b)
    bv = both(da_vec, cat([get("A%d" % i) for i in (1, 2, 3)], 1), triple(rows, save, "vb"), dvb)
    low, high = split(get("ldy") * dyt)
    ones = jnp.ones((16, lanes), bf16)
    col = -(dot1(ones, low, NT) + dot1(ones, high, NT))
    fg, pg = [], []
    for half, value in enumerate((bs, bv)):
        cols = slice(half * feat, (half + 1) * feat)
        total = None
        for t in range(types):
            block = value[STRIDE * t : STRIDE * t + USED, :]
            term = block * phi[t : t + 1, cols]
            total = term if total is None else total + term
            pg.append((half, t, jnp.sum(block * filt[0:USED, cols], axis=0, keepdims=True)))
        fg.append(total)
    base = 7 * share
    place = iota((10, lanes), 1)
    for part in range(parts):
        mine = slice(part * share, (part + 1) * share)
        grads[part, 0:share, :] = rq[mine, 0:feat]
        grads[part, share : 2 * share, :] = rq[mine, feat : 2 * feat]
        grads[part, 2 * share : 4 * share, :] = cg[2 * part * share : 2 * (part + 1) * share, :]
        grads[part, 4 * share : 5 * share, :] = sg[mine, 0:feat]
        grads[part, 5 * share : 6 * share, :] = sg[mine, feat : 2 * feat]
        grads[part, 6 * share : 7 * share, :] = rg[mine, :]
        for half, t, row in pg:
            at = base + half * types + t
            grads[part, at : at + 1, :] = row
        chosen = fg[part // 2]
        rolled = pltpu.roll(chosen, feat // 2, 1)
        here, there = (chosen, rolled) if part % 2 == 0 else (rolled, chosen)
        at = base + 2 * types
        grads[part, at : at + 10, :] = jnp.where(place < feat // 2, here[0:10, :], there[10:20, :])
        grads[part, at + 10 : at + 11, :] = col[0:1, :]
        grads[part, at + 11 :, :] = jnp.zeros((grads.shape[1] - at - 11, lanes), f32)

    dab0 = dot3(wd("B", 0, feat), split(ds1b))
    dabv = thirds(dot3(wd("B", feat, 2 * feat), split(dvb)))
    tables = [dab0] + dabv
    at_sums = 4 * k_rows

    def put(name, q, k, row):
        start = at_sums + (0 if name == "sa" else 4 * slots) + q * slots + k
        tangents[start : start + 1, :] = row

    slot_reads(lambda q: tables[q], kinds, read_sin, read_cos, slots, types, put, False)
    sa = [get("sa%d" % q) for q in range(4)]
    sb = [get("sb%d" % q) for q in range(4)]
    sd = [get("sd%d" % q) for q in range(4)]
    dsa = [sb[q] * dr + tangents[at_sums + q * slots : at_sums + (q + 1) * slots, :] for q in range(4)]
    dsb = [
        tangents[at_sums + (4 + q) * slots : at_sums + (5 + q) * slots, :] - sd[q] * dr for q in range(4)
    ]
    z_sum = sum(unit[c] * sa[c + 1] for c in range(3))
    x_sum = sb[0] + sum(unit[c] * sb[c + 1] for c in range(3))
    dz_sum = sum(du[c] * sa[c + 1] + unit[c] * dsa[c + 1] for c in range(3))
    dx_sum = dsb[0] + sum(du[c] * sb[c + 1] + unit[c] * dsb[c + 1] for c in range(3))
    rb = e * x_sum + e1 * (sa[0] + z_sum) - ir * e * z_sum
    drb = (
        de * x_sum + e * dx_sum + de1 * (sa[0] + z_sum) + e1 * (dsa[0] + dz_sum)
        - (dir_ * e + ir * de) * z_sum - ir * e * dz_sum
    )
    deltas_bar = [
        drb * unit[c] + rb * du[c] + (de * ir + e * dir_) * sa[c + 1] + e * ir * dsa[c + 1]
        for c in range(3)
    ]
    pool_partials(deltas_bar, code, lambda j: index[slots + j : slots + j + 1, :], out, scratch, lanes)


def last_body(
    types, parts, atoms_total, where, total, adjoint, second, index, types_in, spreader,
    adj, enc, spr, fil, rot, ref, com, spl, rea, col,
):
    lanes = adjoint.shape[2]
    slots = index.shape[0] - 8
    feat = lanes
    share = feat // parts
    inverse8 = jnp.broadcast_to(index[slots + 4 : slots + 5, :], (8, lanes))
    for c in range(3):
        rows = [
            atoms_total * (adjoint[j, c : c + 1, :] - second[j, c : c + 1, :]) for j in range(4)
        ]
        adj[c : c + 1, :] = from_pool(rows, inverse8, lanes)[0:1, :]
    rot[...] = total[0:share, :]
    ref[...] = total[share : 2 * share, :]
    com[...] = total[2 * share : 4 * share, :]
    spl[:, 0:feat] = total[4 * share : 5 * share, :]
    spl[:, feat : 2 * feat] = total[5 * share : 6 * share, :]
    rea[...] = total[6 * share : 7 * share, :]
    base = 7 * share
    phib = cat([total[base : base + types, :], total[base + types : base + 2 * types, :]], 1)
    at = base + 2 * types
    block = total[at : at + 10, :]
    fil[0:10, :] = block[:, 0 : feat // 2]
    fil[10:20, :] = pltpu.roll(block, feat // 2, 1)[:, 0 : feat // 2]
    col[...] = total[at + 10 : at + 11, :]
    hidden = types_in[0:types, :]
    slope = types_in[types : 2 * types, :]
    table = types_in[2 * types : 3 * types, :]

    def exact(a, b, dims):
        return lax.dot_general(a, b, (dims, ((), ())), precision=highest, preferred_element_type=f32)

    pre_bar = exact(phib, spreader[...], NT) * slope
    pad = jnp.zeros((lanes - types, feat), f32)
    hidden_t = jnp.transpose(cat([hidden, pad], 0))
    table_t = jnp.transpose(cat([table, pad], 0))
    wide_pad = jnp.zeros((lanes - types, 2 * feat), f32)
    full_spr = exact(hidden_t, cat([phib, wide_pad], 0), NN)
    full_enc = exact(table_t, cat([pre_bar, pad], 0), NN)
    for part in range(parts):
        @pl.when(where[0] == part)
        def _():
            spr[...] = full_spr[part * share : (part + 1) * share, :]
            enc[...] = full_enc[part * share : (part + 1) * share, :]


def shift(x, axis, step):
    count = lax.axis_size(axis)
    return lax.ppermute(x, axis, [(i, (i + step) % count) for i in range(count)])


def corner_sum(groups):
    low, high = groups[0], groups[1]
    high, low = high + shift(low, "slab", -1), low + shift(high, "slab", 1)
    left = jnp.stack([low[0], high[0]])
    right = jnp.stack([low[1], high[1]])
    right, left = right + shift(left, "cross", -1), left + shift(right, "cross", 1)
    return jnp.stack([left[0], right[0], left[1], right[1]])


def swap(x, axis, bit):
    count = lax.axis_size(axis)
    return lax.ppermute(x, axis, [(i, i ^ bit) for i in range(count)])


def halve(x, axis, bit):
    mine = (lax.axis_index(axis) // bit) % 2 == 1
    return jnp.where(mine, x[1], x[0]) + swap(jnp.where(mine, x[0], x[1]), axis, bit)


def join(x, axis, bit):
    mine = (lax.axis_index(axis) // bit) % 2 == 1
    other = swap(x, axis, bit)
    return jnp.where(mine, jnp.stack([other, x]), jnp.stack([x, other]))


def reduce_grads(grads):
    slab_count, cross_count = lax.axis_size("slab"), lax.axis_size("cross")
    parts, rows, lanes = grads.shape
    bits = []
    bit = 1
    while bit < slab_count:
        bits.append(bit)
        bit *= 2
    x = grads
    for bit in bits:
        x = x.reshape(parts, 2, x.shape[1] // 2, lanes).transpose(1, 0, 2, 3)
        x = halve(x, "slab", bit)
    bit = cross_count // 2
    while bit >= 1:
        x = x.reshape((2, x.shape[0] // 2) + x.shape[1:])
        x = halve(x, "cross", bit)
        bit //= 2
    x = x[0]
    for bit in reversed(bits):
        x = join(x, "slab", bit).reshape(2 * x.shape[0], lanes)
    return x


def on_device(
    positions, velocities, inverse_mass, species, type_table, neighbours, slot_count, atom_count,
    pair_bins, send_list, target, encoder, spreader, filters, rotator, reflector, combiner, splitter,
    readout, collector,
):
    lanes = positions.shape[1]
    slots = neighbours.shape[1]
    types, feat = type_table.shape
    bin_total = target.shape[0]
    slab_count, cross_count = lax.axis_size("slab"), lax.axis_size("cross")
    devices = slab_count * cross_count
    atoms_total = float(lanes * devices)
    depth = 1.6 * (lanes // 16)
    parts = cross_count
    send_rows = []
    for j in range(4):
        start, width = own_lanes(j, lanes)
        send_rows.append(jnp.pad(send_list[j // 2, j % 2], (start, lanes - start - width)))
    send = jnp.stack(send_rows)
    row = lambda x: x.reshape(1, x.shape[0])
    species_row = row(species)
    (offers,) = call(
        offer_body, [((4, 8, lanes), f32)], positions, velocities, row(inverse_mass), species_row, send,
        scratch=[pltpu.VMEM((8, lanes), f32)],
    )
    narrow, wide = narrow_rows(feat).total, wide_rows(feat, types).total
    index, masks, features, colmat, nh, nl, wh, wl, phi, types_in, filt = call(
        prep_body,
        [
            ((slots + 8, lanes), jnp.int32), ((slots + 8, lanes), f32), ((feat, lanes), f32), ((feat, lanes), f32),
            ((narrow, feat), bf16), ((narrow, feat), bf16), ((wide, 2 * feat), bf16), ((wide, 2 * feat), bf16),
            ((types, 2 * feat), f32), ((3 * types, feat), f32), ((STRIDE, 2 * feat), f32),
        ],
        neighbours.T, row(slot_count), atom_count, send, species_row, type_table, encoder, spreader, filters,
        rotator, reflector, combiner, splitter, readout, row(collector),
        specs=[VM, VM, SM] + [VM] * 12,
    )
    groups = lambda x: x.reshape((2, 2) + x.shape[1:])
    pool = corner_sum(groups(offers))
    pair_scratch = pltpu.VMEM((16 * slots, lanes), f32)
    save_rows = saved_rows(feat, types, slots).total
    force, save = call(
        functools.partial(force_body, types, depth),
        [((4, 8, lanes), f32), ((save_rows, lanes), f32)],
        pool, positions, index, masks, features, colmat, nh, nl, wh, wl,
        scratch=[pair_scratch],
    )
    force = corner_sum(groups(force))
    bins = pair_bins.T
    next_positions, slopes, hist = call(
        functools.partial(hist_body, depth, bin_total),
        [((3, lanes), f32), ((3 * slots, lanes), f32), ((devices, bin_total), f32)],
        pool, force, index, masks, bins,
        scratch=[pltpu.VMEM((4, 8, lanes), f32), pair_scratch],
    )
    hists = lax.all_to_all(hist.reshape(devices, 1, bin_total), ("slab", "cross"), 0, 0)
    (adjoint,) = call(
        functools.partial(adjoint_body, atoms_total),
        [((4, 8, lanes), f32)],
        hists.reshape(devices, bin_total), row(target), slopes, index, bins,
        scratch=[pair_scratch],
    )
    adjoint = corner_sum(groups(adjoint))
    second, grads = call(
        functools.partial(second_body, types),
        [((4, 8, lanes), f32), ((parts, 2 * feat, lanes), f32)],
        pool, adjoint, index, save, colmat, phi, filt, nh, nl, wh, wl,
        scratch=[pltpu.VMEM((4 * STRIDE * types + 8 * slots, lanes), f32), pair_scratch],
    )
    second = corner_sum(groups(second))
    total = reduce_grads(grads)
    share = feat // parts
    place = lax.axis_index("cross")
    results = call(
        functools.partial(last_body, types, parts, atoms_total),
        [
            ((3, lanes), f32), ((share, feat), f32), ((share, 2 * feat), f32),
            ((filters.shape[0], 2 * feat // parts), f32), ((share, feat), f32), ((share, feat), f32),
            ((2 * share, feat), f32), ((share, 2 * feat), f32), ((share, feat), f32), ((1, feat), f32),
        ],
        place.reshape(1).astype(jnp.int32), total, adjoint, second, index, types_in, spreader,
        specs=[SM] + [VM] * 6,
    )
    adj, enc, spr, fil, rot, ref, com, spl, rea, col = results
    col = lax.dynamic_slice_in_dim(col[0], place * share, share, 0)
    return next_positions, adj, enc, spr, fil, rot, ref, com, spl, rea, col


def solution(mesh):
    both = ("slab", "cross")
    in_specs = (
        P(None, both), P(None, both), P(both), P(both), P(), P(both, None), P(both), P(both), P(both, None),
        P("slab", "cross", None),
    ) + (P(),) * 10
    out_specs = (
        P(None, both), P(None, both), P("cross", None), P("cross", None), P(None, "cross"), P("cross", None),
        P("cross", None), P("cross", None), P("cross", None), P("cross", None), P("cross"),
    )
    return jax.shard_map(on_device, mesh=mesh, in_specs=in_specs, out_specs=out_specs, check_vma=False)
```

```python
import functools

import jax
import jax.numpy as jnp
from jax import lax
from jax.experimental import pallas as pl
from jax.experimental.pallas import tpu as pltpu
from jax.sharding import PartitionSpec as P

cutoff = 5.0
soften = 0.25
sigma_two = 0.18
slab_length = 10.0
cell_length = 10.0
time_step = 0.5
highest = lax.Precision.HIGHEST
f32 = jnp.float32
bf16 = jnp.bfloat16
pi = 3.141592653589793
omega = pi / cutoff

NN = ((1,), (0,))
NT = ((1,), (1,))
VM = pl.BlockSpec(memory_space=pltpu.VMEM)
SM = pl.BlockSpec(memory_space=pltpu.SMEM)
HB = pl.BlockSpec(memory_space=pltpu.HBM)


def call(body, outs, *args, specs=None, scratch=(), keep=True):
    return pl.pallas_call(
        body,
        out_shape=[(pltpu.VMEM if keep else jax.ShapeDtypeStruct)(s, d) for s, d in outs],
        in_specs=[VM] * len(args) if specs is None else specs,
        out_specs=[VM] * len(outs),
        scratch_shapes=list(scratch),
        compiler_params=pltpu.CompilerParams(vmem_limit_bytes=16 * 2**20),
    )(*args)


def in_hbm(*arrays):
    return [pltpu.with_memory_space_constraint(x, pltpu.HBM) for x in arrays]


def fetch(sources, targets, semaphores):
    copies = [
        pltpu.make_async_copy(source, target, semaphores.at[i])
        for i, (source, target) in enumerate(zip(sources, targets))
    ]
    for copy in copies:
        copy.start()
    for copy in copies:
        copy.wait()


def split(x):
    high = x.astype(bf16)
    return high, (x - high.astype(f32)).astype(bf16)


def dot1(a, b, dims):
    return lax.dot_general(a, b, (dims, ((), ())), preferred_element_type=f32)


def dot3(a, b, dims=NN):
    return dot1(a[0], b[0], dims) + (dot1(a[0], b[1], dims) + dot1(a[1], b[0], dims))


def cat(parts, axis):
    return jnp.concatenate(parts, axis=axis)


def iota(shape, dim):
    return lax.broadcasted_iota(jnp.int32, shape, dim)


def lane_take(row, index):
    return jnp.take_along_axis(jnp.broadcast_to(row, index.shape), index, axis=1)


def own_lanes(group, lanes):
    quarter = lanes // 4
    start = 2 * quarter * (1 - group // 2) + quarter * (1 - group % 2)
    return start, quarter


def pool_offsets(group, lanes):
    place = iota((1, lanes), 1)
    up, right = group // 2, group % 2
    half, quarter = lanes // 2, lanes // 4
    first = (place >= half) if up else (place < half)
    second_bit = place % half >= quarter
    second = second_bit if right else jnp.logical_not(second_bit)
    sign_u, sign_r = 2.0 * up - 1.0, 2.0 * right - 1.0
    return (
        jnp.where(first, sign_u * slab_length, 0.0).astype(f32),
        jnp.where(second, sign_r * cell_length, 0.0).astype(f32),
        None,
    )


def from_pool(rows, code, lanes):
    group = code // lanes
    lane = code % lanes
    out = lane_take(rows[0], lane)
    for j in range(1, 4):
        out = jnp.where(group == j, lane_take(rows[j], lane), out)
    return out


def pool_deltas(pool_rows, own_rows, code, lanes, depth):
    deltas = []
    for c in range(3):
        d = from_pool([pool_rows(j, c) for j in range(4)], code, lanes) - own_rows(c)
        if c == 2:
            d = d - depth * jnp.floor(d / depth + 0.5)
        deltas.append(d)
    radius = jnp.sqrt(deltas[0] * deltas[0] + deltas[1] * deltas[1] + deltas[2] * deltas[2] + soften)
    return deltas, radius


def one_hot_rows(index, slots, count):
    lanes = index.shape[1]
    place = iota((count, lanes), 0)
    return cat(
        [(place == index[k : k + 1, :]).astype(f32).astype(bf16) for k in range(slots)], 1
    )


def scatter_lanes(values, index, scratch, count):
    slots = index.shape[0]
    for row in range(16):
        value = values[row] if row < len(values) else None
        if value is None:
            value = jnp.zeros(index.shape, f32)
        scratch[pl.ds(row, slots, stride=16), :] = value
    highs, mids, lows = [], [], []
    for k in range(slots):
        x = scratch[16 * k : 16 * k + 16, :]
        high = x.astype(bf16)
        rest = x - high.astype(f32)
        mid = rest.astype(bf16)
        highs.append(high)
        mids.append(mid)
        lows.append((rest - mid.astype(f32)).astype(bf16))
    left = cat([cat(highs, 1), cat(mids, 1), cat(lows, 1)], 0)
    sums = dot1(left, one_hot_rows(index, slots, count), NT)
    return sums[0:16] + (sums[16:32] + sums[32:48])


def pool_partials(deltas_bar, code, send_index, outs, scratch, lanes):
    group = code // lanes
    lane = code % lanes
    values = []
    for j in range(4):
        for c in range(3):
            values.append(jnp.where(group == j, deltas_bar[c], 0.0))
        values.append(None)
    sums = scatter_lanes(values, lane, scratch, lanes)
    centres = [-jnp.sum(d, axis=0, keepdims=True) for d in deltas_bar]
    place = iota((1, lanes), 1)
    for j in range(4):
        start, width = own_lanes(j, lanes)
        own = jnp.logical_and(place >= start, place < start + width)
        out_ref = outs[j // 2]
        out_ref[j % 2, :, :] = jnp.zeros((8, lanes), f32)
        for c in range(3):
            mine = lane_take(jnp.broadcast_to(centres[c], (8, lanes)), jnp.broadcast_to(send_index(j), (8, lanes)))
            out_ref[j % 2, c : c + 1, :] = sums[4 * j + c : 4 * j + c + 1, :] + jnp.where(
                own, mine[0:1, :], 0.0
            )


def offer_body(
    pos, vel, mass, species, send_list, low, high, own_out, send_out,
    pos_v, vel_v, mass_v, species_v, list_v, semaphores,
):
    fetch((pos, vel, mass, species, send_list), (pos_v, vel_v, mass_v, species_v, list_v), semaphores)
    lanes = pos.shape[1]
    own_out[0:3, :] = pos_v[...]
    own_out[3:6, :] = vel_v[...]
    own_out[6:7, :] = mass_v[...]
    own_out[7:8, :] = species_v[...].astype(f32)
    own_rows = own_out[...]
    place = iota((8, lanes), 1)
    send_out[...] = jnp.zeros((8, lanes), jnp.int32)
    for j in range(4):
        start, width = own_lanes(j, lanes)
        pieces = [list_v[j // 2, j % 2 : j % 2 + 1, :]]
        if start:
            pieces = [jnp.zeros((1, start), jnp.int32)] + pieces
        if start + width < lanes:
            pieces = pieces + [jnp.zeros((1, lanes - start - width), jnp.int32)]
        row = cat(pieces, 1)
        send_out[j : j + 1, :] = row
        own = jnp.logical_and(place >= start, place < start + width)
        taken = jnp.take_along_axis(own_rows, jnp.broadcast_to(row, (8, lanes)), axis=1)
        out = (low, high)[j // 2]
        out[j % 2, :, :] = jnp.where(own, taken, 0.0)


def turn_body(low, high, from_down, from_up, left, right):
    for u, (mine, other) in enumerate(((low, from_down), (high, from_up))):
        left[u, :, :] = mine[0] + other[0]
        right[u, :, :] = mine[1] + other[1]


def whole(pieces, j):
    right = j % 2
    return pieces[right][j // 2] + pieces[2 + right][j // 2]


class Rows:
    def __init__(self, sizes):
        self.at = {}
        self.total = 0
        for name, size in sizes:
            self.at[name] = (self.total, size)
            self.total += size

    def get(self, ref, name):
        start, size = self.at[name]
        return ref[start : start + size, :]

    def put(self, ref, name, value):
        start, size = self.at[name]
        ref[start : start + size, :] = value


STRIDE = 32
USED = 24


def narrow_rows(feat):
    return Rows((("RQT", 2 * feat), ("C", 2 * feat), ("ST", 2 * feat), ("RT", feat), ("R", feat)))


def wide_rows(feat, types):
    return Rows((("BT", 2 * feat), ("B", STRIDE * types), ("RQ", feat), ("CT", feat), ("S", feat)))


def prep_body(
    near_h, count_h, table_h, encoder_h, spreader_h, filters_h, rotator_h, reflector_h, combiner_h, splitter_h,
    readout_h, collector_h, bins_h, target_h, atom_count, send, own_rows,
    index, masks, feat_out, col_out, nh, nl, wh, wl, phi_out, types_out, filt_out, bins, target, spreader,
    near, slot_count, table, encoder, filters, rotator, reflector, combiner, splitter, readout, collector,
    semaphores,
):
    fetch(
        (near_h, count_h, table_h, encoder_h, spreader_h, filters_h, rotator_h, reflector_h, combiner_h,
         splitter_h, readout_h, collector_h, bins_h, target_h),
        (near, slot_count, table, encoder, spreader, filters, rotator, reflector, combiner,
         splitter, readout, collector, bins, target),
        semaphores,
    )
    species = own_rows[7:8, :].astype(jnp.int32)
    slots, lanes = near.shape
    types, feat = table.shape
    basis = filters.shape[0]
    quarter = lanes // 4
    lane_row = iota((16, lanes), 1).astype(f32)
    row_id = iota((16, lanes), 0)
    lefts, rights = [], []
    place = iota((lanes, lanes), 1)
    for j in range(4):
        start, width = own_lanes(j, lanes)
        own = jnp.logical_and(place >= start, place < start + width)
        same = jnp.logical_and(own, iota((lanes, lanes), 0) == send[j : j + 1, :])
        rights.append(same.astype(f32).astype(bf16))
        lefts.append(
            jnp.where(row_id == 0, lane_row, jnp.where(row_id == 1, float(j), 0.0)).astype(bf16)
        )
    found = dot1(cat(lefts, 1), cat(rights, 1), NT)
    inverse = (found[0:1, :] + lanes * found[1:2, :] + 0.5).astype(jnp.int32)
    near_v = near[...]
    ghost = near_v - lanes
    block = ghost // quarter
    p, q, g = block // 4, block % 4, ghost % quarter
    ghost_code = (2 * (p // 2) + q // 2) * lanes + 2 * quarter * (p % 2) + quarter * (q % 2) + g
    own_code = lane_take(inverse, jnp.minimum(near_v, lanes - 1))
    index[...] = jnp.zeros(index.shape, jnp.int32)
    index[0:slots, :] = jnp.where(near_v < lanes, own_code, ghost_code)
    index[slots : slots + 4, :] = send[0:4, :]
    index[slots + 4 : slots + 5, :] = inverse
    masks[...] = jnp.zeros(masks.shape, f32)
    masks[0:slots, :] = (iota((slots, lanes), 0) < slot_count[...]).astype(f32)
    masks[slots : slots + 1, :] = (iota((1, lanes), 1) < atom_count[0]).astype(f32)
    pre = jnp.dot(table[...], encoder[...], precision=highest, preferred_element_type=f32)
    gate = lax.logistic(pre)
    hidden = pre * gate
    phi = jnp.dot(hidden, spreader[...], precision=highest, preferred_element_type=f32)
    phi_out[...] = phi
    types_out[0:types, :] = hidden
    types_out[types : 2 * types, :] = gate * (1.0 + pre * (1.0 - gate))
    types_out[2 * types : 3 * types, :] = table[...]
    filt_out[...] = jnp.zeros(filt_out.shape, f32)
    filt_out[0:basis, :] = filters[...]
    filt = filt_out[...]
    table_pad = cat([table[...]] + [jnp.zeros((lanes - types, feat), f32)], 0)
    table_t = jnp.transpose(table_pad)
    feat_out[...] = jnp.take_along_axis(
        table_t, jnp.broadcast_to(species, (feat, lanes)), axis=1
    )
    col_out[...] = jnp.transpose(jnp.broadcast_to(collector[...], (lanes, feat)))

    narrow = narrow_rows(feat)
    wide = wide_rows(feat, types)

    def put(rows, high_ref, low_ref, name, value, row=0, col=0):
        high, low = split(value)
        start = rows.at[name][0] + row
        high_ref[start : start + value.shape[0], col : col + value.shape[1]] = high
        low_ref[start : start + value.shape[0], col : col + value.shape[1]] = low

    per_half = feat // STRIDE
    for half in range(2):
        cols = slice(half * feat, (half + 1) * feat)
        for chunk in range(types // per_half):
            block = cat(
                [
                    filt[:, cols] * phi[t : t + 1, cols]
                    for t in range(chunk * per_half, (chunk + 1) * per_half)
                ],
                0,
            )
            put(wide, wh, wl, "B", block, chunk * feat, half * feat)
            put(wide, wh, wl, "BT", jnp.transpose(block), half * feat, chunk * feat)
    put(wide, wh, wl, "RQ", rotator[...], 0, 0)
    put(wide, wh, wl, "RQ", reflector[...], 0, feat)
    put(narrow, nh, nl, "RQT", jnp.transpose(rotator[...]), 0)
    put(narrow, nh, nl, "RQT", jnp.transpose(reflector[...]), feat)
    put(narrow, nh, nl, "C", combiner[...])
    put(wide, wh, wl, "CT", jnp.transpose(combiner[0:feat, :]), 0, 0)
    put(wide, wh, wl, "CT", jnp.transpose(combiner[feat : 2 * feat, :]), 0, feat)
    put(wide, wh, wl, "S", splitter[...])
    put(narrow, nh, nl, "ST", jnp.transpose(splitter[:, 0:feat]), 0)
    put(narrow, nh, nl, "ST", jnp.transpose(splitter[:, feat : 2 * feat]), feat)
    put(narrow, nh, nl, "R", readout[...])
    put(narrow, nh, nl, "RT", jnp.transpose(readout[...]))


def saved_rows(feat, types, slots):
    k = STRIDE * types
    pair = ("e", "e1", "e2", "ir", "u0", "u1", "u2", "t")
    sizes = [("A%d" % q, k) for q in range(4)]
    sizes += [("%s%d" % (n, c), feat) for n in ("v", "vb") for c in range(3)]
    sizes += [("%s%d" % (n, c), 2 * feat) for n in ("uw", "uwb") for c in range(3)]
    sizes += [("joined", 2 * feat), ("ab", 2 * feat)]
    sizes += [
        (n, feat)
        for n in ("z", "dz", "d2z", "a2", "q", "n", "s2", "yb", "yc", "ldy", "s2b", "zb", "hb", "qb", "nbn", "s1b")
    ]
    sizes += [("sin", slots * USED), ("cos", slots * USED)]
    sizes += [(n, slots) for n in pair]
    sizes += [("%s%d" % (n, q), slots) for n in ("sa", "sb", "sd") for q in range(4)]
    return Rows(sizes)


def multiples(c1, s1, sin_ref, cos_ref, slots):
    lanes = c1.shape[1]
    powers = [(c1, s1)]
    for _ in range(4):
        c, s = powers[-1]
        powers.append((c * c - s * s, 2.0 * c * s))
    sub = iota((8, lanes), 0)
    bits = [(sub // 2**b) % 2 == 1 for b in range(3)]
    order = sub.astype(f32) + 1.0

    def times(x, y):
        return x[0] * y[0] - x[1] * y[1], x[0] * y[1] + x[1] * y[0]

    for k in range(slots):
        rows = [
            tuple(jnp.broadcast_to(part[k : k + 1, :], (8, lanes)) for part in power)
            for power in powers
        ]
        z = rows[0]
        for b in range(3):
            step = (jnp.where(bits[b], rows[b][0], 1.0), jnp.where(bits[b], rows[b][1], 0.0))
            z = times(z, step)
        for v in range(3):
            if v == 1:
                zv = times(z, rows[3])
            elif v == 2:
                zv = times(z, rows[4])
            else:
                zv = z
            start = k * USED + 8 * v
            sin_ref[start : start + 8, :] = zv[1]
            cos_ref[start : start + 8, :] = zv[0] * ((order + 8.0 * v) * omega)


def slot_sums(read_sin, read_cos, sin_coef, cos_coef, kinds, slots, types, put):
    lanes = kinds.shape[1]
    for q in range(4):
        sums = [None] * types
        for k in range(slots):
            value = read_sin(k) * sin_coef[q][k : k + 1, :]
            if cos_coef is not None:
                value = value + read_cos(k) * cos_coef[q][k : k + 1, :]
            kind = jnp.broadcast_to(kinds[k : k + 1, :], value.shape)
            for t in range(types):
                part = jnp.where(kind == t, value, 0.0)
                sums[t] = part if sums[t] is None else sums[t] + part
        rest = jnp.zeros((STRIDE - USED, lanes), f32)
        put(q, cat([x for t in range(types) for x in (sums[t], rest)], 0))


def slot_reads(values, kinds, read_sin, read_cos, slots, types, put, with_square):
    lanes = kinds.shape[1]
    sub = iota((USED, lanes), 0).astype(f32) + 1.0
    square = sub * sub * (omega * omega)
    for q in range(4):
        tables = [values(q)[STRIDE * t : STRIDE * t + USED, :] for t in range(types)]
        for k in range(slots):
            kind = jnp.broadcast_to(kinds[k : k + 1, :], (USED, lanes))
            picked = tables[0]
            for t in range(1, types):
                picked = jnp.where(kind == t, tables[t], picked)
            with_sin = read_sin(k) * picked
            put("sa", q, k, jnp.sum(with_sin, axis=0, keepdims=True))
            put("sb", q, k, jnp.sum(read_cos(k) * picked, axis=0, keepdims=True))
            if with_square:
                put("sd", q, k, jnp.sum(with_sin * square, axis=0, keepdims=True))


def triple(rows, ref, name):
    return cat([rows.get(ref, "%s%d" % (name, c)) for c in range(3)], 1)


def thirds(value):
    n = value.shape[1] // 3
    return [value[:, c * n : (c + 1) * n] for c in range(3)]


def force_body(
    types, depth, left, right, from_left, from_right, own_rows, index, masks, features, colmat, nh, nl, wh, wl,
    low, high, pool, save, scratch,
):
    lanes = own_rows.shape[1]
    for j in range(4):
        pool[j, :, :] = whole((left, right, from_left, from_right), j)
    slots = index.shape[0] - 8
    feat = features.shape[0]
    rows = saved_rows(feat, types, slots)
    narrow = narrow_rows(feat)
    wide = wide_rows(feat, types)
    code = index[0:slots, :]
    mask = masks[0:slots, :]
    live = masks[slots : slots + 1, :]

    def coords(j, c):
        shift = pool_offsets(j, lanes)[c]
        row = pool[j, c : c + 1, :]
        return row if shift is None else row + shift

    deltas, radius = pool_deltas(coords, lambda c: own_rows[c : c + 1, :], code, lanes, depth)
    kinds = from_pool([pool[j, 7:8, :] for j in range(4)], code, lanes)
    inside = jnp.where(radius < cutoff, mask, 0.0)
    theta = omega * jnp.minimum(radius, cutoff)
    c1, s1 = jnp.cos(theta), jnp.sin(theta)
    ir = 1.0 / radius
    env = 0.5 * (c1 + 1.0) * inside
    e = env * ir
    e1 = ((-0.5 * omega) * s1 * inside - e) * ir
    e2 = ((-0.5 * omega * omega) * c1 * inside - 2.0 * e1) * ir
    unit = [d * ir for d in deltas]
    for name, value in (("e", e), ("e1", e1), ("e2", e2), ("ir", ir), ("t", kinds)):
        rows.put(save, name, value)
    for c in range(3):
        rows.put(save, "u%d" % c, unit[c])
    sin_at, cos_at = rows.at["sin"][0], rows.at["cos"][0]
    multiples(c1, s1, save.at[sin_at : sin_at + slots * USED, :], save.at[cos_at : cos_at + slots * USED, :], slots)

    def read_sin(k):
        return save[sin_at + k * USED : sin_at + (k + 1) * USED, :]

    def read_cos(k):
        return save[cos_at + k * USED : cos_at + (k + 1) * USED, :]

    coefs = [e] + [e * u for u in unit]
    slot_sums(read_sin, read_cos, coefs, None, kinds, slots, types, lambda q, v: rows.put(save, "A%d" % q, v))

    def nw(name):
        return narrow.get(nh, name), narrow.get(nl, name)

    def wd(name, first=None, last=None, rsl=slice(None)):
        return tuple(wide.get(r, name)[rsl, first:last] for r in (wh, wl))

    a0 = split(rows.get(save, "A0"))
    av = split(cat([rows.get(save, "A%d" % q) for q in (1, 2, 3)], 1))
    s_one = features[...] + dot3(wd("BT", rsl=slice(0, feat)), a0)
    v = dot3(wd("BT", rsl=slice(feat, 2 * feat)), av)
    uw = dot3(nw("RQT"), split(v))
    turned, mirrored = thirds(uw[0:feat]), thirds(uw[feat : 2 * feat])
    q = turned[0] * mirrored[0] + turned[1] * mirrored[1] + turned[2] * mirrored[2]
    n = jnp.sqrt(mirrored[0] * mirrored[0] + mirrored[1] * mirrored[1] + mirrored[2] * mirrored[2] + 1.0)
    joined = cat([s_one, n], 0)
    h = dot3(wd("CT"), split(joined))
    gate = lax.logistic(h)
    z = h * gate
    dz = gate * (1.0 + h * (1.0 - gate))
    d2z = gate * (1.0 - gate) * (2.0 + h * (1.0 - 2.0 * gate))
    a = dot3(nw("ST"), split(z))
    a2 = a[feat : 2 * feat]
    s_two = s_one + a[0:feat] + a2 * q
    y = dot3(nw("RT"), split(s_two))
    gate = lax.logistic(y)
    dy = gate * (1.0 + y * (1.0 - gate))
    d2y = gate * (1.0 - gate) * (2.0 + y * (1.0 - 2.0 * gate))
    ldy = dy * live
    yb = colmat[...] * ldy
    s2b = dot3(nw("R"), split(yb))
    ab = cat([s2b, s2b * q], 0)
    qb = s2b * a2
    zb = dot3(wd("S"), split(ab))
    hb = zb * dz
    jb = dot3(nw("C"), split(hb))
    s1b = s2b + jb[0:feat]
    nbn = jb[feat : 2 * feat] / n
    uwb = cat(
        [
            cat([qb * mirrored[c] for c in range(3)], 1),
            cat([nbn * mirrored[c] + qb * turned[c] for c in range(3)], 1),
        ],
        0,
    )
    vb = dot3(wd("RQ"), split(uwb))
    for name, value in (
        ("joined", joined), ("ab", ab), ("z", z), ("dz", dz), ("d2z", d2z), ("a2", a2), ("q", q), ("n", n),
        ("s2", s_two), ("yb", yb), ("yc", colmat[...] * live * d2y), ("ldy", ldy), ("s2b", s2b), ("zb", zb),
        ("hb", hb), ("qb", qb), ("nbn", nbn), ("s1b", s1b),
    ):
        rows.put(save, name, value)
    for name, value in (("v", v), ("uw", uw), ("uwb", uwb), ("vb", vb)):
        for c, part in enumerate(thirds(value)):
            rows.put(save, "%s%d" % (name, c), part)
    ab0 = dot3(wd("B", 0, feat), split(s1b))
    abv = thirds(dot3(wd("B", feat, 2 * feat), split(vb)))

    def put(name, q, k, row):
        start = rows.at["%s%d" % (name, q)][0] + k
        save[start : start + 1, :] = row

    tables = [ab0] + abv
    slot_reads(lambda q: tables[q], kinds, read_sin, read_cos, slots, types, put, True)
    sa = [rows.get(save, "sa%d" % q) for q in range(4)]
    sb = [rows.get(save, "sb%d" % q) for q in range(4)]
    z_sum = unit[0] * sa[1] + unit[1] * sa[2] + unit[2] * sa[3]
    x_sum = sb[0] + unit[0] * sb[1] + unit[1] * sb[2] + unit[2] * sb[3]
    rb = e * x_sum + e1 * (sa[0] + z_sum) - ir * e * z_sum
    deltas_bar = [rb * unit[c] + e * ir * sa[c + 1] for c in range(3)]
    pool_partials(deltas_bar, code, lambda j: index[slots + j : slots + j + 1, :], (low, high), scratch, lanes)


def centres_of(bins, bin_total):
    return 0.1 * jnp.sqrt(3600.0 * (bins.astype(f32) + 0.5) / bin_total)


def hist_body(
    depth, bin_total, pool, left, right, from_left, from_right, index, masks, bins,
    next_own, slopes, hist, moved, scratch,
):
    lanes = pool.shape[2]
    slots = index.shape[0] - 8
    code = index[0:slots, :]
    inverse = index[slots + 4 : slots + 5, :]
    mask = masks[0:slots, :]
    for j in range(4):
        kick = (0.5 * time_step * time_step) * pool[j, 6:7, :]
        force = whole((left, right, from_left, from_right), j)
        moved[j, 0:3, :] = pool[j, 0:3, :] + time_step * pool[j, 3:6, :] - kick * force[0:3, :]
    inverse8 = jnp.broadcast_to(inverse, (8, lanes))
    own = []
    for c in range(3):
        row = from_pool([moved[j, c : c + 1, :] for j in range(4)], inverse8, lanes)[0:1, :]
        next_own[c : c + 1, :] = row
        own.append(row)

    def coords(j, c):
        shift = pool_offsets(j, lanes)[c]
        row = moved[j, c : c + 1, :]
        return row if shift is None else row + shift

    deltas, radius = pool_deltas(coords, lambda c: own[c], code, lanes, depth)
    gap = radius - centres_of(bins[...], bin_total)
    kernel = jnp.exp(-gap * gap / sigma_two) * mask
    scale = kernel * gap * (-2.0 / sigma_two) / radius
    for c in range(3):
        slopes[c * slots : (c + 1) * slots, :] = scale * deltas[c]
    sums = scatter_lanes([kernel], bins[...], scratch, bin_total)
    hist[...] = jnp.broadcast_to(sums[0:1, :], hist.shape)


def adjoint_body(atoms_total, hists, target, slopes, index, bins, low, high, scratch):
    lanes = bins.shape[1]
    slots = bins.shape[0]
    code = index[0:slots, :]
    total = jnp.sum(hists[...], axis=0, keepdims=True)
    weights = 2.0 * (total / atoms_total - target[...]) / atoms_total
    picked = lane_take(weights, bins[...])
    deltas_bar = [picked * slopes[c * slots : (c + 1) * slots, :] for c in range(3)]
    pool_partials(deltas_bar, code, lambda j: index[slots + j : slots + j + 1, :], (low, high), scratch, lanes)


def grads_body(
    types, pool, left, right, from_left, from_right, index, save, colmat, phi, filt, nh, nl, wh, wl,
    keep, send, adjoint, after, tangents, grads,
):
    lanes = pool.shape[2]
    slots = index.shape[0] - 8
    feat = colmat.shape[0]
    rows = saved_rows(feat, types, slots)
    narrow = narrow_rows(feat)
    wide = wide_rows(feat, types)
    code = index[0:slots, :]
    inverse8 = jnp.broadcast_to(index[slots + 4 : slots + 5, :], (8, lanes))

    def get(name):
        return rows.get(save, name)

    for j in range(4):
        adjoint[j, :, :] = whole((left, right, from_left, from_right), j)
    probe = [
        [(0.5 * time_step * time_step) * pool[j, 6:7, :] * adjoint[j, c : c + 1, :] for j in range(4)]
        for c in range(3)
    ]
    moves = [
        from_pool(probe[c], code, lanes) - from_pool(probe[c], inverse8, lanes)[0:1, :] for c in range(3)
    ]
    e, e1, e2, ir, kinds = get("e"), get("e1"), get("e2"), get("ir"), get("t")
    unit = [get("u%d" % c) for c in range(3)]
    dr = unit[0] * moves[0] + unit[1] * moves[1] + unit[2] * moves[2]
    du = [(moves[c] - unit[c] * dr) * ir for c in range(3)]
    de, de1, dir_ = e1 * dr, e2 * dr, -ir * ir * dr
    sin_at, cos_at = rows.at["sin"][0], rows.at["cos"][0]

    def read_sin(k):
        return save[sin_at + k * USED : sin_at + (k + 1) * USED, :]

    def read_cos(k):
        return save[cos_at + k * USED : cos_at + (k + 1) * USED, :]

    k_rows = STRIDE * types

    def put_sum(q, value):
        tangents[q * k_rows : (q + 1) * k_rows, :] = value

    sin_coef = [de] + [de * unit[c] + e * du[c] for c in range(3)]
    cos_coef = [e * dr] + [e * dr * unit[c] for c in range(3)]
    slot_sums(read_sin, read_cos, sin_coef, cos_coef, kinds, slots, types, put_sum)

    def nw(name):
        return narrow.get(nh, name), narrow.get(nl, name)

    def wd(name, first=None, last=None, rsl=slice(None)):
        return tuple(wide.get(r, name)[rsl, first:last] for r in (wh, wl))

    da_zero = tangents[0:k_rows, :]
    da_vec = cat([tangents[q * k_rows : (q + 1) * k_rows, :] for q in (1, 2, 3)], 1)
    ds1 = dot3(wd("BT", rsl=slice(0, feat)), split(da_zero))
    dv = dot3(wd("BT", rsl=slice(feat, 2 * feat)), split(da_vec))
    duw = dot3(nw("RQT"), split(dv))
    d_turn, d_mirr = thirds(duw[0:feat]), thirds(duw[feat : 2 * feat])
    turned = [get("uw%d" % c)[0:feat] for c in range(3)]
    mirrored = [get("uw%d" % c)[feat : 2 * feat] for c in range(3)]
    q, n, a2, dz, d2z = get("q"), get("n"), get("a2"), get("dz"), get("d2z")
    s2b, zb, qb, nbn = get("s2b"), get("zb"), get("qb"), get("nbn")
    dq = sum(d_turn[c] * mirrored[c] + turned[c] * d_mirr[c] for c in range(3))
    dn = sum(mirrored[c] * d_mirr[c] for c in range(3)) / n
    dj = cat([ds1, dn], 0)
    dh = dot3(wd("CT"), split(dj))
    dzt = dz * dh
    da = dot3(nw("ST"), split(dzt))
    da2 = da[feat : 2 * feat]
    ds2 = ds1 + da[0:feat] + da2 * q + a2 * dq
    dyt = dot3(nw("RT"), split(ds2))
    dyb = get("yc") * dyt
    ds2b = dot3(nw("R"), split(dyb))
    dab = cat([ds2b, ds2b * q + s2b * dq], 0)
    dqb = ds2b * a2 + s2b * da2
    dzb = dot3(wd("S"), split(dab))
    dhb = dzb * dz + zb * (d2z * dh)
    djb = dot3(nw("C"), split(dhb))
    ds1b = ds2b + djb[0:feat]
    dnbn = (djb[feat : 2 * feat] - nbn * dn) / n
    duwb = cat(
        [
            cat([dqb * mirrored[c] + qb * d_mirr[c] for c in range(3)], 1),
            cat(
                [
                    dnbn * mirrored[c] + nbn * d_mirr[c] + dqb * turned[c] + qb * d_turn[c]
                    for c in range(3)
                ],
                1,
            ),
        ],
        0,
    )
    dvb = dot3(wd("RQ"), split(duwb))

    def both(first, second, third, fourth):
        return -dot3(split(cat([first, second], 1)), split(cat([third, fourth], 1)), NT)

    parts = grads.shape[0]
    share = feat // parts
    rq = both(dv, triple(rows, save, "v"), triple(rows, save, "uwb"), duwb)
    cg = both(dj, get("joined"), get("hb"), dhb)
    sg = both(dzt, get("z"), get("ab"), dab)
    rg = both(ds2, get("s2"), get("yb"), dyb)
    bs = both(da_zero, get("A0"), get("s1b"), ds1b)
    bv = both(da_vec, cat([get("A%d" % i) for i in (1, 2, 3)], 1), triple(rows, save, "vb"), dvb)
    low, high = split(get("ldy") * dyt)
    ones = jnp.ones((16, lanes), bf16)
    col = -(dot1(ones, low, NT) + dot1(ones, high, NT))
    fg, pg = [], []
    for half, value in enumerate((bs, bv)):
        cols = slice(half * feat, (half + 1) * feat)
        total = None
        for t in range(types):
            block = value[STRIDE * t : STRIDE * t + USED, :]
            term = block * phi[t : t + 1, cols]
            total = term if total is None else total + term
            pg.append((half, t, jnp.sum(block * filt[0:USED, cols], axis=0, keepdims=True)))
        fg.append(total)
    base = 7 * share
    place = iota((10, lanes), 1)
    for part in range(parts):
        mine = slice(part * share, (part + 1) * share)
        grads[part, 0:share, :] = rq[mine, 0:feat]
        grads[part, share : 2 * share, :] = rq[mine, feat : 2 * feat]
        grads[part, 2 * share : 4 * share, :] = cg[2 * part * share : 2 * (part + 1) * share, :]
        grads[part, 4 * share : 5 * share, :] = sg[mine, 0:feat]
        grads[part, 5 * share : 6 * share, :] = sg[mine, feat : 2 * feat]
        grads[part, 6 * share : 7 * share, :] = rg[mine, :]
        for half, t, row in pg:
            at = base + half * types + t
            grads[part, at : at + 1, :] = row
        chosen = fg[part // 2]
        rolled = pltpu.roll(chosen, feat // 2, 1)
        here, there = (chosen, rolled) if part % 2 == 0 else (rolled, chosen)
        at = base + 2 * types
        grads[part, at : at + 10, :] = jnp.where(place < feat // 2, here[0:10, :], there[10:20, :])
        grads[part, at + 10 : at + 11, :] = col[0:1, :]
        grads[part, at + 11 :, :] = jnp.zeros((grads.shape[1] - at - 11, lanes), f32)

    odd = lax.axis_index("slab") % 2
    half = grads.shape[1] // 2
    keep[...] = grads[:, pl.ds(pl.multiple_of(odd * half, half), half), :]
    send[...] = grads[:, pl.ds(pl.multiple_of((1 - odd) * half, half), half), :]
    for c in range(3):
        after[c * slots : (c + 1) * slots, :] = du[c]
        after[4 * slots + (c + 1) * feat : 4 * slots + (c + 2) * feat, :] = dvb[:, c * lanes : (c + 1) * lanes]
    after[3 * slots : 4 * slots, :] = dr
    after[4 * slots : 4 * slots + feat, :] = ds1b


def moves_body(types, index, save, after, wh, wl, low, high, sums, scratch):
    lanes = index.shape[1]
    slots = index.shape[0] - 8
    feat = lanes
    rows = saved_rows(feat, types, slots)
    wide = wide_rows(feat, types)
    code = index[0:slots, :]

    def get(name):
        return rows.get(save, name)

    def wd(name, first, last):
        return tuple(wide.get(r, name)[:, first:last] for r in (wh, wl))

    e, e1, e2, ir, kinds = get("e"), get("e1"), get("e2"), get("ir"), get("t")
    unit = [get("u%d" % c) for c in range(3)]
    du = [after[c * slots : (c + 1) * slots, :] for c in range(3)]
    dr = after[3 * slots : 4 * slots, :]
    de, de1, dir_ = e1 * dr, e2 * dr, -ir * ir * dr
    sin_at, cos_at = rows.at["sin"][0], rows.at["cos"][0]

    def read_sin(k):
        return save[sin_at + k * USED : sin_at + (k + 1) * USED, :]

    def read_cos(k):
        return save[cos_at + k * USED : cos_at + (k + 1) * USED, :]

    ds1b = after[4 * slots : 4 * slots + feat, :]
    dvb = cat([after[4 * slots + (c + 1) * feat : 4 * slots + (c + 2) * feat, :] for c in range(3)], 1)
    dab0 = dot3(wd("B", 0, feat), split(ds1b))
    dabv = thirds(dot3(wd("B", feat, 2 * feat), split(dvb)))
    tables = [dab0] + dabv

    def put(name, q, k, row):
        start = (0 if name == "sa" else 4 * slots) + q * slots + k
        sums[start : start + 1, :] = row

    slot_reads(lambda q: tables[q], kinds, read_sin, read_cos, slots, types, put, False)
    sa = [get("sa%d" % q) for q in range(4)]
    sb = [get("sb%d" % q) for q in range(4)]
    sd = [get("sd%d" % q) for q in range(4)]
    dsa = [sb[q] * dr + sums[q * slots : (q + 1) * slots, :] for q in range(4)]
    dsb = [
        sums[(4 + q) * slots : (5 + q) * slots, :] - sd[q] * dr for q in range(4)
    ]
    z_sum = sum(unit[c] * sa[c + 1] for c in range(3))
    x_sum = sb[0] + sum(unit[c] * sb[c + 1] for c in range(3))
    dz_sum = sum(du[c] * sa[c + 1] + unit[c] * dsa[c + 1] for c in range(3))
    dx_sum = dsb[0] + sum(du[c] * sb[c + 1] + unit[c] * dsb[c + 1] for c in range(3))
    rb = e * x_sum + e1 * (sa[0] + z_sum) - ir * e * z_sum
    drb = (
        de * x_sum + e * dx_sum + de1 * (sa[0] + z_sum) + e1 * (dsa[0] + dz_sum)
        - (dir_ * e + ir * de) * z_sum - ir * e * dz_sum
    )
    deltas_bar = [
        drb * unit[c] + rb * du[c] + (de * ir + e * dir_) * sa[c + 1] + e * ir * dsa[c + 1]
        for c in range(3)
    ]
    pool_partials(deltas_bar, code, lambda j: index[slots + j : slots + j + 1, :], (low, high), scratch, lanes)


def last_body(
    types, parts, atoms_total, mine, other, adjoint, second, index, types_in, spreader, next_own,
    next_out, adj, enc, spr, fil, rot, ref, com, spl, rea, col, total,
):
    next_out[...] = next_own[...]
    odd = lax.axis_index("slab") % 2
    half = mine.shape[0]
    total[pl.ds(pl.multiple_of(odd * half, half), half), :] = mine[...]
    total[pl.ds(pl.multiple_of((1 - odd) * half, half), half), :] = other[...]
    lanes = adjoint.shape[2]
    slots = index.shape[0] - 8
    feat = lanes
    share = feat // parts
    inverse8 = jnp.broadcast_to(index[slots + 4 : slots + 5, :], (8, lanes))
    for c in range(3):
        rows = [
            atoms_total * (adjoint[j, c : c + 1, :] - second[j, c : c + 1, :]) for j in range(4)
        ]
        adj[c : c + 1, :] = from_pool(rows, inverse8, lanes)[0:1, :]
    rot[...] = total[0:share, :]
    ref[...] = total[share : 2 * share, :]
    com[...] = total[2 * share : 4 * share, :]
    spl[:, 0:feat] = total[4 * share : 5 * share, :]
    spl[:, feat : 2 * feat] = total[5 * share : 6 * share, :]
    rea[...] = total[6 * share : 7 * share, :]
    base = 7 * share
    phib = cat([total[base : base + types, :], total[base + types : base + 2 * types, :]], 1)
    at = base + 2 * types
    block = total[at : at + 10, :]
    fil[0:10, :] = block[:, 0 : feat // 2]
    fil[10:20, :] = pltpu.roll(block, feat // 2, 1)[:, 0 : feat // 2]
    col_row = total[at + 10 : at + 11, :]
    hidden = types_in[0:types, :]
    slope = types_in[types : 2 * types, :]
    table = types_in[2 * types : 3 * types, :]

    def exact(a, b, dims):
        return lax.dot_general(a, b, (dims, ((), ())), precision=highest, preferred_element_type=f32)

    pre_bar = exact(phib, spreader[...], NT) * slope
    pad = jnp.zeros((lanes - types, feat), f32)
    hidden_t = jnp.transpose(cat([hidden, pad], 0))
    table_t = jnp.transpose(cat([table, pad], 0))
    wide_pad = jnp.zeros((lanes - types, 2 * feat), f32)
    full_spr = exact(hidden_t, cat([phib, wide_pad], 0), NN)
    full_enc = exact(table_t, cat([pre_bar, pad], 0), NN)
    for part in range(parts):
        @pl.when(lax.axis_index("cross") == part)
        def _():
            spr[...] = full_spr[part * share : (part + 1) * share, :]
            enc[...] = full_enc[part * share : (part + 1) * share, :]
            col[...] = col_row[:, part * share : (part + 1) * share]


def shift(x, axis, step):
    count = lax.axis_size(axis)
    return lax.ppermute(x, axis, [(i, (i + step) % count) for i in range(count)])


def corner_sum(low, high):
    left, right = call(
        turn_body, [(low.shape, f32)] * 2, low, high, shift(high, "slab", 1), shift(low, "slab", -1)
    )
    return left, right, shift(right, "cross", 1), shift(left, "cross", -1)


def swap(x, axis, bit):
    return lax.ppermute(x, axis, [(i, i ^ bit) for i in range(lax.axis_size(axis))])


def halve(bit, x, other, keep, send):
    mine = (lax.axis_index("cross") // bit) % 2
    shape = (x.shape[0] // 2, 2) + x.shape[1:]
    x, other = x.reshape(shape), other.reshape(shape)
    for ref, side in ((keep, mine), (send, 1 - mine)):
        value = x[:, pl.ds(side, 1)] + other[:, pl.ds(side, 1)]
        ref[...] = value.reshape(ref.shape)


def halve_hold_body(bit, x, other, low, high, keep, send, low_out, high_out):
    halve(bit, x, other, keep, send)
    low_out[...] = low[...]
    high_out[...] = high[...]


def halve_turn_body(bit, x, other, low, high, from_down, from_up, keep, send, left, right):
    halve(bit, x, other, keep, send)
    turn_body(low, high, from_down, from_up, left, right)


def add_body(x, other, out):
    out[...] = x[...] + other[...]


def add_whole_body(x, other, left, right, from_left, from_right, out, total):
    add_body(x, other, out)
    for j in range(4):
        total[j, :, :] = whole((left, right, from_left, from_right), j)


def reduce_all(keep, send, low, high):
    slab_count, cross_count = lax.axis_size("slab"), lax.axis_size("cross")
    group = (low.shape, f32)
    other = swap(send, "slab", 1)
    bit, step, pieces = 1, 0, None
    while bit < cross_count:
        half = ((keep.shape[0] // 2,) + keep.shape[1:], f32)
        if step == 0:
            keep, send, low, high = call(
                functools.partial(halve_hold_body, bit), [half, half, group, group], keep, other, low, high
            )
            from_down, from_up = shift(high, "slab", 1), shift(low, "slab", -1)
        elif step == 1:
            keep, send, left, right = call(
                functools.partial(halve_turn_body, bit), [half, half, group, group],
                keep, other, low, high, from_down, from_up,
            )
            pieces = (left, right, shift(right, "cross", 1), shift(left, "cross", -1))
        else:
            raise NotImplementedError
        other = swap(send, "cross", bit)
        bit, step = 2 * bit, step + 1
    x, other = keep[0], other[0]
    bit, total = 2, None
    while bit < slab_count:
        if bit == 4:
            x, total = call(add_whole_body, [(x.shape, f32), ((4,) + low.shape[1:], f32)], x, other, *pieces)
        else:
            (x,) = call(add_body, [(x.shape, f32)], x, other)
        other = swap(x, "slab", bit)
        bit *= 2
    (x,) = call(add_body, [(x.shape, f32)], x, other)
    return x, swap(x, "slab", 1), total


def on_device(
    positions, velocities, inverse_mass, species, type_table, neighbours, slot_count, atom_count,
    pair_bins, send_list, target, encoder, spreader, filters, rotator, reflector, combiner, splitter,
    readout, collector,
):
    lanes = positions.shape[1]
    slots = neighbours.shape[1]
    types, feat = type_table.shape
    bin_total = target.shape[0]
    slab_count, cross_count = lax.axis_size("slab"), lax.axis_size("cross")
    devices = slab_count * cross_count
    atoms_total = float(lanes * devices)
    depth = 1.6 * (lanes // 16)
    parts = cross_count
    row = lambda x: x.reshape(1, x.shape[0])
    i32 = jnp.int32
    vm, dma = pltpu.VMEM, pltpu.SemaphoreType.DMA
    narrow, wide = narrow_rows(feat).total, wide_rows(feat, types).total
    group = ((2, 8, lanes), f32)
    pool_shape = ((4, 8, lanes), f32)
    pair_scratch = vm((16 * slots, lanes), f32)
    low, high, own_rows, send = call(
        offer_body, [group, group, ((8, lanes), f32), ((8, lanes), i32)],
        *in_hbm(positions, velocities, row(inverse_mass), row(species), send_list),
        specs=[HB] * 5,
        scratch=[
            vm((3, lanes), f32), vm((3, lanes), f32), vm((1, lanes), f32), vm((1, lanes), i32),
            vm(send_list.shape, i32), dma((5,)),
        ],
    )
    index, masks, features, colmat, nh, nl, wh, wl, phi, types_in, filt, bins, goal, spreader_in = call(
        prep_body,
        [
            ((slots + 8, lanes), i32), ((slots + 8, lanes), f32), ((feat, lanes), f32), ((feat, lanes), f32),
            ((narrow, feat), bf16), ((narrow, feat), bf16), ((wide, 2 * feat), bf16), ((wide, 2 * feat), bf16),
            ((types, 2 * feat), f32), ((3 * types, feat), f32), ((STRIDE, 2 * feat), f32),
            ((slots, lanes), i32), ((1, bin_total), f32), (spreader.shape, f32),
        ],
        *in_hbm(
            neighbours.T, row(slot_count), type_table, encoder, spreader, filters, rotator, reflector, combiner,
            splitter, readout, row(collector), pair_bins.T, row(target),
        ),
        atom_count, send, own_rows,
        specs=[HB] * 14 + [SM] + [VM] * 2,
        scratch=[
            vm((slots, lanes), i32), vm((1, lanes), i32), vm(type_table.shape, f32), vm(encoder.shape, f32),
            vm(filters.shape, f32), vm(rotator.shape, f32), vm(reflector.shape, f32), vm(combiner.shape, f32),
            vm(splitter.shape, f32), vm(readout.shape, f32), vm((1, feat), f32), dma((14,)),
        ],
    )
    pieces = corner_sum(low, high)
    save_rows = saved_rows(feat, types, slots).total
    low, high, pool, save = call(
        functools.partial(force_body, types, depth),
        [group, group, pool_shape, ((save_rows, lanes), f32)],
        *pieces, own_rows, index, masks, features, colmat, nh, nl, wh, wl,
        scratch=[pair_scratch],
    )
    pieces = corner_sum(low, high)
    next_positions, slopes, hist = call(
        functools.partial(hist_body, depth, bin_total),
        [((3, lanes), f32), ((3 * slots, lanes), f32), ((devices, bin_total), f32)],
        pool, *pieces, index, masks, bins,
        scratch=[vm((4, 8, lanes), f32), pair_scratch],
    )
    hists = lax.all_to_all(hist.reshape(devices, 1, bin_total), ("slab", "cross"), 0, 0)
    low, high = call(
        functools.partial(adjoint_body, atoms_total), [group, group],
        hists.reshape(devices, bin_total), goal, slopes, index, bins,
        scratch=[pair_scratch],
    )
    pieces = corner_sum(low, high)
    half_grads = ((parts, feat, lanes), f32)
    keep, send, adjoint, after = call(
        functools.partial(grads_body, types),
        [half_grads, half_grads, pool_shape, ((4 * slots + 4 * feat, lanes), f32)],
        pool, *pieces, index, save, colmat, phi, filt, nh, nl, wh, wl,
        scratch=[vm((4 * STRIDE * types, lanes), f32), vm((parts, 2 * feat, lanes), f32)],
    )
    low, high = call(
        functools.partial(moves_body, types), [group, group], index, save, after, wh, wl,
        scratch=[vm((8 * slots, lanes), f32), pair_scratch],
    )
    mine, other, second = reduce_all(keep, send, low, high)
    share = feat // parts
    results = call(
        functools.partial(last_body, types, parts, atoms_total),
        [
            ((3, lanes), f32), ((3, lanes), f32), ((share, feat), f32), ((share, 2 * feat), f32),
            ((filters.shape[0], 2 * feat // parts), f32), ((share, feat), f32), ((share, feat), f32),
            ((2 * share, feat), f32), ((share, 2 * feat), f32), ((share, feat), f32), ((1, share), f32),
        ],
        mine, other, adjoint, second, index, types_in, spreader_in, next_positions,
        scratch=[vm((2 * feat, lanes), f32)],
        keep=False,
    )
    return tuple(results[:10]) + (results[10].reshape(share),)


def solution(mesh):
    both = ("slab", "cross")
    in_specs = (
        P(None, both), P(None, both), P(both), P(both), P(), P(both, None), P(both), P(both), P(both, None),
        P("slab", "cross", None),
    ) + (P(),) * 10
    out_specs = (
        P(None, both), P(None, both), P("cross", None), P("cross", None), P(None, "cross"), P("cross", None),
        P("cross", None), P("cross", None), P("cross", None), P("cross", None), P("cross"),
    )
    return jax.shard_map(on_device, mesh=mesh, in_specs=in_specs, out_specs=out_specs, check_vma=False)
```

```python
import functools

import jax
import jax.numpy as jnp
from jax import lax
from jax.experimental import pallas as pl
from jax.experimental.pallas import tpu as pltpu
from jax.sharding import PartitionSpec as P


cutoff = 5.0
soften = 0.25
sigma_two = 0.18
slab_length = 10.0
cell_length = 10.0
time_step = 0.5
highest = lax.Precision.HIGHEST
f32 = jnp.float32
bf16 = jnp.bfloat16
pi = 3.141592653589793
omega = pi / cutoff

NN = ((1,), (0,))
NT = ((1,), (1,))
VM = pl.BlockSpec(memory_space=pltpu.VMEM)
SM = pl.BlockSpec(memory_space=pltpu.SMEM)
HB = pl.BlockSpec(memory_space=pltpu.HBM)


def call(body, outs, *args, specs=None, scratch=(), keep=True):
    return pl.pallas_call(
        body,
        out_shape=[(pltpu.VMEM if keep else jax.ShapeDtypeStruct)(s, d) for s, d in outs],
        in_specs=[VM] * len(args) if specs is None else specs,
        out_specs=[VM] * len(outs),
        scratch_shapes=list(scratch),
        compiler_params=pltpu.CompilerParams(vmem_limit_bytes=16 * 2**20),
    )(*args)


def in_hbm(*arrays):
    return [pltpu.with_memory_space_constraint(x, pltpu.HBM) for x in arrays]


def fetch(sources, targets, semaphores):
    copies = [
        pltpu.make_async_copy(source, target, semaphores.at[i])
        for i, (source, target) in enumerate(zip(sources, targets))
    ]
    for copy in copies:
        copy.start()
    for copy in copies:
        copy.wait()


def split(x):
    high = x.astype(bf16)
    return high, (x - high.astype(f32)).astype(bf16)


def dot1(a, b, dims):
    return lax.dot_general(a, b, (dims, ((), ())), preferred_element_type=f32)


def dot3(a, b, dims=NN):
    return dot1(
        jnp.concatenate([a[0], a[0], a[1]], dims[0][0]), jnp.concatenate([b[0], b[1], b[0]], dims[1][0]), dims
    )


def cat(parts, axis):
    return jnp.concatenate(parts, axis=axis)


def iota(shape, dim):
    return lax.broadcasted_iota(jnp.int32, shape, dim)


def lane_take(row, index):
    return jnp.take_along_axis(jnp.broadcast_to(row, index.shape), index, axis=1)


def own_lanes(group, lanes):
    quarter = lanes // 4
    start = 2 * quarter * (1 - group // 2) + quarter * (1 - group % 2)
    return start, quarter


def pool_offsets(group, lanes):
    place = iota((1, lanes), 1)
    up, right = group // 2, group % 2
    half, quarter = lanes // 2, lanes // 4
    first = (place >= half) if up else (place < half)
    second_bit = place % half >= quarter
    second = second_bit if right else jnp.logical_not(second_bit)
    sign_u, sign_r = 2.0 * up - 1.0, 2.0 * right - 1.0
    return (
        jnp.where(first, sign_u * slab_length, 0.0).astype(f32),
        jnp.where(second, sign_r * cell_length, 0.0).astype(f32),
        None,
    )


def from_pool(rows, code, lanes):
    group = code // lanes
    lane = code % lanes
    out = lane_take(rows[0], lane)
    for j in range(1, 4):
        out = jnp.where(group == j, lane_take(rows[j], lane), out)
    return out


def pool_deltas(pool_rows, own_rows, code, lanes, depth):
    deltas = []
    for c in range(3):
        d = from_pool([pool_rows(j, c) for j in range(4)], code, lanes) - own_rows(c)
        if c == 2:
            d = d - depth * jnp.floor(d / depth + 0.5)
        deltas.append(d)
    radius = jnp.sqrt(deltas[0] * deltas[0] + deltas[1] * deltas[1] + deltas[2] * deltas[2] + soften)
    return deltas, radius


def one_hot_rows(index, slots, count):
    lanes = index.shape[1]
    place = iota((count, lanes), 0)
    return cat(
        [(place == index[k : k + 1, :]).astype(f32).astype(bf16) for k in range(slots)], 1
    )


def scatter_lanes(values, index, scratch, count):
    shape = index.shape
    slots = shape[0]
    for row in range(16):
        value = values[row] if row < len(values) else None
        if value is None:
            value = jnp.zeros(shape, f32)
        scratch[pl.ds(row, slots, stride=16), :] = value
    highs, mids, lows = [], [], []
    for k in range(slots):
        x = scratch[16 * k : 16 * k + 16, :]
        high = x.astype(bf16)
        rest = x - high.astype(f32)
        mid = rest.astype(bf16)
        highs.append(high)
        mids.append(mid)
        lows.append((rest - mid.astype(f32)).astype(bf16))
    left = cat([cat(highs, 1), cat(mids, 1), cat(lows, 1)], 0)
    sums = dot1(left, one_hot_rows(index, slots, count), NT)
    return sums[0:16] + (sums[16:32] + sums[32:48])


def pool_partials(deltas_bar, code, send_index, outs, scratch, lanes):
    group = code // lanes
    values = []
    for j in range(4):
        for c in range(3):
            values.append(jnp.where(group == j, deltas_bar[c], 0.0))
        values.append(None)
    sums = scatter_lanes(values, code % lanes, scratch, lanes)
    centres = [-jnp.sum(d, axis=0, keepdims=True) for d in deltas_bar]
    place = iota((1, lanes), 1)
    for j in range(4):
        start, width = own_lanes(j, lanes)
        own = jnp.logical_and(place >= start, place < start + width)
        out_ref = outs[j // 2]
        out_ref[j % 2, :, :] = jnp.zeros((8, lanes), f32)
        for c in range(3):
            mine = lane_take(jnp.broadcast_to(centres[c], (8, lanes)), jnp.broadcast_to(send_index(j), (8, lanes)))
            out_ref[j % 2, c : c + 1, :] = sums[4 * j + c : 4 * j + c + 1, :] + jnp.where(
                own, mine[0:1, :], 0.0
            )


def offer_body(
    pos, vel, mass, species, send_list, low, high, own_out, send_out,
    pos_v, vel_v, mass_v, species_v, list_v, semaphores,
):
    fetch((pos, vel, mass, species, send_list), (pos_v, vel_v, mass_v, species_v, list_v), semaphores)
    lanes = pos.shape[1]
    own_out[0:3, :] = pos_v[...]
    own_out[3:6, :] = vel_v[...]
    own_out[6:7, :] = mass_v[...]
    own_out[7:8, :] = species_v[...].astype(f32)
    own_rows = own_out[...]
    place = iota((8, lanes), 1)
    send_out[...] = jnp.zeros((8, lanes), jnp.int32)
    for j in range(4):
        start, width = own_lanes(j, lanes)
        pieces = [list_v[j // 2, j % 2 : j % 2 + 1, :]]
        if start:
            pieces = [jnp.zeros((1, start), jnp.int32)] + pieces
        if start + width < lanes:
            pieces = pieces + [jnp.zeros((1, lanes - start - width), jnp.int32)]
        row = cat(pieces, 1)
        send_out[j : j + 1, :] = row
        own = jnp.logical_and(place >= start, place < start + width)
        taken = jnp.take_along_axis(own_rows, jnp.broadcast_to(row, (8, lanes)), axis=1)
        out = (low, high)[j // 2]
        out[j % 2, :, :] = jnp.where(own, taken, 0.0)


def turn_body(low, high, from_down, from_up, left, right):
    for u, (mine, other) in enumerate(((low, from_down), (high, from_up))):
        left[u, :, :] = mine[0] + other[0]
        right[u, :, :] = mine[1] + other[1]


def whole(pieces, j):
    right = j % 2
    return pieces[right][j // 2] + pieces[2 + right][j // 2]


class Rows:
    def __init__(self, sizes):
        self.at = {}
        self.total = 0
        for name, size in sizes:
            self.at[name] = (self.total, size)
            self.total += size

    def get(self, ref, name):
        start, size = self.at[name]
        return ref[start : start + size, :]

    def put(self, ref, name, value):
        start, size = self.at[name]
        ref[start : start + size, :] = value


STRIDE = 32
USED = 24


def narrow_rows(feat):
    return Rows((("RQT", 2 * feat), ("C", 2 * feat), ("ST", 2 * feat), ("RT", feat), ("R", feat)))


def wide_rows(feat, types):
    return Rows((("BT", 2 * feat), ("B", STRIDE * types), ("RQ", feat), ("CT", feat), ("S", feat)))


def weights_body(
    table_h, encoder_h, spreader_h, filters_h, rotator_h, reflector_h, combiner_h, splitter_h, readout_h,
    collector_h, col_out, nh, nl, wh, wl, phi_out, slope_out, hidden_t, table_t, filt_out, spreader,
    table, encoder, filters, rotator, reflector, combiner, splitter, readout, collector, semaphores,
):
    fetch(
        (table_h, encoder_h, spreader_h, filters_h, rotator_h, reflector_h, combiner_h, splitter_h, readout_h,
         collector_h),
        (table, encoder, spreader, filters, rotator, reflector, combiner, splitter, readout, collector),
        semaphores,
    )
    types, feat = table.shape
    lanes = hidden_t.shape[1]
    basis = filters.shape[0]
    pre = jnp.dot(table[...], encoder[...], precision=highest, preferred_element_type=f32)
    gate = lax.logistic(pre)
    hidden = pre * gate
    phi = jnp.dot(hidden, spreader[...], precision=highest, preferred_element_type=f32)
    phi_out[...] = phi
    slope_out[...] = gate * (1.0 + pre * (1.0 - gate))
    rest = [jnp.zeros((lanes - types, feat), f32)]
    hidden_t[...] = jnp.transpose(cat([hidden] + rest, 0))
    table_t[...] = jnp.transpose(cat([table[...]] + rest, 0))
    filt_out[...] = jnp.zeros(filt_out.shape, f32)
    filt_out[0:basis, :] = filters[...]
    filt = filt_out[...]
    col_out[...] = jnp.transpose(jnp.broadcast_to(collector[...], (lanes, feat)))
    narrow = narrow_rows(feat)
    wide = wide_rows(feat, types)

    def put(rows, high_ref, low_ref, name, value, row=0, col=0):
        high, low = split(value)
        start = rows.at[name][0] + row
        high_ref[start : start + value.shape[0], col : col + value.shape[1]] = high
        low_ref[start : start + value.shape[0], col : col + value.shape[1]] = low

    per_half = feat // STRIDE
    for half in range(2):
        cols = slice(half * feat, (half + 1) * feat)
        for chunk in range(types // per_half):
            block = cat(
                [
                    filt[:, cols] * phi[t : t + 1, cols]
                    for t in range(chunk * per_half, (chunk + 1) * per_half)
                ],
                0,
            )
            put(wide, wh, wl, "B", block, chunk * feat, half * feat)
            put(wide, wh, wl, "BT", jnp.transpose(block), half * feat, chunk * feat)
    put(wide, wh, wl, "RQ", rotator[...], 0, 0)
    put(wide, wh, wl, "RQ", reflector[...], 0, feat)
    put(narrow, nh, nl, "RQT", jnp.transpose(rotator[...]), 0)
    put(narrow, nh, nl, "RQT", jnp.transpose(reflector[...]), feat)
    put(narrow, nh, nl, "C", combiner[...])
    put(wide, wh, wl, "CT", jnp.transpose(combiner[0:feat, :]), 0, 0)
    put(wide, wh, wl, "CT", jnp.transpose(combiner[feat : 2 * feat, :]), 0, feat)
    put(wide, wh, wl, "S", splitter[...])
    put(narrow, nh, nl, "ST", jnp.transpose(splitter[:, 0:feat]), 0)
    put(narrow, nh, nl, "ST", jnp.transpose(splitter[:, feat : 2 * feat]), feat)
    put(narrow, nh, nl, "R", readout[...])
    put(narrow, nh, nl, "RT", jnp.transpose(readout[...]))


def index_body(
    near_h, count_h, bins_h, target_h, atom_count, send, own_rows, table_t,
    index, masks, feat_out, bins, target, near, slot_count, semaphores,
):
    fetch((near_h, count_h, bins_h, target_h), (near, slot_count, bins, target), semaphores)
    species = own_rows[7:8, :].astype(jnp.int32)
    slots, lanes = near.shape
    quarter = lanes // 4
    lane_row = iota((16, lanes), 1).astype(f32)
    row_id = iota((16, lanes), 0)
    lefts, rights = [], []
    place = iota((lanes, lanes), 1)
    for j in range(4):
        start, width = own_lanes(j, lanes)
        own = jnp.logical_and(place >= start, place < start + width)
        same = jnp.logical_and(own, iota((lanes, lanes), 0) == send[j : j + 1, :])
        rights.append(same.astype(f32).astype(bf16))
        lefts.append(
            jnp.where(row_id == 0, lane_row, jnp.where(row_id == 1, float(j), 0.0)).astype(bf16)
        )
    found = dot1(cat(lefts, 1), cat(rights, 1), NT)
    inverse = (found[0:1, :] + lanes * found[1:2, :] + 0.5).astype(jnp.int32)
    near_v = near[...]
    ghost = near_v - lanes
    block = ghost // quarter
    p, q, g = block // 4, block % 4, ghost % quarter
    ghost_code = (2 * (p // 2) + q // 2) * lanes + 2 * quarter * (p % 2) + quarter * (q % 2) + g
    own_code = lane_take(inverse, jnp.minimum(near_v, lanes - 1))
    index[...] = jnp.zeros(index.shape, jnp.int32)
    index[0:slots, :] = jnp.where(near_v < lanes, own_code, ghost_code)
    index[slots : slots + 4, :] = send[0:4, :]
    index[slots + 4 : slots + 5, :] = inverse
    masks[...] = jnp.zeros(masks.shape, f32)
    masks[0:slots, :] = (iota((slots, lanes), 0) < slot_count[...]).astype(f32)
    masks[slots : slots + 1, :] = (iota((1, lanes), 1) < atom_count[0]).astype(f32)
    feat_out[...] = jnp.take_along_axis(table_t[...], jnp.broadcast_to(species, table_t.shape), axis=1)


def saved_rows(feat, types, slots):
    k = STRIDE * types
    pair = ("e", "e1", "e2", "ir", "u0", "u1", "u2", "t")
    sizes = [("A%d" % q, k) for q in range(4)]
    sizes += [("%s%d" % (n, c), feat) for n in ("v", "vb") for c in range(3)]
    sizes += [("%s%d" % (n, c), 2 * feat) for n in ("uw", "uwb") for c in range(3)]
    sizes += [("joined", 2 * feat), ("ab", 2 * feat)]
    sizes += [
        (n, feat)
        for n in ("z", "dz", "d2z", "a2", "q", "n", "s2", "yb", "yc", "ldy", "s2b", "zb", "hb", "qb", "nbn", "s1b")
    ]
    sizes += [("sin", slots * USED), ("cos", slots * USED), ("mask", 8 * slots * types)]
    sizes += [(n, slots) for n in pair]
    sizes += [("%s%d" % (n, q), slots) for n in ("sa", "sb", "sd") for q in range(4)]
    return Rows(sizes)


def multiples(c1, s1, sin_ref, cos_ref, slots):
    lanes = c1.shape[1]
    powers = [(c1, s1)]
    for _ in range(4):
        c, s = powers[-1]
        powers.append((c * c - s * s, 2.0 * c * s))
    sub = iota((8, lanes), 0)
    bits = [(sub // 2**b) % 2 == 1 for b in range(3)]
    order = sub.astype(f32) + 1.0

    def times(x, y):
        return x[0] * y[0] - x[1] * y[1], x[0] * y[1] + x[1] * y[0]

    for k in range(slots):
        rows = [
            tuple(jnp.broadcast_to(part[k : k + 1, :], (8, lanes)) for part in power)
            for power in powers
        ]
        z = rows[0]
        for b in range(3):
            step = (jnp.where(bits[b], rows[b][0], 1.0), jnp.where(bits[b], rows[b][1], 0.0))
            z = times(z, step)
        for v in range(3):
            if v == 1:
                zv = times(z, rows[3])
            elif v == 2:
                zv = times(z, rows[4])
            else:
                zv = z
            start = k * USED + 8 * v
            sin_ref[start : start + 8, :] = zv[1]
            cos_ref[start : start + 8, :] = zv[0] * ((order + 8.0 * v) * omega)


def type_masks(kinds, types, put):
    slots, lanes = kinds.shape
    for k in range(slots):
        kind = jnp.broadcast_to(kinds[k : k + 1, :], (8, lanes))
        for t in range(types):
            put(k * types + t, jnp.where(kind == t, 1.0, 0.0))


def choose(options, bits):
    for bit in bits:
        options = [
            jnp.where(bit, options[i + 1], options[i]) if i + 1 < len(options) else options[i]
            for i in range(0, len(options), 2)
        ]
    return options[0]


def slot_sums(read_sin, read_cos, sin_coef, cos_coef, read_mask, slots, types, put):
    lanes = sin_coef[0].shape[1]
    tiles = USED // 8
    for q in range(4):
        sums = [[None] * tiles for _ in range(types)]
        for k in range(slots):
            value = read_sin(k) * sin_coef[q][k : k + 1, :]
            if cos_coef is not None:
                value = value + read_cos(k) * cos_coef[q][k : k + 1, :]
            for t in range(types):
                mask = read_mask(k * types + t)
                for v in range(tiles):
                    part = value[8 * v : 8 * v + 8] * mask
                    sums[t][v] = part if sums[t][v] is None else sums[t][v] + part
        rest = jnp.zeros((STRIDE - USED, lanes), f32)
        put(q, cat([x for t in range(types) for x in sums[t] + [rest]], 0))


def slot_reads(values, kinds, read_sin, read_cos, slots, types, put, with_square):
    lanes = kinds.shape[1]
    tiles = USED // 8
    whole_kinds = (kinds + 0.5).astype(jnp.int32)
    kind_bits = [((whole_kinds // 2**b) % 2).astype(f32) for b in range((types - 1).bit_length())]
    square = [((iota((8, lanes), 0).astype(f32) + (8.0 * v + 1.0)) * omega) ** 2 for v in range(tiles)]
    for q in range(4):
        value = values(q)
        tables = [
            [value[STRIDE * t + 8 * v : STRIDE * t + 8 * v + 8] for v in range(tiles)] for t in range(types)
        ]
        for k in range(slots):
            bits = [jnp.broadcast_to(part[k : k + 1, :], (8, lanes)) > 0.5 for part in kind_bits]
            picked = [choose([table[v] for table in tables], bits) for v in range(tiles)]
            sines, cosines = read_sin(k), read_cos(k)
            with_sin = [sines[8 * v : 8 * v + 8] * picked[v] for v in range(tiles)]
            put("sa", q, k, jnp.sum(sum(with_sin), axis=0, keepdims=True))
            with_cos = [cosines[8 * v : 8 * v + 8] * picked[v] for v in range(tiles)]
            put("sb", q, k, jnp.sum(sum(with_cos), axis=0, keepdims=True))
            if with_square:
                with_sin = [with_sin[v] * square[v] for v in range(tiles)]
                put("sd", q, k, jnp.sum(sum(with_sin), axis=0, keepdims=True))


def triple(rows, ref, name):
    return cat([rows.get(ref, "%s%d" % (name, c)) for c in range(3)], 1)


def thirds(value):
    n = value.shape[1] // 3
    return [value[:, c * n : (c + 1) * n] for c in range(3)]


def force_body(
    types, depth, left, right, from_left, from_right, own_rows, index, masks, features, colmat, nh, nl, wh, wl,
    low, high, pool, save, scratch,
):
    lanes = own_rows.shape[1]
    for j in range(4):
        pool[j, :, :] = whole((left, right, from_left, from_right), j)
    slots = index.shape[0] - 8
    feat = features.shape[0]
    rows = saved_rows(feat, types, slots)
    narrow = narrow_rows(feat)
    wide = wide_rows(feat, types)
    code = index[0:slots, :]
    mask = masks[0:slots, :]
    live = masks[slots : slots + 1, :]

    def coords(j, c):
        shift = pool_offsets(j, lanes)[c]
        row = pool[j, c : c + 1, :]
        return row if shift is None else row + shift

    deltas, radius = pool_deltas(coords, lambda c: own_rows[c : c + 1, :], code, lanes, depth)
    kinds = from_pool([pool[j, 7:8, :] for j in range(4)], code, lanes)
    inside = jnp.where(radius < cutoff, mask, 0.0)
    theta = omega * jnp.minimum(radius, cutoff)
    c1, s1 = jnp.cos(theta), jnp.sin(theta)
    ir = 1.0 / radius
    env = 0.5 * (c1 + 1.0) * inside
    e = env * ir
    e1 = ((-0.5 * omega) * s1 * inside - e) * ir
    e2 = ((-0.5 * omega * omega) * c1 * inside - 2.0 * e1) * ir
    unit = [d * ir for d in deltas]
    for name, value in (("e", e), ("e1", e1), ("e2", e2), ("ir", ir), ("t", kinds)):
        rows.put(save, name, value)
    for c in range(3):
        rows.put(save, "u%d" % c, unit[c])
    sin_at, cos_at = rows.at["sin"][0], rows.at["cos"][0]
    multiples(c1, s1, save.at[sin_at : sin_at + slots * USED, :], save.at[cos_at : cos_at + slots * USED, :], slots)

    def read_sin(k):
        return save[sin_at + k * USED : sin_at + (k + 1) * USED, :]

    def read_cos(k):
        return save[cos_at + k * USED : cos_at + (k + 1) * USED, :]

    coefs = [e] + [e * u for u in unit]
    mask_at = rows.at["mask"][0]

    def put_mask(i, value):
        save[mask_at + 8 * i : mask_at + 8 * i + 8, :] = value

    type_masks(kinds, types, put_mask)

    def read_mask(i):
        return save[mask_at + 8 * i : mask_at + 8 * i + 8, :]

    slot_sums(read_sin, read_cos, coefs, None, read_mask, slots, types, lambda q, v: rows.put(save, "A%d" % q, v))

    def nw(name):
        return narrow.get(nh, name), narrow.get(nl, name)

    def wd(name, first=None, last=None, rsl=slice(None)):
        return tuple(wide.get(r, name)[rsl, first:last] for r in (wh, wl))

    a0 = split(rows.get(save, "A0"))
    av = split(cat([rows.get(save, "A%d" % q) for q in (1, 2, 3)], 1))
    s_one = features[...] + dot3(wd("BT", rsl=slice(0, feat)), a0)
    v = dot3(wd("BT", rsl=slice(feat, 2 * feat)), av)
    uw = dot3(nw("RQT"), split(v))
    turned, mirrored = thirds(uw[0:feat]), thirds(uw[feat : 2 * feat])
    q = turned[0] * mirrored[0] + turned[1] * mirrored[1] + turned[2] * mirrored[2]
    n = jnp.sqrt(mirrored[0] * mirrored[0] + mirrored[1] * mirrored[1] + mirrored[2] * mirrored[2] + 1.0)
    joined = cat([s_one, n], 0)
    h = dot3(wd("CT"), split(joined))
    gate = lax.logistic(h)
    z = h * gate
    dz = gate * (1.0 + h * (1.0 - gate))
    d2z = gate * (1.0 - gate) * (2.0 + h * (1.0 - 2.0 * gate))
    a = dot3(nw("ST"), split(z))
    a2 = a[feat : 2 * feat]
    s_two = s_one + a[0:feat] + a2 * q
    y = dot3(nw("RT"), split(s_two))
    gate = lax.logistic(y)
    dy = gate * (1.0 + y * (1.0 - gate))
    d2y = gate * (1.0 - gate) * (2.0 + y * (1.0 - 2.0 * gate))
    ldy = dy * live
    yb = colmat[...] * ldy
    s2b = dot3(nw("R"), split(yb))
    ab = cat([s2b, s2b * q], 0)
    qb = s2b * a2
    zb = dot3(wd("S"), split(ab))
    hb = zb * dz
    jb = dot3(nw("C"), split(hb))
    s1b = s2b + jb[0:feat]
    nbn = jb[feat : 2 * feat] / n
    uwb = cat(
        [
            cat([qb * mirrored[c] for c in range(3)], 1),
            cat([nbn * mirrored[c] + qb * turned[c] for c in range(3)], 1),
        ],
        0,
    )
    vb = dot3(wd("RQ"), split(uwb))
    for name, value in (
        ("joined", joined), ("ab", ab), ("z", z), ("dz", dz), ("d2z", d2z), ("a2", a2), ("q", q), ("n", n),
        ("s2", s_two), ("yb", yb), ("yc", colmat[...] * live * d2y), ("ldy", ldy), ("s2b", s2b), ("zb", zb),
        ("hb", hb), ("qb", qb), ("nbn", nbn), ("s1b", s1b),
    ):
        rows.put(save, name, value)
    for name, value in (("v", v), ("uw", uw), ("uwb", uwb), ("vb", vb)):
        for c, part in enumerate(thirds(value)):
            rows.put(save, "%s%d" % (name, c), part)
    ab0 = dot3(wd("B", 0, feat), split(s1b))
    abv = thirds(dot3(wd("B", feat, 2 * feat), split(vb)))

    def put(name, q, k, row):
        start = rows.at["%s%d" % (name, q)][0] + k
        save[start : start + 1, :] = row

    tables = [ab0] + abv
    slot_reads(lambda q: tables[q], kinds, read_sin, read_cos, slots, types, put, True)
    sa = [rows.get(save, "sa%d" % q) for q in range(4)]
    sb = [rows.get(save, "sb%d" % q) for q in range(4)]
    z_sum = unit[0] * sa[1] + unit[1] * sa[2] + unit[2] * sa[3]
    x_sum = sb[0] + unit[0] * sb[1] + unit[1] * sb[2] + unit[2] * sb[3]
    rb = e * x_sum + e1 * (sa[0] + z_sum) - ir * e * z_sum
    deltas_bar = [rb * unit[c] + e * ir * sa[c + 1] for c in range(3)]
    pool_partials(deltas_bar, code, lambda j: index[slots + j : slots + j + 1, :], (low, high), scratch, lanes)


def centres_of(bins, bin_total):
    return 0.1 * jnp.sqrt(3600.0 * (bins.astype(f32) + 0.5) / bin_total)


def hist_body(
    depth, bin_total, pool, left, right, from_left, from_right, index, masks, bins,
    next_own, slopes, hist, moved, scratch,
):
    lanes = pool.shape[2]
    slots = index.shape[0] - 8
    code = index[0:slots, :]
    inverse = index[slots + 4 : slots + 5, :]
    mask = masks[0:slots, :]
    for j in range(4):
        kick = (0.5 * time_step * time_step) * pool[j, 6:7, :]
        force = whole((left, right, from_left, from_right), j)
        moved[j, 0:3, :] = pool[j, 0:3, :] + time_step * pool[j, 3:6, :] - kick * force[0:3, :]
    inverse8 = jnp.broadcast_to(inverse, (8, lanes))
    own = []
    for c in range(3):
        row = from_pool([moved[j, c : c + 1, :] for j in range(4)], inverse8, lanes)[0:1, :]
        next_own[c : c + 1, :] = row
        own.append(row)

    def coords(j, c):
        shift = pool_offsets(j, lanes)[c]
        row = moved[j, c : c + 1, :]
        return row if shift is None else row + shift

    deltas, radius = pool_deltas(coords, lambda c: own[c], code, lanes, depth)
    gap = radius - centres_of(bins[...], bin_total)
    kernel = jnp.exp(-gap * gap / sigma_two) * mask
    scale = kernel * gap * (-2.0 / sigma_two) / radius
    for c in range(3):
        slopes[c * slots : (c + 1) * slots, :] = scale * deltas[c]
    sums = scatter_lanes([kernel], bins[...], scratch, bin_total)
    hist[...] = jnp.broadcast_to(sums[0:1, :], hist.shape)


def adjoint_body(atoms_total, hists, target, slopes, index, bins, low, high, scratch):
    lanes = bins.shape[1]
    slots = bins.shape[0]
    code = index[0:slots, :]
    total = jnp.sum(hists[...], axis=0, keepdims=True)
    weights = 2.0 * (total / atoms_total - target[...]) / atoms_total
    picked = lane_take(weights, bins[...])
    deltas_bar = [picked * slopes[c * slots : (c + 1) * slots, :] for c in range(3)]
    pool_partials(deltas_bar, code, lambda j: index[slots + j : slots + j + 1, :], (low, high), scratch, lanes)


def grads_body(
    types, pool, left, right, from_left, from_right, index, save, colmat, phi, filt, nh, nl, wh, wl,
    keep, send, adjoint, after, tangents, grads,
):
    lanes = pool.shape[2]
    slots = index.shape[0] - 8
    feat = colmat.shape[0]
    rows = saved_rows(feat, types, slots)
    narrow = narrow_rows(feat)
    wide = wide_rows(feat, types)
    code = index[0:slots, :]
    inverse8 = jnp.broadcast_to(index[slots + 4 : slots + 5, :], (8, lanes))

    def get(name):
        return rows.get(save, name)

    for j in range(4):
        adjoint[j, :, :] = whole((left, right, from_left, from_right), j)
    probe = [
        [(0.5 * time_step * time_step) * pool[j, 6:7, :] * adjoint[j, c : c + 1, :] for j in range(4)]
        for c in range(3)
    ]
    moves = [
        from_pool(probe[c], code, lanes) - from_pool(probe[c], inverse8, lanes)[0:1, :] for c in range(3)
    ]
    e, e1, e2, ir, kinds = get("e"), get("e1"), get("e2"), get("ir"), get("t")
    unit = [get("u%d" % c) for c in range(3)]
    dr = unit[0] * moves[0] + unit[1] * moves[1] + unit[2] * moves[2]
    du = [(moves[c] - unit[c] * dr) * ir for c in range(3)]
    de = e1 * dr
    sin_at, cos_at = rows.at["sin"][0], rows.at["cos"][0]

    def read_sin(k):
        return save[sin_at + k * USED : sin_at + (k + 1) * USED, :]

    def read_cos(k):
        return save[cos_at + k * USED : cos_at + (k + 1) * USED, :]

    k_rows = STRIDE * types

    def put_sum(q, value):
        tangents[q * k_rows : (q + 1) * k_rows, :] = value

    sin_coef = [de] + [de * unit[c] + e * du[c] for c in range(3)]
    cos_coef = [e * dr] + [e * dr * unit[c] for c in range(3)]
    mask_at = rows.at["mask"][0]

    def read_mask(i):
        return save[mask_at + 8 * i : mask_at + 8 * i + 8, :]

    slot_sums(read_sin, read_cos, sin_coef, cos_coef, read_mask, slots, types, put_sum)

    def nw(name):
        return narrow.get(nh, name), narrow.get(nl, name)

    def wd(name, first=None, last=None, rsl=slice(None)):
        return tuple(wide.get(r, name)[rsl, first:last] for r in (wh, wl))

    da_zero = tangents[0:k_rows, :]
    da_vec = cat([tangents[q * k_rows : (q + 1) * k_rows, :] for q in (1, 2, 3)], 1)
    ds1 = dot3(wd("BT", rsl=slice(0, feat)), split(da_zero))
    dv = dot3(wd("BT", rsl=slice(feat, 2 * feat)), split(da_vec))
    duw = dot3(nw("RQT"), split(dv))
    d_turn, d_mirr = thirds(duw[0:feat]), thirds(duw[feat : 2 * feat])
    turned = [get("uw%d" % c)[0:feat] for c in range(3)]
    mirrored = [get("uw%d" % c)[feat : 2 * feat] for c in range(3)]
    q, n, a2, dz, d2z = get("q"), get("n"), get("a2"), get("dz"), get("d2z")
    s2b, zb, qb, nbn = get("s2b"), get("zb"), get("qb"), get("nbn")
    dq = sum(d_turn[c] * mirrored[c] + turned[c] * d_mirr[c] for c in range(3))
    dn = sum(mirrored[c] * d_mirr[c] for c in range(3)) / n
    dj = cat([ds1, dn], 0)
    dh = dot3(wd("CT"), split(dj))
    dzt = dz * dh
    da = dot3(nw("ST"), split(dzt))
    da2 = da[feat : 2 * feat]
    ds2 = ds1 + da[0:feat] + da2 * q + a2 * dq
    dyt = dot3(nw("RT"), split(ds2))
    dyb = get("yc") * dyt
    ds2b = dot3(nw("R"), split(dyb))
    dab = cat([ds2b, ds2b * q + s2b * dq], 0)
    dqb = ds2b * a2 + s2b * da2
    dzb = dot3(wd("S"), split(dab))
    dhb = dzb * dz + zb * (d2z * dh)
    djb = dot3(nw("C"), split(dhb))
    ds1b = ds2b + djb[0:feat]
    dnbn = (djb[feat : 2 * feat] - nbn * dn) / n
    duwb = cat(
        [
            cat([dqb * mirrored[c] + qb * d_mirr[c] for c in range(3)], 1),
            cat(
                [
                    dnbn * mirrored[c] + nbn * d_mirr[c] + dqb * turned[c] + qb * d_turn[c]
                    for c in range(3)
                ],
                1,
            ),
        ],
        0,
    )
    dvb = dot3(wd("RQ"), split(duwb))

    def both(first, second, third, fourth):
        return -dot3(split(cat([first, second], 1)), split(cat([third, fourth], 1)), NT)

    parts = grads.shape[0]
    share = feat // parts
    rq = both(dv, triple(rows, save, "v"), triple(rows, save, "uwb"), duwb)
    cg = both(dj, get("joined"), get("hb"), dhb)
    sg = both(dzt, get("z"), get("ab"), dab)
    rg = both(ds2, get("s2"), get("yb"), dyb)
    bs = both(da_zero, get("A0"), get("s1b"), ds1b)
    bv = both(da_vec, cat([get("A%d" % i) for i in (1, 2, 3)], 1), triple(rows, save, "vb"), dvb)
    low, high = split(get("ldy") * dyt)
    ones = jnp.ones((16, lanes), bf16)
    col = -(dot1(ones, low, NT) + dot1(ones, high, NT))
    fg, pg = [], []
    for half, value in enumerate((bs, bv)):
        cols = slice(half * feat, (half + 1) * feat)
        total = None
        for t in range(types):
            block = value[STRIDE * t : STRIDE * t + USED, :]
            term = block * phi[t : t + 1, cols]
            total = term if total is None else total + term
            pg.append((half, t, jnp.sum(block * filt[0:USED, cols], axis=0, keepdims=True)))
        fg.append(total)
    base = 7 * share
    place = iota((10, lanes), 1)
    for part in range(parts):
        mine = slice(part * share, (part + 1) * share)
        grads[part, 0:share, :] = rq[mine, 0:feat]
        grads[part, share : 2 * share, :] = rq[mine, feat : 2 * feat]
        grads[part, 2 * share : 4 * share, :] = cg[2 * part * share : 2 * (part + 1) * share, :]
        grads[part, 4 * share : 5 * share, :] = sg[mine, 0:feat]
        grads[part, 5 * share : 6 * share, :] = sg[mine, feat : 2 * feat]
        grads[part, 6 * share : 7 * share, :] = rg[mine, :]
        for half, t, row in pg:
            at = base + half * types + t
            grads[part, at : at + 1, :] = row
        chosen = fg[part // 2]
        rolled = pltpu.roll(chosen, feat // 2, 1)
        here, there = (chosen, rolled) if part % 2 == 0 else (rolled, chosen)
        at = base + 2 * types
        grads[part, at : at + 10, :] = jnp.where(place < feat // 2, here[0:10, :], there[10:20, :])
        grads[part, at + 10 : at + 11, :] = col[0:1, :]
        grads[part, at + 11 :, :] = jnp.zeros((grads.shape[1] - at - 11, lanes), f32)

    odd = lax.axis_index("slab") % 2
    half = grads.shape[1] // 2
    keep[...] = grads[:, pl.ds(pl.multiple_of(odd * half, half), half), :]
    send[...] = grads[:, pl.ds(pl.multiple_of((1 - odd) * half, half), half), :]
    for c in range(3):
        after[c * slots : (c + 1) * slots, :] = du[c]
        after[4 * slots + (c + 1) * feat : 4 * slots + (c + 2) * feat, :] = dvb[:, c * lanes : (c + 1) * lanes]
    after[3 * slots : 4 * slots, :] = dr
    after[4 * slots : 4 * slots + feat, :] = ds1b


def moves_body(types, index, save, after, wh, wl, low, high, sums, scratch):
    lanes = index.shape[1]
    slots = index.shape[0] - 8
    feat = lanes
    rows = saved_rows(feat, types, slots)
    wide = wide_rows(feat, types)
    code = index[0:slots, :]

    def get(name):
        return rows.get(save, name)

    def wd(name, first, last):
        return tuple(wide.get(r, name)[:, first:last] for r in (wh, wl))

    e, e1, e2, ir, kinds = get("e"), get("e1"), get("e2"), get("ir"), get("t")
    unit = [get("u%d" % c) for c in range(3)]
    du = [after[c * slots : (c + 1) * slots, :] for c in range(3)]
    dr = after[3 * slots : 4 * slots, :]
    de, de1, dir_ = e1 * dr, e2 * dr, -ir * ir * dr
    sin_at, cos_at = rows.at["sin"][0], rows.at["cos"][0]

    def read_sin(k):
        return save[sin_at + k * USED : sin_at + (k + 1) * USED, :]

    def read_cos(k):
        return save[cos_at + k * USED : cos_at + (k + 1) * USED, :]

    ds1b = after[4 * slots : 4 * slots + feat, :]
    dvb = cat([after[4 * slots + (c + 1) * feat : 4 * slots + (c + 2) * feat, :] for c in range(3)], 1)
    dab0 = dot3(wd("B", 0, feat), split(ds1b))
    dabv = thirds(dot3(wd("B", feat, 2 * feat), split(dvb)))
    tables = [dab0] + dabv

    def put(name, q, k, row):
        start = (0 if name == "sa" else 4 * slots) + q * slots + k
        sums[start : start + 1, :] = row

    slot_reads(lambda q: tables[q], kinds, read_sin, read_cos, slots, types, put, False)
    sa = [get("sa%d" % q) for q in range(4)]
    sb = [get("sb%d" % q) for q in range(4)]
    sd = [get("sd%d" % q) for q in range(4)]
    dsa = [sb[q] * dr + sums[q * slots : (q + 1) * slots, :] for q in range(4)]
    dsb = [
        sums[(4 + q) * slots : (5 + q) * slots, :] - sd[q] * dr for q in range(4)
    ]
    z_sum = sum(unit[c] * sa[c + 1] for c in range(3))
    x_sum = sb[0] + sum(unit[c] * sb[c + 1] for c in range(3))
    dz_sum = sum(du[c] * sa[c + 1] + unit[c] * dsa[c + 1] for c in range(3))
    dx_sum = dsb[0] + sum(du[c] * sb[c + 1] + unit[c] * dsb[c + 1] for c in range(3))
    rb = e * x_sum + e1 * (sa[0] + z_sum) - ir * e * z_sum
    drb = (
        de * x_sum + e * dx_sum + de1 * (sa[0] + z_sum) + e1 * (dsa[0] + dz_sum)
        - (dir_ * e + ir * de) * z_sum - ir * e * dz_sum
    )
    deltas_bar = [
        drb * unit[c] + rb * du[c] + (de * ir + e * dir_) * sa[c + 1] + e * ir * dsa[c + 1]
        for c in range(3)
    ]
    pool_partials(deltas_bar, code, lambda j: index[slots + j : slots + j + 1, :], (low, high), scratch, lanes)


def last_body(
    types, parts, atoms_total, mine, other, adjoint, left, right, index, slope, hidden_t, table_t, spreader, next_own,
    next_out, adj, enc, spr, fil, rot, ref, com, spl, rea, col, total,
):
    next_out[...] = next_own[...]
    odd = lax.axis_index("slab") % 2
    half = mine.shape[0]
    total[pl.ds(pl.multiple_of(odd * half, half), half), :] = mine[...]
    total[pl.ds(pl.multiple_of((1 - odd) * half, half), half), :] = other[...]
    lanes = adjoint.shape[2]
    slots = index.shape[0] - 8
    feat = lanes
    share = feat // parts
    inverse8 = jnp.broadcast_to(index[slots + 4 : slots + 5, :], (8, lanes))
    for c in range(3):
        rows = [
            atoms_total * (adjoint[j, c : c + 1, :] - (left, right)[j % 2][j // 2, c : c + 1, :]) for j in range(4)
        ]
        adj[c : c + 1, :] = from_pool(rows, inverse8, lanes)[0:1, :]
    rot[...] = total[0:share, :]
    ref[...] = total[share : 2 * share, :]
    com[...] = total[2 * share : 4 * share, :]
    spl[:, 0:feat] = total[4 * share : 5 * share, :]
    spl[:, feat : 2 * feat] = total[5 * share : 6 * share, :]
    rea[...] = total[6 * share : 7 * share, :]
    base = 7 * share
    phib = cat([total[base : base + types, :], total[base + types : base + 2 * types, :]], 1)
    at = base + 2 * types
    block = total[at : at + 10, :]
    fil[0:10, :] = block[:, 0 : feat // 2]
    fil[10:20, :] = pltpu.roll(block, feat // 2, 1)[:, 0 : feat // 2]
    col_row = total[at + 10 : at + 11, :]
    spare = jnp.zeros((types, 2 * feat), f32)
    pre_bar = dot3(split(cat([phib, spare], 0)), split(spreader[...]), NT)[0:types] * slope[...]
    here = pl.ds(pl.multiple_of(lax.axis_index("cross") * share, share), share)
    rest = jnp.zeros((lanes - types, feat), f32)
    spr[...] = dot3(split(hidden_t[here, :]), split(cat([phib, cat([rest, rest], 1)], 0)))
    enc[...] = dot3(split(table_t[here, :]), split(cat([pre_bar, rest], 0)))
    for part in range(parts):
        @pl.when(lax.axis_index("cross") == part)
        def _():
            col[...] = col_row[:, part * share : (part + 1) * share]


def shift(x, axis, step):
    count = lax.axis_size(axis)
    return lax.ppermute(x, axis, [(i, (i + step) % count) for i in range(count)])


def both_ways(first, second, axis):
    return shift(first, axis, 1), shift(second, axis, -1)


def corner_sum(low, high):
    left, right = call(turn_body, [(low.shape, f32)] * 2, low, high, *both_ways(high, low, "slab"))
    return (left, right) + both_ways(right, left, "cross")


def swap(x, axis, bit):
    return lax.ppermute(x, axis, [(i, i ^ bit) for i in range(lax.axis_size(axis))])


def halve(bit, x, other, keep, send):
    mine = (lax.axis_index("cross") // bit) % 2
    shape = (x.shape[0] // 2, 2) + x.shape[1:]
    x, other = x.reshape(shape), other.reshape(shape)
    for ref, side in ((keep, mine), (send, 1 - mine)):
        value = x[:, pl.ds(side, 1)] + other[:, pl.ds(side, 1)]
        ref[...] = value.reshape(ref.shape)


def halve_hold_body(bit, x, other, low, high, keep, send, low_out, high_out):
    halve(bit, x, other, keep, send)
    low_out[...] = low[...]
    high_out[...] = high[...]


def halve_turn_body(bit, x, other, low, high, from_down, from_up, keep, send, left, right):
    halve(bit, x, other, keep, send)
    turn_body(low, high, from_down, from_up, left, right)


def add_body(x, other, out):
    out[...] = x[...] + other[...]


def add_two_body(x, other, side, from_side, out, total):
    add_body(x, other, out)
    add_body(side, from_side, total)


def reduce_all(keep, send, low, high):
    slab_count, cross_count = lax.axis_size("slab"), lax.axis_size("cross")
    group = (low.shape, f32)
    other = swap(send, "slab", 1)
    bit, step, pieces = 1, 0, None
    while bit < cross_count:
        half = ((keep.shape[0] // 2,) + keep.shape[1:], f32)
        if step == 0:
            keep, send, low, high = call(
                functools.partial(halve_hold_body, bit), [half, half, group, group], keep, other, low, high
            )
            from_down, from_up = both_ways(high, low, "slab")
        elif step == 1:
            keep, send, left, right = call(
                functools.partial(halve_turn_body, bit), [half, half, group, group],
                keep, other, low, high, from_down, from_up,
            )
            pieces = (left, right) + both_ways(right, left, "cross")
        else:
            raise NotImplementedError
        other = swap(send, "cross", bit)
        bit, step = 2 * bit, step + 1
    x, other = keep[0], other[0]
    left, right, from_left, from_right = pieces
    waiting, sides = [(left, from_left), (right, from_right)], []

    def add(x, other):
        shapes = [(x.shape, f32)]
        if waiting:
            x, side = call(add_two_body, shapes + [group], x, other, *waiting.pop(0))
            sides.append(side)
            return x
        return call(add_body, shapes, x, other)[0]

    bit = 2
    while bit < slab_count:
        x = add(x, other)
        other = swap(x, "slab", bit)
        bit *= 2
    x = add(x, other)
    while waiting:
        sides += call(add_body, [group], *waiting.pop(0))
    return x, swap(x, "slab", 1), sides


def device_step(
    positions, velocities, inverse_mass, species, type_table, neighbours, slot_count, atom_count,
    pair_bins, send_list, target, encoder, spreader, filters, rotator, reflector, combiner, splitter,
    readout, collector,
):
    lanes = positions.shape[1]
    slots = neighbours.shape[1]
    types, feat = type_table.shape
    bin_total = target.shape[0]
    slab_count, cross_count = lax.axis_size("slab"), lax.axis_size("cross")
    devices = slab_count * cross_count
    atoms_total = float(lanes * devices)
    depth = 1.6 * (lanes // 16)
    parts = cross_count
    row = lambda x: x.reshape(1, x.shape[0])
    i32 = jnp.int32
    vm, dma = pltpu.VMEM, pltpu.SemaphoreType.DMA
    narrow, wide = narrow_rows(feat).total, wide_rows(feat, types).total
    group = ((2, 8, lanes), f32)
    pool_shape = ((4, 8, lanes), f32)
    pair_scratch = vm((16 * slots, lanes), f32)
    low, high, own_rows, send = call(
        offer_body, [group, group, ((8, lanes), f32), ((8, lanes), i32)],
        *in_hbm(positions, velocities, row(inverse_mass), row(species), send_list),
        specs=[HB] * 5,
        scratch=[
            vm((3, lanes), f32), vm((3, lanes), f32), vm((1, lanes), f32), vm((1, lanes), i32),
            vm(send_list.shape, i32), dma((5,)),
        ],
    )
    colmat, nh, nl, wh, wl, phi, slope, hidden_t, table_t, filt, spreader_in = call(
        weights_body,
        [
            ((feat, lanes), f32), ((narrow, feat), bf16), ((narrow, feat), bf16), ((wide, 2 * feat), bf16),
            ((wide, 2 * feat), bf16), ((types, 2 * feat), f32), ((types, feat), f32), ((feat, lanes), f32),
            ((feat, lanes), f32), ((STRIDE, 2 * feat), f32), (spreader.shape, f32),
        ],
        *in_hbm(
            type_table, encoder, spreader, filters, rotator, reflector, combiner, splitter, readout,
            row(collector),
        ),
        specs=[HB] * 10,
        scratch=[
            vm(type_table.shape, f32), vm(encoder.shape, f32), vm(filters.shape, f32), vm(rotator.shape, f32),
            vm(reflector.shape, f32), vm(combiner.shape, f32), vm(splitter.shape, f32), vm(readout.shape, f32),
            vm((1, feat), f32), dma((10,)),
        ],
    )
    index, masks, features, bins, goal = call(
        index_body,
        [
            ((slots + 8, lanes), i32), ((slots + 8, lanes), f32), ((feat, lanes), f32), ((slots, lanes), i32),
            ((1, bin_total), f32),
        ],
        *in_hbm(neighbours.T, row(slot_count), pair_bins.T, row(target)),
        atom_count, send, own_rows, table_t,
        specs=[HB] * 4 + [SM] + [VM] * 3,
        scratch=[vm((slots, lanes), i32), vm((1, lanes), i32), dma((4,))],
    )
    pieces = corner_sum(low, high)
    save_rows = saved_rows(feat, types, slots).total
    low, high, pool, save = call(
        functools.partial(force_body, types, depth),
        [group, group, pool_shape, ((save_rows, lanes), f32)],
        *pieces, own_rows, index, masks, features, colmat, nh, nl, wh, wl,
        scratch=[pair_scratch],
    )
    pieces = corner_sum(low, high)
    next_positions, slopes, hist = call(
        functools.partial(hist_body, depth, bin_total),
        [((3, lanes), f32), ((3 * slots, lanes), f32), ((devices, bin_total), f32)],
        pool, *pieces, index, masks, bins,
        scratch=[vm((4, 8, lanes), f32), pair_scratch],
    )
    hists = lax.all_to_all(hist.reshape(devices, 1, bin_total), ("slab", "cross"), 0, 0)
    low, high = call(
        functools.partial(adjoint_body, atoms_total), [group, group],
        hists.reshape(devices, bin_total), goal, slopes, index, bins,
        scratch=[pair_scratch],
    )
    pieces = corner_sum(low, high)
    half_grads = ((parts, feat, lanes), f32)
    keep, send, adjoint, after = call(
        functools.partial(grads_body, types),
        [half_grads, half_grads, pool_shape, ((4 * slots + 4 * feat, lanes), f32)],
        pool, *pieces, index, save, colmat, phi, filt, nh, nl, wh, wl,
        scratch=[vm((4 * STRIDE * types, lanes), f32), vm((parts, 2 * feat, lanes), f32)],
    )
    low, high = call(
        functools.partial(moves_body, types), [group, group], index, save, after, wh, wl,
        scratch=[vm((8 * slots, lanes), f32), pair_scratch],
    )
    mine, other, sides = reduce_all(keep, send, low, high)
    share = feat // parts
    results = call(
        functools.partial(last_body, types, parts, atoms_total),
        [
            ((3, lanes), f32), ((3, lanes), f32), ((share, feat), f32), ((share, 2 * feat), f32),
            ((filters.shape[0], 2 * feat // parts), f32), ((share, feat), f32), ((share, feat), f32),
            ((2 * share, feat), f32), ((share, 2 * feat), f32), ((share, feat), f32), ((1, share), f32),
        ],
        mine, other, adjoint, *sides, index, slope, hidden_t, table_t, spreader_in, next_positions,
        scratch=[vm((2 * feat, lanes), f32)],
        keep=False,
    )
    return tuple(results[:10]) + (results[10].reshape(share),)


def solution(mesh):
    both = ("slab", "cross")
    in_specs = (
        P(None, both), P(None, both), P(both), P(both), P(), P(both, None), P(both), P(both), P(both, None),
        P("slab", "cross", None),
    ) + (P(),) * 10
    out_specs = (
        P(None, both), P(None, both), P("cross", None), P("cross", None), P(None, "cross"), P("cross", None),
        P("cross", None), P("cross", None), P("cross", None), P("cross", None), P("cross"),
    )
    return jax.shard_map(device_step, mesh=mesh, in_specs=in_specs, out_specs=out_specs, check_vma=False)
```

```python
import functools

import jax
import jax.numpy as jnp
from jax import lax
from jax.experimental import pallas as pl
from jax.experimental.pallas import tpu as pltpu
from jax.sharding import PartitionSpec as P


cutoff = 5.0
soften = 0.25
sigma_two = 0.18
slab_length = 10.0
cell_length = 10.0
time_step = 0.5
highest = lax.Precision.HIGHEST
f32 = jnp.float32
bf16 = jnp.bfloat16
pi = 3.141592653589793
omega = pi / cutoff

NN = ((1,), (0,))
NT = ((1,), (1,))
VM = pl.BlockSpec(memory_space=pltpu.VMEM)
SM = pl.BlockSpec(memory_space=pltpu.SMEM)
HB = pl.BlockSpec(memory_space=pltpu.HBM)


def call(body, outs, *args, specs=None, scratch=(), keep=True):
    return pl.pallas_call(
        body,
        out_shape=[(pltpu.VMEM if keep else jax.ShapeDtypeStruct)(s, d) for s, d in outs],
        in_specs=[VM] * len(args) if specs is None else specs,
        out_specs=[VM] * len(outs),
        scratch_shapes=list(scratch),
        compiler_params=pltpu.CompilerParams(vmem_limit_bytes=16 * 2**20),
    )(*args)


def in_hbm(*arrays):
    return [pltpu.with_memory_space_constraint(x, pltpu.HBM) for x in arrays]


def fetch(sources, targets, semaphores):
    copies = [
        pltpu.make_async_copy(source, target, semaphores.at[i])
        for i, (source, target) in enumerate(zip(sources, targets))
    ]
    for copy in copies:
        copy.start()
    for copy in copies:
        copy.wait()


def split(x):
    high = x.astype(bf16)
    return high, (x - high.astype(f32)).astype(bf16)


def dot1(a, b, dims):
    return lax.dot_general(a, b, (dims, ((), ())), preferred_element_type=f32)


def dot3(a, b, dims=NN):
    return dot1(
        jnp.concatenate([a[0], a[0], a[1]], dims[0][0]), jnp.concatenate([b[0], b[1], b[0]], dims[1][0]), dims
    )


def cat(parts, axis):
    return jnp.concatenate(parts, axis=axis)


def iota(shape, dim):
    return lax.broadcasted_iota(jnp.int32, shape, dim)


def lane_take(row, index):
    return jnp.take_along_axis(jnp.broadcast_to(row, index.shape), index, axis=1)


def own_lanes(group, lanes):
    quarter = lanes // 4
    start = 2 * quarter * (1 - group // 2) + quarter * (1 - group % 2)
    return start, quarter


def pool_offsets(group, lanes):
    place = iota((1, lanes), 1)
    up, right = group // 2, group % 2
    half, quarter = lanes // 2, lanes // 4
    first = (place >= half) if up else (place < half)
    second_bit = place % half >= quarter
    second = second_bit if right else jnp.logical_not(second_bit)
    sign_u, sign_r = 2.0 * up - 1.0, 2.0 * right - 1.0
    return (
        jnp.where(first, sign_u * slab_length, 0.0).astype(f32),
        jnp.where(second, sign_r * cell_length, 0.0).astype(f32),
        None,
    )


def from_pool(rows, code, lanes):
    group = code // lanes
    lane = code % lanes
    out = lane_take(rows[0], lane)
    for j in range(1, 4):
        out = jnp.where(group == j, lane_take(rows[j], lane), out)
    return out


def pool_deltas(pool_rows, own_rows, code, lanes, depth):
    deltas = []
    for c in range(3):
        d = from_pool([pool_rows(j, c) for j in range(4)], code, lanes) - own_rows(c)
        if c == 2:
            d = d - depth * jnp.floor(d / depth + 0.5)
        deltas.append(d)
    radius = jnp.sqrt(deltas[0] * deltas[0] + deltas[1] * deltas[1] + deltas[2] * deltas[2] + soften)
    return deltas, radius


def one_hot_rows(index, slots, count):
    lanes = index.shape[1]
    place = iota((count, lanes), 0)
    return cat(
        [(place == index[k : k + 1, :]).astype(f32).astype(bf16) for k in range(slots)], 1
    )


def scatter_lanes(values, index, scratch, count):
    shape = index.shape
    slots = shape[0]
    for row in range(16):
        value = values[row] if row < len(values) else None
        if value is None:
            value = jnp.zeros(shape, f32)
        scratch[pl.ds(row, slots, stride=16), :] = value
    highs, mids, lows = [], [], []
    for k in range(slots):
        x = scratch[16 * k : 16 * k + 16, :]
        high = x.astype(bf16)
        rest = x - high.astype(f32)
        mid = rest.astype(bf16)
        highs.append(high)
        mids.append(mid)
        lows.append((rest - mid.astype(f32)).astype(bf16))
    left = cat([cat(highs, 1), cat(mids, 1), cat(lows, 1)], 0)
    sums = dot1(left, one_hot_rows(index, slots, count), NT)
    return sums[0:16] + (sums[16:32] + sums[32:48])


def pool_partials(deltas_bar, code, send_index, outs, groups, scratch, lanes):
    group = code // lanes
    values = []
    for j in range(4):
        for c in range(3):
            values.append(jnp.where(group == j, deltas_bar[c], 0.0))
        values.append(None)
    sums = scatter_lanes(values, code % lanes, scratch, lanes)
    centres = [-jnp.sum(d, axis=0, keepdims=True) for d in deltas_bar]
    place = iota((1, lanes), 1)
    for j in range(4):
        start, width = own_lanes(j, lanes)
        own = jnp.logical_and(place >= start, place < start + width)
        groups[j, :, :] = jnp.zeros((8, lanes), f32)
        for c in range(3):
            mine = lane_take(jnp.broadcast_to(centres[c], (8, lanes)), jnp.broadcast_to(send_index(j), (8, lanes)))
            groups[j, c : c + 1, :] = sums[4 * j + c : 4 * j + c + 1, :] + jnp.where(
                own, mine[0:1, :], 0.0
            )
    by_side(groups[...], *outs)


def offer_body(
    pos, vel, mass, species, send_list, near, far, own_out, send_out,
    pos_v, vel_v, mass_v, species_v, list_v, groups, semaphores,
):
    fetch((pos, vel, mass, species, send_list), (pos_v, vel_v, mass_v, species_v, list_v), semaphores)
    lanes = pos.shape[1]
    own_out[0:3, :] = pos_v[...]
    own_out[3:6, :] = vel_v[...]
    own_out[6:7, :] = mass_v[...]
    own_out[7:8, :] = species_v[...].astype(f32)
    own_rows = own_out[...]
    place = iota((8, lanes), 1)
    send_out[...] = jnp.zeros((8, lanes), jnp.int32)
    for j in range(4):
        start, width = own_lanes(j, lanes)
        pieces = [list_v[j // 2, j % 2 : j % 2 + 1, :]]
        if start:
            pieces = [jnp.zeros((1, start), jnp.int32)] + pieces
        if start + width < lanes:
            pieces = pieces + [jnp.zeros((1, lanes - start - width), jnp.int32)]
        row = cat(pieces, 1)
        send_out[j : j + 1, :] = row
        own = jnp.logical_and(place >= start, place < start + width)
        taken = jnp.take_along_axis(own_rows, jnp.broadcast_to(row, (8, lanes)), axis=1)
        groups[j, :, :] = jnp.where(own, taken, 0.0)
    by_side(groups[...], near, far)


def parity(axis):
    return lax.axis_index(axis) % 2 == 1


def by_side(groups, near, far):
    odd = parity("slab")
    low, high = groups[0:2], groups[2:4]
    near[...] = jnp.where(odd, low, high)
    far[...] = jnp.where(odd, high, low)


def turn_body(near, far, from_near, from_far, near_out, far_out):
    odd = parity("slab")
    near_sum, far_sum = near[...] + from_near[...], far[...] + from_far[...]
    low, high = jnp.where(odd, near_sum, far_sum), jnp.where(odd, far_sum, near_sum)
    odd = parity("cross")
    for u, part in enumerate((low, high)):
        near_out[u, :, :] = jnp.where(odd, part[0], part[1])
        far_out[u, :, :] = jnp.where(odd, part[1], part[0])


def whole(pieces, j):
    u = j // 2
    near_sum, far_sum = pieces[0][u] + pieces[2][u], pieces[1][u] + pieces[3][u]
    odd = parity("cross")
    return jnp.where(odd, far_sum, near_sum) if j % 2 else jnp.where(odd, near_sum, far_sum)


class Rows:
    def __init__(self, sizes):
        self.at = {}
        self.total = 0
        for name, size in sizes:
            self.at[name] = (self.total, size)
            self.total += size

    def get(self, ref, name):
        start, size = self.at[name]
        return ref[start : start + size, :]

    def put(self, ref, name, value):
        start, size = self.at[name]
        ref[start : start + size, :] = value


STRIDE = 32
USED = 24


def narrow_rows(feat):
    return Rows((("RQT", 2 * feat), ("C", 2 * feat), ("ST", 2 * feat), ("RT", feat), ("R", feat)))


def wide_rows(feat, types):
    return Rows((("BT", 2 * feat), ("B", STRIDE * types), ("RQ", feat), ("CT", feat), ("S", feat)))


def weights_body(
    table_h, encoder_h, spreader_h, filters_h, rotator_h, reflector_h, combiner_h, splitter_h, readout_h,
    collector_h, col_out, nh, nl, wh, wl, phi_out, slope_out, hidden_t, table_t, filt_out, spreader,
    table, encoder, filters, rotator, reflector, combiner, splitter, readout, collector, semaphores,
):
    fetch(
        (table_h, encoder_h, spreader_h, filters_h, rotator_h, reflector_h, combiner_h, splitter_h, readout_h,
         collector_h),
        (table, encoder, spreader, filters, rotator, reflector, combiner, splitter, readout, collector),
        semaphores,
    )
    types, feat = table.shape
    lanes = hidden_t.shape[1]
    basis = filters.shape[0]
    pre = jnp.dot(table[...], encoder[...], precision=highest, preferred_element_type=f32)
    gate = lax.logistic(pre)
    hidden = pre * gate
    phi = jnp.dot(hidden, spreader[...], precision=highest, preferred_element_type=f32)
    phi_out[...] = phi
    slope_out[...] = gate * (1.0 + pre * (1.0 - gate))
    rest = [jnp.zeros((lanes - types, feat), f32)]
    hidden_t[...] = jnp.transpose(cat([hidden] + rest, 0))
    table_t[...] = jnp.transpose(cat([table[...]] + rest, 0))
    filt_out[...] = jnp.zeros(filt_out.shape, f32)
    filt_out[0:basis, :] = filters[...]
    filt = filt_out[...]
    col_out[...] = jnp.transpose(jnp.broadcast_to(collector[...], (lanes, feat)))
    narrow = narrow_rows(feat)
    wide = wide_rows(feat, types)

    def put(rows, high_ref, low_ref, name, value, row=0, col=0):
        high, low = split(value)
        start = rows.at[name][0] + row
        high_ref[start : start + value.shape[0], col : col + value.shape[1]] = high
        low_ref[start : start + value.shape[0], col : col + value.shape[1]] = low

    per_half = feat // STRIDE
    for half in range(2):
        cols = slice(half * feat, (half + 1) * feat)
        for chunk in range(types // per_half):
            block = cat(
                [
                    filt[:, cols] * phi[t : t + 1, cols]
                    for t in range(chunk * per_half, (chunk + 1) * per_half)
                ],
                0,
            )
            put(wide, wh, wl, "B", block, chunk * feat, half * feat)
            put(wide, wh, wl, "BT", jnp.transpose(block), half * feat, chunk * feat)
    put(wide, wh, wl, "RQ", rotator[...], 0, 0)
    put(wide, wh, wl, "RQ", reflector[...], 0, feat)
    put(narrow, nh, nl, "RQT", jnp.transpose(rotator[...]), 0)
    put(narrow, nh, nl, "RQT", jnp.transpose(reflector[...]), feat)
    put(narrow, nh, nl, "C", combiner[...])
    put(wide, wh, wl, "CT", jnp.transpose(combiner[0:feat, :]), 0, 0)
    put(wide, wh, wl, "CT", jnp.transpose(combiner[feat : 2 * feat, :]), 0, feat)
    put(wide, wh, wl, "S", splitter[...])
    put(narrow, nh, nl, "ST", jnp.transpose(splitter[:, 0:feat]), 0)
    put(narrow, nh, nl, "ST", jnp.transpose(splitter[:, feat : 2 * feat]), feat)
    put(narrow, nh, nl, "R", readout[...])
    put(narrow, nh, nl, "RT", jnp.transpose(readout[...]))


def index_body(
    near_h, count_h, bins_h, target_h, atom_count, send, own_rows, table_t,
    index, masks, feat_out, bins, target, near, slot_count, semaphores,
):
    fetch((near_h, count_h, bins_h, target_h), (near, slot_count, bins, target), semaphores)
    species = own_rows[7:8, :].astype(jnp.int32)
    slots, lanes = near.shape
    quarter = lanes // 4
    lane_row = iota((16, lanes), 1).astype(f32)
    row_id = iota((16, lanes), 0)
    lefts, rights = [], []
    place = iota((lanes, lanes), 1)
    for j in range(4):
        start, width = own_lanes(j, lanes)
        own = jnp.logical_and(place >= start, place < start + width)
        same = jnp.logical_and(own, iota((lanes, lanes), 0) == send[j : j + 1, :])
        rights.append(same.astype(f32).astype(bf16))
        lefts.append(
            jnp.where(row_id == 0, lane_row, jnp.where(row_id == 1, float(j), 0.0)).astype(bf16)
        )
    found = dot1(cat(lefts, 1), cat(rights, 1), NT)
    inverse = (found[0:1, :] + lanes * found[1:2, :] + 0.5).astype(jnp.int32)
    near_v = near[...]
    ghost = near_v - lanes
    block = ghost // quarter
    p, q, g = block // 4, block % 4, ghost % quarter
    ghost_code = (2 * (p // 2) + q // 2) * lanes + 2 * quarter * (p % 2) + quarter * (q % 2) + g
    own_code = lane_take(inverse, jnp.minimum(near_v, lanes - 1))
    index[...] = jnp.zeros(index.shape, jnp.int32)
    index[0:slots, :] = jnp.where(near_v < lanes, own_code, ghost_code)
    index[slots : slots + 4, :] = send[0:4, :]
    index[slots + 4 : slots + 5, :] = inverse
    masks[...] = jnp.zeros(masks.shape, f32)
    masks[0:slots, :] = (iota((slots, lanes), 0) < slot_count[...]).astype(f32)
    masks[slots : slots + 1, :] = (iota((1, lanes), 1) < atom_count[0]).astype(f32)
    feat_out[...] = jnp.take_along_axis(table_t[...], jnp.broadcast_to(species, table_t.shape), axis=1)


def saved_rows(feat, types, slots):
    k = STRIDE * types
    pair = ("e", "e1", "e2", "ir", "u0", "u1", "u2", "t")
    sizes = [("A%d" % q, k) for q in range(4)]
    sizes += [("%s%d" % (n, c), feat) for n in ("v", "vb") for c in range(3)]
    sizes += [("%s%d" % (n, c), 2 * feat) for n in ("uw", "uwb") for c in range(3)]
    sizes += [("joined", 2 * feat), ("ab", 2 * feat)]
    sizes += [
        (n, feat)
        for n in ("z", "dz", "d2z", "a2", "q", "n", "s2", "yb", "yc", "ldy", "s2b", "zb", "hb", "qb", "nbn", "s1b")
    ]
    sizes += [("sin", slots * USED), ("cos", slots * USED), ("mask", 8 * slots * types)]
    sizes += [(n, slots) for n in pair]
    sizes += [("%s%d" % (n, q), slots) for n in ("sa", "sb", "sd") for q in range(4)]
    return Rows(sizes)


def multiples(c1, s1, sin_ref, cos_ref, slots):
    lanes = c1.shape[1]
    powers = [(c1, s1)]
    for _ in range(4):
        c, s = powers[-1]
        powers.append((c * c - s * s, 2.0 * c * s))
    sub = iota((8, lanes), 0)
    bits = [(sub // 2**b) % 2 == 1 for b in range(3)]
    order = sub.astype(f32) + 1.0

    def times(x, y):
        return x[0] * y[0] - x[1] * y[1], x[0] * y[1] + x[1] * y[0]

    for k in range(slots):
        rows = [
            tuple(jnp.broadcast_to(part[k : k + 1, :], (8, lanes)) for part in power)
            for power in powers
        ]
        z = rows[0]
        for b in range(3):
            step = (jnp.where(bits[b], rows[b][0], 1.0), jnp.where(bits[b], rows[b][1], 0.0))
            z = times(z, step)
        for v in range(3):
            if v == 1:
                zv = times(z, rows[3])
            elif v == 2:
                zv = times(z, rows[4])
            else:
                zv = z
            start = k * USED + 8 * v
            sin_ref[start : start + 8, :] = zv[1]
            cos_ref[start : start + 8, :] = zv[0] * ((order + 8.0 * v) * omega)


def type_masks(kinds, types, put):
    slots, lanes = kinds.shape
    for k in range(slots):
        kind = jnp.broadcast_to(kinds[k : k + 1, :], (8, lanes))
        for t in range(types):
            put(k * types + t, jnp.where(kind == t, 1.0, 0.0))


def choose(options, bits):
    for bit in bits:
        options = [
            jnp.where(bit, options[i + 1], options[i]) if i + 1 < len(options) else options[i]
            for i in range(0, len(options), 2)
        ]
    return options[0]


def slot_sums(read_sin, read_cos, sin_coef, cos_coef, read_mask, slots, types, put):
    lanes = sin_coef[0].shape[1]
    tiles = USED // 8
    for q in range(4):
        sums = [[None] * tiles for _ in range(types)]
        for k in range(slots):
            value = read_sin(k) * sin_coef[q][k : k + 1, :]
            if cos_coef is not None:
                value = value + read_cos(k) * cos_coef[q][k : k + 1, :]
            for t in range(types):
                mask = read_mask(k * types + t)
                for v in range(tiles):
                    part = value[8 * v : 8 * v + 8] * mask
                    sums[t][v] = part if sums[t][v] is None else sums[t][v] + part
        rest = jnp.zeros((STRIDE - USED, lanes), f32)
        put(q, cat([x for t in range(types) for x in sums[t] + [rest]], 0))


def slot_reads(values, kinds, read_sin, read_cos, slots, types, put, with_square):
    lanes = kinds.shape[1]
    tiles = USED // 8
    whole_kinds = (kinds + 0.5).astype(jnp.int32)
    kind_bits = [((whole_kinds // 2**b) % 2).astype(f32) for b in range((types - 1).bit_length())]
    square = [((iota((8, lanes), 0).astype(f32) + (8.0 * v + 1.0)) * omega) ** 2 for v in range(tiles)]
    for q in range(4):
        value = values(q)
        tables = [
            [value[STRIDE * t + 8 * v : STRIDE * t + 8 * v + 8] for v in range(tiles)] for t in range(types)
        ]
        for k in range(slots):
            bits = [jnp.broadcast_to(part[k : k + 1, :], (8, lanes)) > 0.5 for part in kind_bits]
            picked = [choose([table[v] for table in tables], bits) for v in range(tiles)]
            sines, cosines = read_sin(k), read_cos(k)
            with_sin = [sines[8 * v : 8 * v + 8] * picked[v] for v in range(tiles)]
            put("sa", q, k, jnp.sum(sum(with_sin), axis=0, keepdims=True))
            with_cos = [cosines[8 * v : 8 * v + 8] * picked[v] for v in range(tiles)]
            put("sb", q, k, jnp.sum(sum(with_cos), axis=0, keepdims=True))
            if with_square:
                with_sin = [with_sin[v] * square[v] for v in range(tiles)]
                put("sd", q, k, jnp.sum(sum(with_sin), axis=0, keepdims=True))


def triple(rows, ref, name):
    return cat([rows.get(ref, "%s%d" % (name, c)) for c in range(3)], 1)


def thirds(value):
    n = value.shape[1] // 3
    return [value[:, c * n : (c + 1) * n] for c in range(3)]


def force_body(
    types, depth, near, far, from_near, from_far, own_rows, index, masks, features, colmat, nh, nl, wh, wl,
    near_out, far_out, pool, save, groups, scratch,
):
    lanes = own_rows.shape[1]
    for j in range(4):
        pool[j, :, :] = whole((near, far, from_near, from_far), j)
    slots = index.shape[0] - 8
    feat = features.shape[0]
    rows = saved_rows(feat, types, slots)
    narrow = narrow_rows(feat)
    wide = wide_rows(feat, types)
    code = index[0:slots, :]
    mask = masks[0:slots, :]
    live = masks[slots : slots + 1, :]

    def coords(j, c):
        shift = pool_offsets(j, lanes)[c]
        row = pool[j, c : c + 1, :]
        return row if shift is None else row + shift

    deltas, radius = pool_deltas(coords, lambda c: own_rows[c : c + 1, :], code, lanes, depth)
    kinds = from_pool([pool[j, 7:8, :] for j in range(4)], code, lanes)
    inside = jnp.where(radius < cutoff, mask, 0.0)
    theta = omega * jnp.minimum(radius, cutoff)
    c1, s1 = jnp.cos(theta), jnp.sin(theta)
    ir = 1.0 / radius
    env = 0.5 * (c1 + 1.0) * inside
    e = env * ir
    e1 = ((-0.5 * omega) * s1 * inside - e) * ir
    e2 = ((-0.5 * omega * omega) * c1 * inside - 2.0 * e1) * ir
    unit = [d * ir for d in deltas]
    for name, value in (("e", e), ("e1", e1), ("e2", e2), ("ir", ir), ("t", kinds)):
        rows.put(save, name, value)
    for c in range(3):
        rows.put(save, "u%d" % c, unit[c])
    sin_at, cos_at = rows.at["sin"][0], rows.at["cos"][0]
    multiples(c1, s1, save.at[sin_at : sin_at + slots * USED, :], save.at[cos_at : cos_at + slots * USED, :], slots)

    def read_sin(k):
        return save[sin_at + k * USED : sin_at + (k + 1) * USED, :]

    def read_cos(k):
        return save[cos_at + k * USED : cos_at + (k + 1) * USED, :]

    coefs = [e] + [e * u for u in unit]
    mask_at = rows.at["mask"][0]

    def put_mask(i, value):
        save[mask_at + 8 * i : mask_at + 8 * i + 8, :] = value

    type_masks(kinds, types, put_mask)

    def read_mask(i):
        return save[mask_at + 8 * i : mask_at + 8 * i + 8, :]

    slot_sums(read_sin, read_cos, coefs, None, read_mask, slots, types, lambda q, v: rows.put(save, "A%d" % q, v))

    def nw(name):
        return narrow.get(nh, name), narrow.get(nl, name)

    def wd(name, first=None, last=None, rsl=slice(None)):
        return tuple(wide.get(r, name)[rsl, first:last] for r in (wh, wl))

    a0 = split(rows.get(save, "A0"))
    av = split(cat([rows.get(save, "A%d" % q) for q in (1, 2, 3)], 1))
    s_one = features[...] + dot3(wd("BT", rsl=slice(0, feat)), a0)
    v = dot3(wd("BT", rsl=slice(feat, 2 * feat)), av)
    uw = dot3(nw("RQT"), split(v))
    turned, mirrored = thirds(uw[0:feat]), thirds(uw[feat : 2 * feat])
    q = turned[0] * mirrored[0] + turned[1] * mirrored[1] + turned[2] * mirrored[2]
    n = jnp.sqrt(mirrored[0] * mirrored[0] + mirrored[1] * mirrored[1] + mirrored[2] * mirrored[2] + 1.0)
    joined = cat([s_one, n], 0)
    h = dot3(wd("CT"), split(joined))
    gate = lax.logistic(h)
    z = h * gate
    dz = gate * (1.0 + h * (1.0 - gate))
    d2z = gate * (1.0 - gate) * (2.0 + h * (1.0 - 2.0 * gate))
    a = dot3(nw("ST"), split(z))
    a2 = a[feat : 2 * feat]
    s_two = s_one + a[0:feat] + a2 * q
    y = dot3(nw("RT"), split(s_two))
    gate = lax.logistic(y)
    dy = gate * (1.0 + y * (1.0 - gate))
    d2y = gate * (1.0 - gate) * (2.0 + y * (1.0 - 2.0 * gate))
    ldy = dy * live
    yb = colmat[...] * ldy
    s2b = dot3(nw("R"), split(yb))
    ab = cat([s2b, s2b * q], 0)
    qb = s2b * a2
    zb = dot3(wd("S"), split(ab))
    hb = zb * dz
    jb = dot3(nw("C"), split(hb))
    s1b = s2b + jb[0:feat]
    nbn = jb[feat : 2 * feat] / n
    uwb = cat(
        [
            cat([qb * mirrored[c] for c in range(3)], 1),
            cat([nbn * mirrored[c] + qb * turned[c] for c in range(3)], 1),
        ],
        0,
    )
    vb = dot3(wd("RQ"), split(uwb))
    for name, value in (
        ("joined", joined), ("ab", ab), ("z", z), ("dz", dz), ("d2z", d2z), ("a2", a2), ("q", q), ("n", n),
        ("s2", s_two), ("yb", yb), ("yc", colmat[...] * live * d2y), ("ldy", ldy), ("s2b", s2b), ("zb", zb),
        ("hb", hb), ("qb", qb), ("nbn", nbn), ("s1b", s1b),
    ):
        rows.put(save, name, value)
    for name, value in (("v", v), ("uw", uw), ("uwb", uwb), ("vb", vb)):
        for c, part in enumerate(thirds(value)):
            rows.put(save, "%s%d" % (name, c), part)
    ab0 = dot3(wd("B", 0, feat), split(s1b))
    abv = thirds(dot3(wd("B", feat, 2 * feat), split(vb)))

    def put(name, q, k, row):
        start = rows.at["%s%d" % (name, q)][0] + k
        save[start : start + 1, :] = row

    tables = [ab0] + abv
    slot_reads(lambda q: tables[q], kinds, read_sin, read_cos, slots, types, put, True)
    sa = [rows.get(save, "sa%d" % q) for q in range(4)]
    sb = [rows.get(save, "sb%d" % q) for q in range(4)]
    z_sum = unit[0] * sa[1] + unit[1] * sa[2] + unit[2] * sa[3]
    x_sum = sb[0] + unit[0] * sb[1] + unit[1] * sb[2] + unit[2] * sb[3]
    rb = e * x_sum + e1 * (sa[0] + z_sum) - ir * e * z_sum
    deltas_bar = [rb * unit[c] + e * ir * sa[c + 1] for c in range(3)]
    pool_partials(deltas_bar, code, lambda j: index[slots + j : slots + j + 1, :], (near_out, far_out), groups, scratch, lanes)


def centres_of(bins, bin_total):
    return 0.1 * jnp.sqrt(3600.0 * (bins.astype(f32) + 0.5) / bin_total)


def hist_body(
    depth, bin_total, pool, near, far, from_near, from_far, index, masks, bins,
    next_own, slopes, hist, moved, scratch,
):
    lanes = pool.shape[2]
    slots = index.shape[0] - 8
    code = index[0:slots, :]
    inverse = index[slots + 4 : slots + 5, :]
    mask = masks[0:slots, :]
    for j in range(4):
        kick = (0.5 * time_step * time_step) * pool[j, 6:7, :]
        force = whole((near, far, from_near, from_far), j)
        moved[j, 0:3, :] = pool[j, 0:3, :] + time_step * pool[j, 3:6, :] - kick * force[0:3, :]
    inverse8 = jnp.broadcast_to(inverse, (8, lanes))
    own = []
    for c in range(3):
        row = from_pool([moved[j, c : c + 1, :] for j in range(4)], inverse8, lanes)[0:1, :]
        next_own[c : c + 1, :] = row
        own.append(row)

    def coords(j, c):
        shift = pool_offsets(j, lanes)[c]
        row = moved[j, c : c + 1, :]
        return row if shift is None else row + shift

    deltas, radius = pool_deltas(coords, lambda c: own[c], code, lanes, depth)
    gap = radius - centres_of(bins[...], bin_total)
    kernel = jnp.exp(-gap * gap / sigma_two) * mask
    scale = kernel * gap * (-2.0 / sigma_two) / radius
    for c in range(3):
        slopes[c * slots : (c + 1) * slots, :] = scale * deltas[c]
    sums = scatter_lanes([kernel], bins[...], scratch, bin_total)
    hist[...] = jnp.broadcast_to(sums[0:1, :], hist.shape)


def adjoint_body(atoms_total, hists, target, slopes, index, bins, near, far, groups, scratch):
    lanes = bins.shape[1]
    slots = bins.shape[0]
    code = index[0:slots, :]
    total = jnp.sum(hists[...], axis=0, keepdims=True)
    weights = 2.0 * (total / atoms_total - target[...]) / atoms_total
    picked = lane_take(weights, bins[...])
    deltas_bar = [picked * slopes[c * slots : (c + 1) * slots, :] for c in range(3)]
    pool_partials(deltas_bar, code, lambda j: index[slots + j : slots + j + 1, :], (near, far), groups, scratch, lanes)


def grads_body(
    types, pool, near, far, from_near, from_far, index, save, colmat, phi, filt, nh, nl, wh, wl,
    keep, send, adjoint, after, tangents, grads,
):
    lanes = pool.shape[2]
    slots = index.shape[0] - 8
    feat = colmat.shape[0]
    rows = saved_rows(feat, types, slots)
    narrow = narrow_rows(feat)
    wide = wide_rows(feat, types)
    code = index[0:slots, :]
    inverse8 = jnp.broadcast_to(index[slots + 4 : slots + 5, :], (8, lanes))

    def get(name):
        return rows.get(save, name)

    for j in range(4):
        adjoint[j, :, :] = whole((near, far, from_near, from_far), j)
    probe = [
        [(0.5 * time_step * time_step) * pool[j, 6:7, :] * adjoint[j, c : c + 1, :] for j in range(4)]
        for c in range(3)
    ]
    moves = [
        from_pool(probe[c], code, lanes) - from_pool(probe[c], inverse8, lanes)[0:1, :] for c in range(3)
    ]
    e, e1, e2, ir, kinds = get("e"), get("e1"), get("e2"), get("ir"), get("t")
    unit = [get("u%d" % c) for c in range(3)]
    dr = unit[0] * moves[0] + unit[1] * moves[1] + unit[2] * moves[2]
    du = [(moves[c] - unit[c] * dr) * ir for c in range(3)]
    de = e1 * dr
    sin_at, cos_at = rows.at["sin"][0], rows.at["cos"][0]

    def read_sin(k):
        return save[sin_at + k * USED : sin_at + (k + 1) * USED, :]

    def read_cos(k):
        return save[cos_at + k * USED : cos_at + (k + 1) * USED, :]

    k_rows = STRIDE * types

    def put_sum(q, value):
        tangents[q * k_rows : (q + 1) * k_rows, :] = value

    sin_coef = [de] + [de * unit[c] + e * du[c] for c in range(3)]
    cos_coef = [e * dr] + [e * dr * unit[c] for c in range(3)]
    mask_at = rows.at["mask"][0]

    def read_mask(i):
        return save[mask_at + 8 * i : mask_at + 8 * i + 8, :]

    slot_sums(read_sin, read_cos, sin_coef, cos_coef, read_mask, slots, types, put_sum)

    def nw(name):
        return narrow.get(nh, name), narrow.get(nl, name)

    def wd(name, first=None, last=None, rsl=slice(None)):
        return tuple(wide.get(r, name)[rsl, first:last] for r in (wh, wl))

    da_zero = tangents[0:k_rows, :]
    da_vec = cat([tangents[q * k_rows : (q + 1) * k_rows, :] for q in (1, 2, 3)], 1)
    ds1 = dot3(wd("BT", rsl=slice(0, feat)), split(da_zero))
    dv = dot3(wd("BT", rsl=slice(feat, 2 * feat)), split(da_vec))
    duw = dot3(nw("RQT"), split(dv))
    d_turn, d_mirr = thirds(duw[0:feat]), thirds(duw[feat : 2 * feat])
    turned = [get("uw%d" % c)[0:feat] for c in range(3)]
    mirrored = [get("uw%d" % c)[feat : 2 * feat] for c in range(3)]
    q, n, a2, dz, d2z = get("q"), get("n"), get("a2"), get("dz"), get("d2z")
    s2b, zb, qb, nbn = get("s2b"), get("zb"), get("qb"), get("nbn")
    dq = sum(d_turn[c] * mirrored[c] + turned[c] * d_mirr[c] for c in range(3))
    dn = sum(mirrored[c] * d_mirr[c] for c in range(3)) / n
    dj = cat([ds1, dn], 0)
    dh = dot3(wd("CT"), split(dj))
    dzt = dz * dh
    da = dot3(nw("ST"), split(dzt))
    da2 = da[feat : 2 * feat]
    ds2 = ds1 + da[0:feat] + da2 * q + a2 * dq
    dyt = dot3(nw("RT"), split(ds2))
    dyb = get("yc") * dyt
    ds2b = dot3(nw("R"), split(dyb))
    dab = cat([ds2b, ds2b * q + s2b * dq], 0)
    dqb = ds2b * a2 + s2b * da2
    dzb = dot3(wd("S"), split(dab))
    dhb = dzb * dz + zb * (d2z * dh)
    djb = dot3(nw("C"), split(dhb))
    ds1b = ds2b + djb[0:feat]
    dnbn = (djb[feat : 2 * feat] - nbn * dn) / n
    duwb = cat(
        [
            cat([dqb * mirrored[c] + qb * d_mirr[c] for c in range(3)], 1),
            cat(
                [
                    dnbn * mirrored[c] + nbn * d_mirr[c] + dqb * turned[c] + qb * d_turn[c]
                    for c in range(3)
                ],
                1,
            ),
        ],
        0,
    )
    dvb = dot3(wd("RQ"), split(duwb))

    def both(first, second, third, fourth):
        return -dot3(split(cat([first, second], 1)), split(cat([third, fourth], 1)), NT)

    parts = grads.shape[0]
    share = feat // parts
    rq = both(dv, triple(rows, save, "v"), triple(rows, save, "uwb"), duwb)
    cg = both(dj, get("joined"), get("hb"), dhb)
    sg = both(dzt, get("z"), get("ab"), dab)
    rg = both(ds2, get("s2"), get("yb"), dyb)
    bs = both(da_zero, get("A0"), get("s1b"), ds1b)
    bv = both(da_vec, cat([get("A%d" % i) for i in (1, 2, 3)], 1), triple(rows, save, "vb"), dvb)
    low, high = split(get("ldy") * dyt)
    ones = jnp.ones((16, lanes), bf16)
    col = -(dot1(ones, low, NT) + dot1(ones, high, NT))
    fg, pg = [], []
    for half, value in enumerate((bs, bv)):
        cols = slice(half * feat, (half + 1) * feat)
        total = None
        for t in range(types):
            block = value[STRIDE * t : STRIDE * t + USED, :]
            term = block * phi[t : t + 1, cols]
            total = term if total is None else total + term
            pg.append((half, t, jnp.sum(block * filt[0:USED, cols], axis=0, keepdims=True)))
        fg.append(total)
    base = 7 * share
    place = iota((10, lanes), 1)
    for part in range(parts):
        mine = slice(part * share, (part + 1) * share)
        grads[part, 0:share, :] = rq[mine, 0:feat]
        grads[part, share : 2 * share, :] = rq[mine, feat : 2 * feat]
        grads[part, 2 * share : 4 * share, :] = cg[2 * part * share : 2 * (part + 1) * share, :]
        grads[part, 4 * share : 5 * share, :] = sg[mine, 0:feat]
        grads[part, 5 * share : 6 * share, :] = sg[mine, feat : 2 * feat]
        grads[part, 6 * share : 7 * share, :] = rg[mine, :]
        for half, t, row in pg:
            at = base + half * types + t
            grads[part, at : at + 1, :] = row
        chosen = fg[part // 2]
        rolled = pltpu.roll(chosen, feat // 2, 1)
        here, there = (chosen, rolled) if part % 2 == 0 else (rolled, chosen)
        at = base + 2 * types
        grads[part, at : at + 10, :] = jnp.where(place < feat // 2, here[0:10, :], there[10:20, :])
        grads[part, at + 10 : at + 11, :] = col[0:1, :]
        grads[part, at + 11 :, :] = jnp.zeros((grads.shape[1] - at - 11, lanes), f32)

    odd = lax.axis_index("slab") % 2
    half = grads.shape[1] // 2
    keep[...] = grads[:, pl.ds(pl.multiple_of(odd * half, half), half), :]
    send[...] = grads[:, pl.ds(pl.multiple_of((1 - odd) * half, half), half), :]
    for c in range(3):
        after[c * slots : (c + 1) * slots, :] = du[c]
        after[4 * slots + (c + 1) * feat : 4 * slots + (c + 2) * feat, :] = dvb[:, c * lanes : (c + 1) * lanes]
    after[3 * slots : 4 * slots, :] = dr
    after[4 * slots : 4 * slots + feat, :] = ds1b


def moves_body(types, index, save, after, wh, wl, near, far, sums, groups, scratch):
    lanes = index.shape[1]
    slots = index.shape[0] - 8
    feat = lanes
    rows = saved_rows(feat, types, slots)
    wide = wide_rows(feat, types)
    code = index[0:slots, :]

    def get(name):
        return rows.get(save, name)

    def wd(name, first, last):
        return tuple(wide.get(r, name)[:, first:last] for r in (wh, wl))

    e, e1, e2, ir, kinds = get("e"), get("e1"), get("e2"), get("ir"), get("t")
    unit = [get("u%d" % c) for c in range(3)]
    du = [after[c * slots : (c + 1) * slots, :] for c in range(3)]
    dr = after[3 * slots : 4 * slots, :]
    de, de1, dir_ = e1 * dr, e2 * dr, -ir * ir * dr
    sin_at, cos_at = rows.at["sin"][0], rows.at["cos"][0]

    def read_sin(k):
        return save[sin_at + k * USED : sin_at + (k + 1) * USED, :]

    def read_cos(k):
        return save[cos_at + k * USED : cos_at + (k + 1) * USED, :]

    ds1b = after[4 * slots : 4 * slots + feat, :]
    dvb = cat([after[4 * slots + (c + 1) * feat : 4 * slots + (c + 2) * feat, :] for c in range(3)], 1)
    dab0 = dot3(wd("B", 0, feat), split(ds1b))
    dabv = thirds(dot3(wd("B", feat, 2 * feat), split(dvb)))
    tables = [dab0] + dabv

    def put(name, q, k, row):
        start = (0 if name == "sa" else 4 * slots) + q * slots + k
        sums[start : start + 1, :] = row

    slot_reads(lambda q: tables[q], kinds, read_sin, read_cos, slots, types, put, False)
    sa = [get("sa%d" % q) for q in range(4)]
    sb = [get("sb%d" % q) for q in range(4)]
    sd = [get("sd%d" % q) for q in range(4)]
    dsa = [sb[q] * dr + sums[q * slots : (q + 1) * slots, :] for q in range(4)]
    dsb = [
        sums[(4 + q) * slots : (5 + q) * slots, :] - sd[q] * dr for q in range(4)
    ]
    z_sum = sum(unit[c] * sa[c + 1] for c in range(3))
    x_sum = sb[0] + sum(unit[c] * sb[c + 1] for c in range(3))
    dz_sum = sum(du[c] * sa[c + 1] + unit[c] * dsa[c + 1] for c in range(3))
    dx_sum = dsb[0] + sum(du[c] * sb[c + 1] + unit[c] * dsb[c + 1] for c in range(3))
    rb = e * x_sum + e1 * (sa[0] + z_sum) - ir * e * z_sum
    drb = (
        de * x_sum + e * dx_sum + de1 * (sa[0] + z_sum) + e1 * (dsa[0] + dz_sum)
        - (dir_ * e + ir * de) * z_sum - ir * e * dz_sum
    )
    deltas_bar = [
        drb * unit[c] + rb * du[c] + (de * ir + e * dir_) * sa[c + 1] + e * ir * dsa[c + 1]
        for c in range(3)
    ]
    pool_partials(deltas_bar, code, lambda j: index[slots + j : slots + j + 1, :], (near, far), groups, scratch, lanes)


def last_body(
    types, parts, atoms_total, mine, other, adjoint, near, far, index, slope, hidden_t, table_t, spreader, next_own,
    next_out, adj, enc, spr, fil, rot, ref, com, spl, rea, col, total,
):
    next_out[...] = next_own[...]
    odd = lax.axis_index("slab") % 2
    half = mine.shape[0]
    total[pl.ds(pl.multiple_of(odd * half, half), half), :] = mine[...]
    total[pl.ds(pl.multiple_of((1 - odd) * half, half), half), :] = other[...]
    lanes = adjoint.shape[2]
    slots = index.shape[0] - 8
    feat = lanes
    share = feat // parts
    inverse8 = jnp.broadcast_to(index[slots + 4 : slots + 5, :], (8, lanes))
    crossed = parity("cross")
    near_v, far_v = near[...], far[...]
    second = (jnp.where(crossed, near_v, far_v), jnp.where(crossed, far_v, near_v))
    for c in range(3):
        rows = [
            atoms_total * (adjoint[j, c : c + 1, :] - second[j % 2][j // 2, c : c + 1, :]) for j in range(4)
        ]
        adj[c : c + 1, :] = from_pool(rows, inverse8, lanes)[0:1, :]
    rot[...] = total[0:share, :]
    ref[...] = total[share : 2 * share, :]
    com[...] = total[2 * share : 4 * share, :]
    spl[:, 0:feat] = total[4 * share : 5 * share, :]
    spl[:, feat : 2 * feat] = total[5 * share : 6 * share, :]
    rea[...] = total[6 * share : 7 * share, :]
    base = 7 * share
    phib = cat([total[base : base + types, :], total[base + types : base + 2 * types, :]], 1)
    at = base + 2 * types
    block = total[at : at + 10, :]
    fil[0:10, :] = block[:, 0 : feat // 2]
    fil[10:20, :] = pltpu.roll(block, feat // 2, 1)[:, 0 : feat // 2]
    col_row = total[at + 10 : at + 11, :]
    spare = jnp.zeros((types, 2 * feat), f32)
    pre_bar = dot3(split(cat([phib, spare], 0)), split(spreader[...]), NT)[0:types] * slope[...]
    here = pl.ds(pl.multiple_of(lax.axis_index("cross") * share, share), share)
    rest = jnp.zeros((lanes - types, feat), f32)
    spr[...] = dot3(split(hidden_t[here, :]), split(cat([phib, cat([rest, rest], 1)], 0)))
    enc[...] = dot3(split(table_t[here, :]), split(cat([pre_bar, rest], 0)))
    for part in range(parts):
        @pl.when(lax.axis_index("cross") == part)
        def _():
            col[...] = col_row[:, part * share : (part + 1) * share]


def neighbours_swap(near, far, axis):
    count = lax.axis_size(axis)
    forward = [(i, (i + 1) % count) for i in range(count)]
    pairs = [[p for a, b in forward if a % 2 == side for p in ((a, b), (b, a))] for side in (0, 1)]
    from_far = lax.ppermute(far, axis, pairs[1])
    from_near = lax.ppermute(near, axis, pairs[0])
    return from_near, from_far


def corner_sum(near, far):
    near, far = call(turn_body, [(near.shape, f32)] * 2, near, far, *neighbours_swap(near, far, "slab"))
    return (near, far) + neighbours_swap(near, far, "cross")


def swap(x, axis, bit):
    return lax.ppermute(x, axis, [(i, i ^ bit) for i in range(lax.axis_size(axis))])


def halve(bit, x, other, keep, send):
    mine = (lax.axis_index("cross") // bit) % 2
    shape = (x.shape[0] // 2, 2) + x.shape[1:]
    x, other = x.reshape(shape), other.reshape(shape)
    for ref, side in ((keep, mine), (send, 1 - mine)):
        value = x[:, pl.ds(side, 1)] + other[:, pl.ds(side, 1)]
        ref[...] = value.reshape(ref.shape)


def halve_hold_body(bit, x, other, near, far, keep, send, near_out, far_out):
    halve(bit, x, other, keep, send)
    near_out[...] = near[...]
    far_out[...] = far[...]


def halve_turn_body(bit, x, other, near, far, from_near, from_far, keep, send, near_out, far_out):
    halve(bit, x, other, keep, send)
    turn_body(near, far, from_near, from_far, near_out, far_out)


def add_body(x, other, out):
    out[...] = x[...] + other[...]


def add_two_body(x, other, side, from_side, out, total):
    add_body(x, other, out)
    add_body(side, from_side, total)


def reduce_all(keep, send, near, far):
    slab_count, cross_count = lax.axis_size("slab"), lax.axis_size("cross")
    group = (near.shape, f32)
    other = swap(send, "slab", 1)
    bit, step, received = 1, 0, None
    while bit < cross_count:
        half = ((keep.shape[0] // 2,) + keep.shape[1:], f32)
        if step == 0:
            keep, send, near, far = call(
                functools.partial(halve_hold_body, bit), [half, half, group, group], keep, other, near, far
            )
            received = neighbours_swap(near, far, "slab")
        elif step == 1:
            keep, send, near, far = call(
                functools.partial(halve_turn_body, bit), [half, half, group, group],
                keep, other, near, far, *received,
            )
            received = neighbours_swap(near, far, "cross")
        else:
            raise NotImplementedError
        other = swap(send, "cross", bit)
        bit, step = 2 * bit, step + 1
    x, other = keep[0], other[0]
    waiting, sides = [(far, received[1]), (near, received[0])], []

    def add(x, other):
        shapes = [(x.shape, f32)]
        if waiting:
            x, side = call(add_two_body, shapes + [group], x, other, *waiting.pop(0))
            sides.append(side)
            return x
        return call(add_body, shapes, x, other)[0]

    bit = 2
    while bit < slab_count:
        x = add(x, other)
        other = swap(x, "slab", bit)
        bit *= 2
    x = add(x, other)
    while waiting:
        sides += call(add_body, [group], *waiting.pop(0))
    return x, swap(x, "slab", 1), sides[::-1]


def device_step(
    positions, velocities, inverse_mass, species, type_table, neighbours, slot_count, atom_count,
    pair_bins, send_list, target, encoder, spreader, filters, rotator, reflector, combiner, splitter,
    readout, collector,
):
    lanes = positions.shape[1]
    slots = neighbours.shape[1]
    types, feat = type_table.shape
    bin_total = target.shape[0]
    slab_count, cross_count = lax.axis_size("slab"), lax.axis_size("cross")
    devices = slab_count * cross_count
    atoms_total = float(lanes * devices)
    depth = 1.6 * (lanes // 16)
    parts = cross_count
    row = lambda x: x.reshape(1, x.shape[0])
    i32 = jnp.int32
    vm, dma = pltpu.VMEM, pltpu.SemaphoreType.DMA
    narrow, wide = narrow_rows(feat).total, wide_rows(feat, types).total
    group = ((2, 8, lanes), f32)
    pool_shape = ((4, 8, lanes), f32)
    pair_scratch = vm((16 * slots, lanes), f32)
    near, far, own_rows, send = call(
        offer_body, [group, group, ((8, lanes), f32), ((8, lanes), i32)],
        *in_hbm(positions, velocities, row(inverse_mass), row(species), send_list),
        specs=[HB] * 5,
        scratch=[
            vm((3, lanes), f32), vm((3, lanes), f32), vm((1, lanes), f32), vm((1, lanes), i32),
            vm(send_list.shape, i32), vm((4, 8, lanes), f32), dma((5,)),
        ],
    )
    colmat, nh, nl, wh, wl, phi, slope, hidden_t, table_t, filt, spreader_in = call(
        weights_body,
        [
            ((feat, lanes), f32), ((narrow, feat), bf16), ((narrow, feat), bf16), ((wide, 2 * feat), bf16),
            ((wide, 2 * feat), bf16), ((types, 2 * feat), f32), ((types, feat), f32), ((feat, lanes), f32),
            ((feat, lanes), f32), ((STRIDE, 2 * feat), f32), (spreader.shape, f32),
        ],
        *in_hbm(
            type_table, encoder, spreader, filters, rotator, reflector, combiner, splitter, readout,
            row(collector),
        ),
        specs=[HB] * 10,
        scratch=[
            vm(type_table.shape, f32), vm(encoder.shape, f32), vm(filters.shape, f32), vm(rotator.shape, f32),
            vm(reflector.shape, f32), vm(combiner.shape, f32), vm(splitter.shape, f32), vm(readout.shape, f32),
            vm((1, feat), f32), dma((10,)),
        ],
    )
    index, masks, features, bins, goal = call(
        index_body,
        [
            ((slots + 8, lanes), i32), ((slots + 8, lanes), f32), ((feat, lanes), f32), ((slots, lanes), i32),
            ((1, bin_total), f32),
        ],
        *in_hbm(neighbours.T, row(slot_count), pair_bins.T, row(target)),
        atom_count, send, own_rows, table_t,
        specs=[HB] * 4 + [SM] + [VM] * 3,
        scratch=[vm((slots, lanes), i32), vm((1, lanes), i32), dma((4,))],
    )
    pieces = corner_sum(near, far)
    save_rows = saved_rows(feat, types, slots).total
    near, far, pool, save = call(
        functools.partial(force_body, types, depth),
        [group, group, pool_shape, ((save_rows, lanes), f32)],
        *pieces, own_rows, index, masks, features, colmat, nh, nl, wh, wl,
        scratch=[vm((4, 8, lanes), f32), pair_scratch],
    )
    pieces = corner_sum(near, far)
    next_positions, slopes, hist = call(
        functools.partial(hist_body, depth, bin_total),
        [((3, lanes), f32), ((3 * slots, lanes), f32), ((devices, bin_total), f32)],
        pool, *pieces, index, masks, bins,
        scratch=[vm((4, 8, lanes), f32), pair_scratch],
    )
    hists = lax.all_to_all(hist.reshape(devices, 1, bin_total), ("slab", "cross"), 0, 0)
    near, far = call(
        functools.partial(adjoint_body, atoms_total), [group, group],
        hists.reshape(devices, bin_total), goal, slopes, index, bins,
        scratch=[vm((4, 8, lanes), f32), pair_scratch],
    )
    pieces = corner_sum(near, far)
    half_grads = ((parts, feat, lanes), f32)
    keep, send, adjoint, after = call(
        functools.partial(grads_body, types),
        [half_grads, half_grads, pool_shape, ((4 * slots + 4 * feat, lanes), f32)],
        pool, *pieces, index, save, colmat, phi, filt, nh, nl, wh, wl,
        scratch=[vm((4 * STRIDE * types, lanes), f32), vm((parts, 2 * feat, lanes), f32)],
    )
    near, far = call(
        functools.partial(moves_body, types), [group, group], index, save, after, wh, wl,
        scratch=[vm((8 * slots, lanes), f32), vm((4, 8, lanes), f32), pair_scratch],
    )
    mine, other, sides = reduce_all(keep, send, near, far)
    share = feat // parts
    results = call(
        functools.partial(last_body, types, parts, atoms_total),
        [
            ((3, lanes), f32), ((3, lanes), f32), ((share, feat), f32), ((share, 2 * feat), f32),
            ((filters.shape[0], 2 * feat // parts), f32), ((share, feat), f32), ((share, feat), f32),
            ((2 * share, feat), f32), ((share, 2 * feat), f32), ((share, feat), f32), ((1, share), f32),
        ],
        mine, other, adjoint, *sides, index, slope, hidden_t, table_t, spreader_in, next_positions,
        scratch=[vm((2 * feat, lanes), f32)],
        keep=False,
    )
    return tuple(results[:10]) + (results[10].reshape(share),)


def solution(mesh):
    both = ("slab", "cross")
    in_specs = (
        P(None, both), P(None, both), P(both), P(both), P(), P(both, None), P(both), P(both), P(both, None),
        P("slab", "cross", None),
    ) + (P(),) * 10
    out_specs = (
        P(None, both), P(None, both), P("cross", None), P("cross", None), P(None, "cross"), P("cross", None),
        P("cross", None), P("cross", None), P("cross", None), P("cross", None), P("cross"),
    )
    return jax.shard_map(device_step, mesh=mesh, in_specs=in_specs, out_specs=out_specs, check_vma=False)
```

```python
import functools

import jax
import jax.numpy as jnp
from jax import lax
from jax.experimental import pallas as pl
from jax.experimental.pallas import tpu as pltpu
from jax.sharding import PartitionSpec as P


cutoff = 5.0
soften = 0.25
sigma_two = 0.18
slab_length = 10.0
cell_length = 10.0
time_step = 0.5
highest = lax.Precision.HIGHEST
f32 = jnp.float32
bf16 = jnp.bfloat16
pi = 3.141592653589793
omega = pi / cutoff

NN = ((1,), (0,))
NT = ((1,), (1,))
VM = pl.BlockSpec(memory_space=pltpu.VMEM)
SM = pl.BlockSpec(memory_space=pltpu.SMEM)
HB = pl.BlockSpec(memory_space=pltpu.HBM)


def call(body, outs, *args, specs=None, scratch=(), keep=True):
    return pl.pallas_call(
        body,
        out_shape=[(pltpu.VMEM if keep else jax.ShapeDtypeStruct)(s, d) for s, d in outs],
        in_specs=[VM] * len(args) if specs is None else specs,
        out_specs=[VM] * len(outs),
        scratch_shapes=list(scratch),
        compiler_params=pltpu.CompilerParams(vmem_limit_bytes=16 * 2**20),
    )(*args)


def in_hbm(*arrays):
    return [pltpu.with_memory_space_constraint(x, pltpu.HBM) for x in arrays]


def fetch(sources, targets, semaphores):
    copies = [
        pltpu.make_async_copy(source, target, semaphores.at[i])
        for i, (source, target) in enumerate(zip(sources, targets))
    ]
    for copy in copies:
        copy.start()
    for copy in copies:
        copy.wait()


def split(x):
    high = x.astype(bf16)
    return high, (x - high.astype(f32)).astype(bf16)


def dot1(a, b, dims):
    return lax.dot_general(a, b, (dims, ((), ())), preferred_element_type=f32)


def dot3(a, b, dims=NN):
    return dot1(
        jnp.concatenate([a[0], a[0], a[1]], dims[0][0]), jnp.concatenate([b[0], b[1], b[0]], dims[1][0]), dims
    )


def cat(parts, axis):
    return jnp.concatenate(parts, axis=axis)


def iota(shape, dim):
    return lax.broadcasted_iota(jnp.int32, shape, dim)


def lane_take(row, index):
    return jnp.take_along_axis(jnp.broadcast_to(row, index.shape), index, axis=1)


def own_lanes(group, lanes):
    quarter = lanes // 4
    start = 2 * quarter * (1 - group // 2) + quarter * (1 - group % 2)
    return start, quarter


def pool_offsets(group, lanes):
    place = iota((1, lanes), 1)
    up, right = group // 2, group % 2
    half, quarter = lanes // 2, lanes // 4
    first = (place >= half) if up else (place < half)
    second_bit = place % half >= quarter
    second = second_bit if right else jnp.logical_not(second_bit)
    sign_u, sign_r = 2.0 * up - 1.0, 2.0 * right - 1.0
    return (
        jnp.where(first, sign_u * slab_length, 0.0).astype(f32),
        jnp.where(second, sign_r * cell_length, 0.0).astype(f32),
        None,
    )


def from_pool(rows, code, lanes):
    group = code // lanes
    lane = code % lanes
    out = lane_take(rows[0], lane)
    for j in range(1, 4):
        out = jnp.where(group == j, lane_take(rows[j], lane), out)
    return out


def pool_deltas(pool_rows, own_rows, code, lanes, depth):
    deltas = []
    for c in range(3):
        d = from_pool([pool_rows(j, c) for j in range(4)], code, lanes) - own_rows(c)
        if c == 2:
            d = d - depth * jnp.floor(d / depth + 0.5)
        deltas.append(d)
    radius = jnp.sqrt(deltas[0] * deltas[0] + deltas[1] * deltas[1] + deltas[2] * deltas[2] + soften)
    return deltas, radius


def one_hot_rows(index, slots, count):
    lanes = index.shape[1]
    place = iota((count, lanes), 0)
    return cat(
        [(place == index[k : k + 1, :]).astype(f32).astype(bf16) for k in range(slots)], 1
    )


def scatter_lanes(values, index, scratch, count):
    shape = index.shape
    slots = shape[0]
    for row in range(16):
        value = values[row] if row < len(values) else None
        if value is None:
            value = jnp.zeros(shape, f32)
        scratch[pl.ds(row, slots, stride=16), :] = value
    highs, mids, lows = [], [], []
    for k in range(slots):
        x = scratch[16 * k : 16 * k + 16, :]
        high = x.astype(bf16)
        rest = x - high.astype(f32)
        mid = rest.astype(bf16)
        highs.append(high)
        mids.append(mid)
        lows.append((rest - mid.astype(f32)).astype(bf16))
    left = cat([cat(highs, 1), cat(mids, 1), cat(lows, 1)], 0)
    sums = dot1(left, one_hot_rows(index, slots, count), NT)
    return sums[0:16] + (sums[16:32] + sums[32:48])


def pool_partials(deltas_bar, code, send_index, outs, groups, scratch, lanes):
    group = code // lanes
    values = []
    for j in range(4):
        for c in range(3):
            values.append(jnp.where(group == j, deltas_bar[c], 0.0))
        values.append(None)
    sums = scatter_lanes(values, code % lanes, scratch, lanes)
    centres = [-jnp.sum(d, axis=0, keepdims=True) for d in deltas_bar]
    place = iota((1, lanes), 1)
    for j in range(4):
        start, width = own_lanes(j, lanes)
        own = jnp.logical_and(place >= start, place < start + width)
        groups[j, :, :] = jnp.zeros((8, lanes), f32)
        for c in range(3):
            mine = lane_take(jnp.broadcast_to(centres[c], (8, lanes)), jnp.broadcast_to(send_index(j), (8, lanes)))
            groups[j, c : c + 1, :] = sums[4 * j + c : 4 * j + c + 1, :] + jnp.where(
                own, mine[0:1, :], 0.0
            )
    by_side(groups[...], *outs)


def offer_body(
    pos, vel, mass, species, send_list, near, far, own_out, send_out,
    pos_v, vel_v, mass_v, species_v, list_v, groups, semaphores,
):
    fetch((pos, vel, mass, species, send_list), (pos_v, vel_v, mass_v, species_v, list_v), semaphores)
    lanes = pos.shape[1]
    own_out[0:3, :] = pos_v[...]
    own_out[3:6, :] = vel_v[...]
    own_out[6:7, :] = mass_v[...]
    own_out[7:8, :] = species_v[...].astype(f32)
    own_rows = own_out[...]
    place = iota((8, lanes), 1)
    send_out[...] = jnp.zeros((8, lanes), jnp.int32)
    for j in range(4):
        start, width = own_lanes(j, lanes)
        pieces = [list_v[j // 2, j % 2 : j % 2 + 1, :]]
        if start:
            pieces = [jnp.zeros((1, start), jnp.int32)] + pieces
        if start + width < lanes:
            pieces = pieces + [jnp.zeros((1, lanes - start - width), jnp.int32)]
        row = cat(pieces, 1)
        send_out[j : j + 1, :] = row
        own = jnp.logical_and(place >= start, place < start + width)
        taken = jnp.take_along_axis(own_rows, jnp.broadcast_to(row, (8, lanes)), axis=1)
        groups[j, :, :] = jnp.where(own, taken, 0.0)
    by_side(groups[...], near, far)


def parity(axis):
    return lax.axis_index(axis) % 2 == 1


def by_side(groups, near, far):
    odd = parity("slab")
    low, high = groups[0:2], groups[2:4]
    near[...] = jnp.where(odd, low, high)
    far[...] = jnp.where(odd, high, low)


def turn_body(near, far, from_near, from_far, near_out, far_out):
    odd = parity("slab")
    near_sum, far_sum = near[...] + from_near[...], far[...] + from_far[...]
    low, high = jnp.where(odd, near_sum, far_sum), jnp.where(odd, far_sum, near_sum)
    odd = parity("cross")
    for u, part in enumerate((low, high)):
        near_out[u, :, :] = jnp.where(odd, part[0], part[1])
        far_out[u, :, :] = jnp.where(odd, part[1], part[0])


def whole(pieces, j):
    u = j // 2
    near_sum, far_sum = pieces[0][u] + pieces[2][u], pieces[1][u] + pieces[3][u]
    odd = parity("cross")
    return jnp.where(odd, far_sum, near_sum) if j % 2 else jnp.where(odd, near_sum, far_sum)


class Rows:
    def __init__(self, sizes):
        self.at = {}
        self.total = 0
        for name, size in sizes:
            self.at[name] = (self.total, size)
            self.total += size

    def get(self, ref, name):
        start, size = self.at[name]
        return ref[start : start + size, :]

    def put(self, ref, name, value):
        start, size = self.at[name]
        ref[start : start + size, :] = value


STRIDE = 32
USED = 24


def narrow_rows(feat):
    return Rows((("RQT", 2 * feat), ("C", 2 * feat), ("ST", 2 * feat), ("RT", feat), ("R", feat)))


def wide_rows(feat, types):
    return Rows((("BT", 2 * feat), ("B", STRIDE * types), ("RQ", feat), ("CT", feat), ("S", feat)))


def weights_body(
    table_h, encoder_h, spreader_h, filters_h, rotator_h, reflector_h, combiner_h, splitter_h, readout_h,
    collector_h, col_out, nh, nl, wh, wl, phi_out, slope_out, hidden_t, table_t, filt_out, spreader,
    table, encoder, filters, rotator, reflector, combiner, splitter, readout, collector, semaphores,
):
    fetch(
        (table_h, encoder_h, spreader_h, filters_h, rotator_h, reflector_h, combiner_h, splitter_h, readout_h,
         collector_h),
        (table, encoder, spreader, filters, rotator, reflector, combiner, splitter, readout, collector),
        semaphores,
    )
    types, feat = table.shape
    lanes = hidden_t.shape[1]
    basis = filters.shape[0]
    pre = jnp.dot(table[...], encoder[...], precision=highest, preferred_element_type=f32)
    gate = lax.logistic(pre)
    hidden = pre * gate
    phi = jnp.dot(hidden, spreader[...], precision=highest, preferred_element_type=f32)
    phi_out[...] = phi
    slope_out[...] = gate * (1.0 + pre * (1.0 - gate))
    rest = [jnp.zeros((lanes - types, feat), f32)]
    hidden_t[...] = jnp.transpose(cat([hidden] + rest, 0))
    table_t[...] = jnp.transpose(cat([table[...]] + rest, 0))
    filt_out[...] = jnp.zeros(filt_out.shape, f32)
    filt_out[0:basis, :] = filters[...]
    filt = filt_out[...]
    col_out[...] = jnp.transpose(jnp.broadcast_to(collector[...], (lanes, feat)))
    narrow = narrow_rows(feat)
    wide = wide_rows(feat, types)

    def put(rows, high_ref, low_ref, name, value, row=0, col=0):
        high, low = split(value)
        start = rows.at[name][0] + row
        high_ref[start : start + value.shape[0], col : col + value.shape[1]] = high
        low_ref[start : start + value.shape[0], col : col + value.shape[1]] = low

    per_half = feat // STRIDE
    for half in range(2):
        cols = slice(half * feat, (half + 1) * feat)
        for chunk in range(types // per_half):
            block = cat(
                [
                    filt[:, cols] * phi[t : t + 1, cols]
                    for t in range(chunk * per_half, (chunk + 1) * per_half)
                ],
                0,
            )
            put(wide, wh, wl, "B", block, chunk * feat, half * feat)
            put(wide, wh, wl, "BT", jnp.transpose(block), half * feat, chunk * feat)
    put(wide, wh, wl, "RQ", rotator[...], 0, 0)
    put(wide, wh, wl, "RQ", reflector[...], 0, feat)
    put(narrow, nh, nl, "RQT", jnp.transpose(rotator[...]), 0)
    put(narrow, nh, nl, "RQT", jnp.transpose(reflector[...]), feat)
    put(narrow, nh, nl, "C", combiner[...])
    put(wide, wh, wl, "CT", jnp.transpose(combiner[0:feat, :]), 0, 0)
    put(wide, wh, wl, "CT", jnp.transpose(combiner[feat : 2 * feat, :]), 0, feat)
    put(wide, wh, wl, "S", splitter[...])
    put(narrow, nh, nl, "ST", jnp.transpose(splitter[:, 0:feat]), 0)
    put(narrow, nh, nl, "ST", jnp.transpose(splitter[:, feat : 2 * feat]), feat)
    put(narrow, nh, nl, "R", readout[...])
    put(narrow, nh, nl, "RT", jnp.transpose(readout[...]))


def index_body(
    near_h, count_h, bins_h, target_h, atom_count, send, own_rows, table_t,
    index, masks, feat_out, bins, target, near, slot_count, semaphores,
):
    fetch((near_h, count_h, bins_h, target_h), (near, slot_count, bins, target), semaphores)
    species = own_rows[7:8, :].astype(jnp.int32)
    slots, lanes = near.shape
    quarter = lanes // 4
    lane_row = iota((16, lanes), 1).astype(f32)
    row_id = iota((16, lanes), 0)
    lefts, rights = [], []
    place = iota((lanes, lanes), 1)
    for j in range(4):
        start, width = own_lanes(j, lanes)
        own = jnp.logical_and(place >= start, place < start + width)
        same = jnp.logical_and(own, iota((lanes, lanes), 0) == send[j : j + 1, :])
        rights.append(same.astype(f32).astype(bf16))
        lefts.append(
            jnp.where(row_id == 0, lane_row, jnp.where(row_id == 1, float(j), 0.0)).astype(bf16)
        )
    found = dot1(cat(lefts, 1), cat(rights, 1), NT)
    inverse = (found[0:1, :] + lanes * found[1:2, :] + 0.5).astype(jnp.int32)
    near_v = near[...]
    ghost = near_v - lanes
    block = ghost // quarter
    p, q, g = block // 4, block % 4, ghost % quarter
    ghost_code = (2 * (p // 2) + q // 2) * lanes + 2 * quarter * (p % 2) + quarter * (q % 2) + g
    own_code = lane_take(inverse, jnp.minimum(near_v, lanes - 1))
    index[...] = jnp.zeros(index.shape, jnp.int32)
    index[0:slots, :] = jnp.where(near_v < lanes, own_code, ghost_code)
    index[slots : slots + 4, :] = send[0:4, :]
    index[slots + 4 : slots + 5, :] = inverse
    masks[...] = jnp.zeros(masks.shape, f32)
    masks[0:slots, :] = (iota((slots, lanes), 0) < slot_count[...]).astype(f32)
    masks[slots : slots + 1, :] = (iota((1, lanes), 1) < atom_count[0]).astype(f32)
    feat_out[...] = jnp.take_along_axis(table_t[...], jnp.broadcast_to(species, table_t.shape), axis=1)


def saved_rows(feat, types, slots):
    k = STRIDE * types
    pair = ("e", "e1", "e2", "ir", "u0", "u1", "u2", "t")
    sizes = [("A%d" % q, k) for q in range(4)]
    sizes += [("%s%d" % (n, c), feat) for n in ("v", "vb") for c in range(3)]
    sizes += [("%s%d" % (n, c), 2 * feat) for n in ("uw", "uwb") for c in range(3)]
    sizes += [("joined", 2 * feat), ("ab", 2 * feat)]
    sizes += [
        (n, feat)
        for n in ("z", "dz", "d2z", "a2", "q", "n", "s2", "yb", "yc", "ldy", "s2b", "zb", "hb", "qb", "nbn", "s1b")
    ]
    sizes += [("sin", slots * USED), ("cos", slots * USED), ("mask", 8 * slots * types)]
    sizes += [(n, slots) for n in pair]
    sizes += [("%s%d" % (n, q), slots) for n in ("sa", "sb", "sd") for q in range(4)]
    return Rows(sizes)


def multiples(c1, s1, sin_ref, cos_ref, slots):
    lanes = c1.shape[1]
    powers = [(c1, s1)]
    for _ in range(4):
        c, s = powers[-1]
        powers.append((c * c - s * s, 2.0 * c * s))
    sub = iota((8, lanes), 0)
    bits = [(sub // 2**b) % 2 == 1 for b in range(3)]
    order = sub.astype(f32) + 1.0

    def times(x, y):
        return x[0] * y[0] - x[1] * y[1], x[0] * y[1] + x[1] * y[0]

    for k in range(slots):
        rows = [
            tuple(jnp.broadcast_to(part[k : k + 1, :], (8, lanes)) for part in power)
            for power in powers
        ]
        z = rows[0]
        for b in range(3):
            step = (jnp.where(bits[b], rows[b][0], 1.0), jnp.where(bits[b], rows[b][1], 0.0))
            z = times(z, step)
        for v in range(3):
            if v == 1:
                zv = times(z, rows[3])
            elif v == 2:
                zv = times(z, rows[4])
            else:
                zv = z
            start = k * USED + 8 * v
            sin_ref[start : start + 8, :] = zv[1]
            cos_ref[start : start + 8, :] = zv[0] * ((order + 8.0 * v) * omega)


def type_masks(kinds, types, put):
    slots, lanes = kinds.shape
    for k in range(slots):
        kind = jnp.broadcast_to(kinds[k : k + 1, :], (8, lanes))
        for t in range(types):
            put(k * types + t, jnp.where(kind == t, 1.0, 0.0))


def choose(options, bits):
    for bit in bits:
        options = [
            jnp.where(bit, options[i + 1], options[i]) if i + 1 < len(options) else options[i]
            for i in range(0, len(options), 2)
        ]
    return options[0]


def slot_sums(read_sin, read_cos, sin_coef, cos_coef, read_mask, slots, types, put):
    lanes = sin_coef[0].shape[1]
    tiles = USED // 8
    for q in range(4):
        sums = [[None] * tiles for _ in range(types)]
        for k in range(slots):
            value = read_sin(k) * sin_coef[q][k : k + 1, :]
            if cos_coef is not None:
                value = value + read_cos(k) * cos_coef[q][k : k + 1, :]
            for t in range(types):
                mask = read_mask(k * types + t)
                for v in range(tiles):
                    part = value[8 * v : 8 * v + 8] * mask
                    sums[t][v] = part if sums[t][v] is None else sums[t][v] + part
        rest = jnp.zeros((STRIDE - USED, lanes), f32)
        put(q, cat([x for t in range(types) for x in sums[t] + [rest]], 0))


def slot_reads(values, kinds, read_sin, read_cos, slots, types, put, with_square):
    lanes = kinds.shape[1]
    tiles = USED // 8
    whole_kinds = (kinds + 0.5).astype(jnp.int32)
    kind_bits = [((whole_kinds // 2**b) % 2).astype(f32) for b in range((types - 1).bit_length())]
    square = [((iota((8, lanes), 0).astype(f32) + (8.0 * v + 1.0)) * omega) ** 2 for v in range(tiles)]
    for q in range(4):
        value = values(q)
        tables = [
            [value[STRIDE * t + 8 * v : STRIDE * t + 8 * v + 8] for v in range(tiles)] for t in range(types)
        ]
        for k in range(slots):
            bits = [jnp.broadcast_to(part[k : k + 1, :], (8, lanes)) > 0.5 for part in kind_bits]
            picked = [choose([table[v] for table in tables], bits) for v in range(tiles)]
            sines, cosines = read_sin(k), read_cos(k)
            with_sin = [sines[8 * v : 8 * v + 8] * picked[v] for v in range(tiles)]
            put("sa", q, k, jnp.sum(sum(with_sin), axis=0, keepdims=True))
            with_cos = [cosines[8 * v : 8 * v + 8] * picked[v] for v in range(tiles)]
            put("sb", q, k, jnp.sum(sum(with_cos), axis=0, keepdims=True))
            if with_square:
                with_sin = [with_sin[v] * square[v] for v in range(tiles)]
                put("sd", q, k, jnp.sum(sum(with_sin), axis=0, keepdims=True))


def triple(rows, ref, name):
    return cat([rows.get(ref, "%s%d" % (name, c)) for c in range(3)], 1)


def thirds(value):
    n = value.shape[1] // 3
    return [value[:, c * n : (c + 1) * n] for c in range(3)]


def force_body(
    types, depth, near, far, from_near, from_far, own_rows, index, masks, features, colmat, nh, nl, wh, wl,
    near_out, far_out, pool, save, groups, scratch,
):
    lanes = own_rows.shape[1]
    for j in range(4):
        pool[j, :, :] = whole((near, far, from_near, from_far), j)
    slots = index.shape[0] - 8
    feat = features.shape[0]
    rows = saved_rows(feat, types, slots)
    narrow = narrow_rows(feat)
    wide = wide_rows(feat, types)
    code = index[0:slots, :]
    mask = masks[0:slots, :]
    live = masks[slots : slots + 1, :]

    def coords(j, c):
        shift = pool_offsets(j, lanes)[c]
        row = pool[j, c : c + 1, :]
        return row if shift is None else row + shift

    deltas, radius = pool_deltas(coords, lambda c: own_rows[c : c + 1, :], code, lanes, depth)
    kinds = from_pool([pool[j, 7:8, :] for j in range(4)], code, lanes)
    inside = jnp.where(radius < cutoff, mask, 0.0)
    theta = omega * jnp.minimum(radius, cutoff)
    c1, s1 = jnp.cos(theta), jnp.sin(theta)
    ir = 1.0 / radius
    env = 0.5 * (c1 + 1.0) * inside
    e = env * ir
    e1 = ((-0.5 * omega) * s1 * inside - e) * ir
    e2 = ((-0.5 * omega * omega) * c1 * inside - 2.0 * e1) * ir
    unit = [d * ir for d in deltas]
    for name, value in (("e", e), ("e1", e1), ("e2", e2), ("ir", ir), ("t", kinds)):
        rows.put(save, name, value)
    for c in range(3):
        rows.put(save, "u%d" % c, unit[c])
    sin_at, cos_at = rows.at["sin"][0], rows.at["cos"][0]
    multiples(c1, s1, save.at[sin_at : sin_at + slots * USED, :], save.at[cos_at : cos_at + slots * USED, :], slots)

    def read_sin(k):
        return save[sin_at + k * USED : sin_at + (k + 1) * USED, :]

    def read_cos(k):
        return save[cos_at + k * USED : cos_at + (k + 1) * USED, :]

    coefs = [e] + [e * u for u in unit]
    mask_at = rows.at["mask"][0]

    def put_mask(i, value):
        save[mask_at + 8 * i : mask_at + 8 * i + 8, :] = value

    type_masks(kinds, types, put_mask)

    def read_mask(i):
        return save[mask_at + 8 * i : mask_at + 8 * i + 8, :]

    slot_sums(read_sin, read_cos, coefs, None, read_mask, slots, types, lambda q, v: rows.put(save, "A%d" % q, v))

    def nw(name):
        return narrow.get(nh, name), narrow.get(nl, name)

    def wd(name, first=None, last=None, rsl=slice(None)):
        return tuple(wide.get(r, name)[rsl, first:last] for r in (wh, wl))

    a0 = split(rows.get(save, "A0"))
    av = split(cat([rows.get(save, "A%d" % q) for q in (1, 2, 3)], 1))
    s_one = features[...] + dot3(wd("BT", rsl=slice(0, feat)), a0)
    v = dot3(wd("BT", rsl=slice(feat, 2 * feat)), av)
    uw = dot3(nw("RQT"), split(v))
    turned, mirrored = thirds(uw[0:feat]), thirds(uw[feat : 2 * feat])
    q = turned[0] * mirrored[0] + turned[1] * mirrored[1] + turned[2] * mirrored[2]
    n = jnp.sqrt(mirrored[0] * mirrored[0] + mirrored[1] * mirrored[1] + mirrored[2] * mirrored[2] + 1.0)
    joined = cat([s_one, n], 0)
    h = dot3(wd("CT"), split(joined))
    gate = lax.logistic(h)
    z = h * gate
    dz = gate * (1.0 + h * (1.0 - gate))
    d2z = gate * (1.0 - gate) * (2.0 + h * (1.0 - 2.0 * gate))
    a = dot3(nw("ST"), split(z))
    a2 = a[feat : 2 * feat]
    s_two = s_one + a[0:feat] + a2 * q
    y = dot3(nw("RT"), split(s_two))
    gate = lax.logistic(y)
    dy = gate * (1.0 + y * (1.0 - gate))
    d2y = gate * (1.0 - gate) * (2.0 + y * (1.0 - 2.0 * gate))
    ldy = dy * live
    yb = colmat[...] * ldy
    s2b = dot3(nw("R"), split(yb))
    ab = cat([s2b, s2b * q], 0)
    qb = s2b * a2
    zb = dot3(wd("S"), split(ab))
    hb = zb * dz
    jb = dot3(nw("C"), split(hb))
    s1b = s2b + jb[0:feat]
    nbn = jb[feat : 2 * feat] / n
    uwb = cat(
        [
            cat([qb * mirrored[c] for c in range(3)], 1),
            cat([nbn * mirrored[c] + qb * turned[c] for c in range(3)], 1),
        ],
        0,
    )
    vb = dot3(wd("RQ"), split(uwb))
    for name, value in (
        ("joined", joined), ("ab", ab), ("z", z), ("dz", dz), ("d2z", d2z), ("a2", a2), ("q", q), ("n", n),
        ("s2", s_two), ("yb", yb), ("yc", colmat[...] * live * d2y), ("ldy", ldy), ("s2b", s2b), ("zb", zb),
        ("hb", hb), ("qb", qb), ("nbn", nbn), ("s1b", s1b),
    ):
        rows.put(save, name, value)
    for name, value in (("v", v), ("uw", uw), ("uwb", uwb), ("vb", vb)):
        for c, part in enumerate(thirds(value)):
            rows.put(save, "%s%d" % (name, c), part)
    ab0 = dot3(wd("B", 0, feat), split(s1b))
    abv = thirds(dot3(wd("B", feat, 2 * feat), split(vb)))

    def put(name, q, k, row):
        start = rows.at["%s%d" % (name, q)][0] + k
        save[start : start + 1, :] = row

    tables = [ab0] + abv
    slot_reads(lambda q: tables[q], kinds, read_sin, read_cos, slots, types, put, True)
    sa = [rows.get(save, "sa%d" % q) for q in range(4)]
    sb = [rows.get(save, "sb%d" % q) for q in range(4)]
    z_sum = unit[0] * sa[1] + unit[1] * sa[2] + unit[2] * sa[3]
    x_sum = sb[0] + unit[0] * sb[1] + unit[1] * sb[2] + unit[2] * sb[3]
    rb = e * x_sum + e1 * (sa[0] + z_sum) - ir * e * z_sum
    deltas_bar = [rb * unit[c] + e * ir * sa[c + 1] for c in range(3)]
    pool_partials(deltas_bar, code, lambda j: index[slots + j : slots + j + 1, :], (near_out, far_out), groups, scratch, lanes)


def centres_of(bins, bin_total):
    return 0.1 * jnp.sqrt(3600.0 * (bins.astype(f32) + 0.5) / bin_total)


def hist_body(
    depth, bin_total, pool, near, far, from_near, from_far, index, masks, bins,
    next_own, slopes, hist, moved, scratch,
):
    lanes = pool.shape[2]
    slots = index.shape[0] - 8
    code = index[0:slots, :]
    inverse = index[slots + 4 : slots + 5, :]
    mask = masks[0:slots, :]
    for j in range(4):
        kick = (0.5 * time_step * time_step) * pool[j, 6:7, :]
        force = whole((near, far, from_near, from_far), j)
        moved[j, 0:3, :] = pool[j, 0:3, :] + time_step * pool[j, 3:6, :] - kick * force[0:3, :]
    inverse8 = jnp.broadcast_to(inverse, (8, lanes))
    own = []
    for c in range(3):
        row = from_pool([moved[j, c : c + 1, :] for j in range(4)], inverse8, lanes)[0:1, :]
        next_own[c : c + 1, :] = row
        own.append(row)

    def coords(j, c):
        shift = pool_offsets(j, lanes)[c]
        row = moved[j, c : c + 1, :]
        return row if shift is None else row + shift

    deltas, radius = pool_deltas(coords, lambda c: own[c], code, lanes, depth)
    gap = radius - centres_of(bins[...], bin_total)
    kernel = jnp.exp(-gap * gap / sigma_two) * mask
    scale = kernel * gap * (-2.0 / sigma_two) / radius
    for c in range(3):
        slopes[c * slots : (c + 1) * slots, :] = scale * deltas[c]
    sums = scatter_lanes([kernel], bins[...], scratch, bin_total)
    hist[...] = jnp.broadcast_to(sums[0:1, :], hist.shape)


def adjoint_body(atoms_total, hists, target, slopes, index, bins, near, far, groups, scratch):
    lanes = bins.shape[1]
    slots = bins.shape[0]
    code = index[0:slots, :]
    total = jnp.sum(hists[...], axis=0, keepdims=True)
    weights = 2.0 * (total / atoms_total - target[...]) / atoms_total
    picked = lane_take(weights, bins[...])
    deltas_bar = [picked * slopes[c * slots : (c + 1) * slots, :] for c in range(3)]
    pool_partials(deltas_bar, code, lambda j: index[slots + j : slots + j + 1, :], (near, far), groups, scratch, lanes)


def grads_body(
    types, pool, near, far, from_near, from_far, index, save, colmat, phi, filt, nh, nl, wh, wl,
    keep, send, adjoint, after, tangents, grads,
):
    lanes = pool.shape[2]
    slots = index.shape[0] - 8
    feat = colmat.shape[0]
    rows = saved_rows(feat, types, slots)
    narrow = narrow_rows(feat)
    wide = wide_rows(feat, types)
    code = index[0:slots, :]
    inverse8 = jnp.broadcast_to(index[slots + 4 : slots + 5, :], (8, lanes))

    def get(name):
        return rows.get(save, name)

    for j in range(4):
        adjoint[j, :, :] = whole((near, far, from_near, from_far), j)
    probe = [
        [(0.5 * time_step * time_step) * pool[j, 6:7, :] * adjoint[j, c : c + 1, :] for j in range(4)]
        for c in range(3)
    ]
    moves = [
        from_pool(probe[c], code, lanes) - from_pool(probe[c], inverse8, lanes)[0:1, :] for c in range(3)
    ]
    e, e1, e2, ir, kinds = get("e"), get("e1"), get("e2"), get("ir"), get("t")
    unit = [get("u%d" % c) for c in range(3)]
    dr = unit[0] * moves[0] + unit[1] * moves[1] + unit[2] * moves[2]
    du = [(moves[c] - unit[c] * dr) * ir for c in range(3)]
    de = e1 * dr
    sin_at, cos_at = rows.at["sin"][0], rows.at["cos"][0]

    def read_sin(k):
        return save[sin_at + k * USED : sin_at + (k + 1) * USED, :]

    def read_cos(k):
        return save[cos_at + k * USED : cos_at + (k + 1) * USED, :]

    k_rows = STRIDE * types

    def put_sum(q, value):
        tangents[q * k_rows : (q + 1) * k_rows, :] = value

    sin_coef = [de] + [de * unit[c] + e * du[c] for c in range(3)]
    cos_coef = [e * dr] + [e * dr * unit[c] for c in range(3)]
    mask_at = rows.at["mask"][0]

    def read_mask(i):
        return save[mask_at + 8 * i : mask_at + 8 * i + 8, :]

    slot_sums(read_sin, read_cos, sin_coef, cos_coef, read_mask, slots, types, put_sum)

    def nw(name):
        return narrow.get(nh, name), narrow.get(nl, name)

    def wd(name, first=None, last=None, rsl=slice(None)):
        return tuple(wide.get(r, name)[rsl, first:last] for r in (wh, wl))

    da_zero = tangents[0:k_rows, :]
    da_vec = cat([tangents[q * k_rows : (q + 1) * k_rows, :] for q in (1, 2, 3)], 1)
    ds1 = dot3(wd("BT", rsl=slice(0, feat)), split(da_zero))
    dv = dot3(wd("BT", rsl=slice(feat, 2 * feat)), split(da_vec))
    duw = dot3(nw("RQT"), split(dv))
    d_turn, d_mirr = thirds(duw[0:feat]), thirds(duw[feat : 2 * feat])
    turned = [get("uw%d" % c)[0:feat] for c in range(3)]
    mirrored = [get("uw%d" % c)[feat : 2 * feat] for c in range(3)]
    q, n, a2, dz, d2z = get("q"), get("n"), get("a2"), get("dz"), get("d2z")
    s2b, zb, qb, nbn = get("s2b"), get("zb"), get("qb"), get("nbn")
    dq = sum(d_turn[c] * mirrored[c] + turned[c] * d_mirr[c] for c in range(3))
    dn = sum(mirrored[c] * d_mirr[c] for c in range(3)) / n
    dj = cat([ds1, dn], 0)
    dh = dot3(wd("CT"), split(dj))
    dzt = dz * dh
    da = dot3(nw("ST"), split(dzt))
    da2 = da[feat : 2 * feat]
    ds2 = ds1 + da[0:feat] + da2 * q + a2 * dq
    dyt = dot3(nw("RT"), split(ds2))
    dyb = get("yc") * dyt
    ds2b = dot3(nw("R"), split(dyb))
    dab = cat([ds2b, ds2b * q + s2b * dq], 0)
    dqb = ds2b * a2 + s2b * da2
    dzb = dot3(wd("S"), split(dab))
    dhb = dzb * dz + zb * (d2z * dh)
    djb = dot3(nw("C"), split(dhb))
    ds1b = ds2b + djb[0:feat]
    dnbn = (djb[feat : 2 * feat] - nbn * dn) / n
    duwb = cat(
        [
            cat([dqb * mirrored[c] + qb * d_mirr[c] for c in range(3)], 1),
            cat(
                [
                    dnbn * mirrored[c] + nbn * d_mirr[c] + dqb * turned[c] + qb * d_turn[c]
                    for c in range(3)
                ],
                1,
            ),
        ],
        0,
    )
    dvb = dot3(wd("RQ"), split(duwb))

    def both(first, second, third, fourth):
        return -dot3(split(cat([first, second], 1)), split(cat([third, fourth], 1)), NT)

    parts = grads.shape[0]
    share = feat // parts
    rq = both(dv, triple(rows, save, "v"), triple(rows, save, "uwb"), duwb)
    cg = both(dj, get("joined"), get("hb"), dhb)
    sg = both(dzt, get("z"), get("ab"), dab)
    rg = both(ds2, get("s2"), get("yb"), dyb)
    bs = both(da_zero, get("A0"), get("s1b"), ds1b)
    bv = both(da_vec, cat([get("A%d" % i) for i in (1, 2, 3)], 1), triple(rows, save, "vb"), dvb)
    low, high = split(get("ldy") * dyt)
    ones = jnp.ones((16, lanes), bf16)
    col = -(dot1(ones, low, NT) + dot1(ones, high, NT))
    fg, pg = [], []
    for half, value in enumerate((bs, bv)):
        cols = slice(half * feat, (half + 1) * feat)
        total = None
        for t in range(types):
            block = value[STRIDE * t : STRIDE * t + USED, :]
            term = block * phi[t : t + 1, cols]
            total = term if total is None else total + term
            pg.append((half, t, jnp.sum(block * filt[0:USED, cols], axis=0, keepdims=True)))
        fg.append(total)
    base = 7 * share
    place = iota((10, lanes), 1)
    for part in range(parts):
        mine = slice(part * share, (part + 1) * share)
        grads[part, 0:share, :] = rq[mine, 0:feat]
        grads[part, share : 2 * share, :] = rq[mine, feat : 2 * feat]
        grads[part, 2 * share : 4 * share, :] = cg[2 * part * share : 2 * (part + 1) * share, :]
        grads[part, 4 * share : 5 * share, :] = sg[mine, 0:feat]
        grads[part, 5 * share : 6 * share, :] = sg[mine, feat : 2 * feat]
        grads[part, 6 * share : 7 * share, :] = rg[mine, :]
        for half, t, row in pg:
            at = base + half * types + t
            grads[part, at : at + 1, :] = row
        chosen = fg[part // 2]
        rolled = pltpu.roll(chosen, feat // 2, 1)
        here, there = (chosen, rolled) if part % 2 == 0 else (rolled, chosen)
        at = base + 2 * types
        grads[part, at : at + 10, :] = jnp.where(place < feat // 2, here[0:10, :], there[10:20, :])
        grads[part, at + 10 : at + 11, :] = col[0:1, :]
        grads[part, at + 11 :, :] = jnp.zeros((grads.shape[1] - at - 11, lanes), f32)

    odd = lax.axis_index("slab") % 2
    half = grads.shape[1] // 2
    keep[...] = grads[:, pl.ds(pl.multiple_of(odd * half, half), half), :]
    send[...] = grads[:, pl.ds(pl.multiple_of((1 - odd) * half, half), half), :]
    for c in range(3):
        after[c * slots : (c + 1) * slots, :] = du[c]
        after[4 * slots + (c + 1) * feat : 4 * slots + (c + 2) * feat, :] = dvb[:, c * lanes : (c + 1) * lanes]
    after[3 * slots : 4 * slots, :] = dr
    after[4 * slots : 4 * slots + feat, :] = ds1b


def moves_body(types, index, save, after, wh, wl, near, far, sums, groups, scratch):
    lanes = index.shape[1]
    slots = index.shape[0] - 8
    feat = lanes
    rows = saved_rows(feat, types, slots)
    wide = wide_rows(feat, types)
    code = index[0:slots, :]

    def get(name):
        return rows.get(save, name)

    def wd(name, first, last):
        return tuple(wide.get(r, name)[:, first:last] for r in (wh, wl))

    e, e1, e2, ir, kinds = get("e"), get("e1"), get("e2"), get("ir"), get("t")
    unit = [get("u%d" % c) for c in range(3)]
    du = [after[c * slots : (c + 1) * slots, :] for c in range(3)]
    dr = after[3 * slots : 4 * slots, :]
    de, de1, dir_ = e1 * dr, e2 * dr, -ir * ir * dr
    sin_at, cos_at = rows.at["sin"][0], rows.at["cos"][0]

    def read_sin(k):
        return save[sin_at + k * USED : sin_at + (k + 1) * USED, :]

    def read_cos(k):
        return save[cos_at + k * USED : cos_at + (k + 1) * USED, :]

    ds1b = after[4 * slots : 4 * slots + feat, :]
    dvb = cat([after[4 * slots + (c + 1) * feat : 4 * slots + (c + 2) * feat, :] for c in range(3)], 1)
    dab0 = dot3(wd("B", 0, feat), split(ds1b))
    dabv = thirds(dot3(wd("B", feat, 2 * feat), split(dvb)))
    tables = [dab0] + dabv

    def put(name, q, k, row):
        start = (0 if name == "sa" else 4 * slots) + q * slots + k
        sums[start : start + 1, :] = row

    slot_reads(lambda q: tables[q], kinds, read_sin, read_cos, slots, types, put, False)
    sa = [get("sa%d" % q) for q in range(4)]
    sb = [get("sb%d" % q) for q in range(4)]
    sd = [get("sd%d" % q) for q in range(4)]
    dsa = [sb[q] * dr + sums[q * slots : (q + 1) * slots, :] for q in range(4)]
    dsb = [
        sums[(4 + q) * slots : (5 + q) * slots, :] - sd[q] * dr for q in range(4)
    ]
    z_sum = sum(unit[c] * sa[c + 1] for c in range(3))
    x_sum = sb[0] + sum(unit[c] * sb[c + 1] for c in range(3))
    dz_sum = sum(du[c] * sa[c + 1] + unit[c] * dsa[c + 1] for c in range(3))
    dx_sum = dsb[0] + sum(du[c] * sb[c + 1] + unit[c] * dsb[c + 1] for c in range(3))
    rb = e * x_sum + e1 * (sa[0] + z_sum) - ir * e * z_sum
    drb = (
        de * x_sum + e * dx_sum + de1 * (sa[0] + z_sum) + e1 * (dsa[0] + dz_sum)
        - (dir_ * e + ir * de) * z_sum - ir * e * dz_sum
    )
    deltas_bar = [
        drb * unit[c] + rb * du[c] + (de * ir + e * dir_) * sa[c + 1] + e * ir * dsa[c + 1]
        for c in range(3)
    ]
    pool_partials(deltas_bar, code, lambda j: index[slots + j : slots + j + 1, :], (near, far), groups, scratch, lanes)


def last_body(
    types, parts, atoms_total, mine, other, adjoint, near, far, index, slope, hidden_t, table_t, spreader, next_own,
    next_out, adj, enc, spr, fil, rot, ref, com, spl, rea, col, total,
):
    next_out[...] = next_own[...]
    odd = lax.axis_index("slab") % 2
    half = mine.shape[0]
    total[pl.ds(pl.multiple_of(odd * half, half), half), :] = mine[...]
    total[pl.ds(pl.multiple_of((1 - odd) * half, half), half), :] = other[...]
    lanes = adjoint.shape[2]
    slots = index.shape[0] - 8
    feat = lanes
    share = feat // parts
    inverse8 = jnp.broadcast_to(index[slots + 4 : slots + 5, :], (8, lanes))
    crossed = parity("cross")
    near_v, far_v = near[...], far[...]
    second = (jnp.where(crossed, near_v, far_v), jnp.where(crossed, far_v, near_v))
    for c in range(3):
        rows = [
            atoms_total * (adjoint[j, c : c + 1, :] - second[j % 2][j // 2, c : c + 1, :]) for j in range(4)
        ]
        adj[c : c + 1, :] = from_pool(rows, inverse8, lanes)[0:1, :]
    rot[...] = total[0:share, :]
    ref[...] = total[share : 2 * share, :]
    com[...] = total[2 * share : 4 * share, :]
    spl[:, 0:feat] = total[4 * share : 5 * share, :]
    spl[:, feat : 2 * feat] = total[5 * share : 6 * share, :]
    rea[...] = total[6 * share : 7 * share, :]
    base = 7 * share
    phib = cat([total[base : base + types, :], total[base + types : base + 2 * types, :]], 1)
    at = base + 2 * types
    block = total[at : at + 10, :]
    fil[0:10, :] = block[:, 0 : feat // 2]
    fil[10:20, :] = pltpu.roll(block, feat // 2, 1)[:, 0 : feat // 2]
    col_row = total[at + 10 : at + 11, :]
    spare = jnp.zeros((types, 2 * feat), f32)
    pre_bar = dot3(split(cat([phib, spare], 0)), split(spreader[...]), NT)[0:types] * slope[...]
    here = pl.ds(pl.multiple_of(lax.axis_index("cross") * share, share), share)
    rest = jnp.zeros((lanes - types, feat), f32)
    spr[...] = dot3(split(hidden_t[here, :]), split(cat([phib, cat([rest, rest], 1)], 0)))
    enc[...] = dot3(split(table_t[here, :]), split(cat([pre_bar, rest], 0)))
    for part in range(parts):
        @pl.when(lax.axis_index("cross") == part)
        def _():
            col[...] = col_row[:, part * share : (part + 1) * share]


def neighbours_swap(near, far, axis):
    count = lax.axis_size(axis)
    forward = [(i, (i + 1) % count) for i in range(count)]
    pairs = [[p for a, b in forward if a % 2 == side for p in ((a, b), (b, a))] for side in (0, 1)]
    from_far = lax.ppermute(far, axis, pairs[1])
    from_near = lax.ppermute(near, axis, pairs[0])
    return from_near, from_far


def corner_sum(near, far):
    near, far = call(turn_body, [(near.shape, f32)] * 2, near, far, *neighbours_swap(near, far, "slab"))
    return (near, far) + neighbours_swap(near, far, "cross")


def swap(x, axis, bit):
    return lax.ppermute(x, axis, [(i, i ^ bit) for i in range(lax.axis_size(axis))])


def halve(bit, x, other, keep, send):
    mine = (lax.axis_index("cross") // bit) % 2
    shape = (x.shape[0] // 2, 2) + x.shape[1:]
    x, other = x.reshape(shape), other.reshape(shape)
    for ref, side in ((keep, mine), (send, 1 - mine)):
        value = x[:, pl.ds(side, 1)] + other[:, pl.ds(side, 1)]
        ref[...] = value.reshape(ref.shape)


def halve_hold_body(bit, x, other, near, far, keep, send, near_out, far_out):
    halve(bit, x, other, keep, send)
    near_out[...] = near[...]
    far_out[...] = far[...]


def halve_turn_body(bit, x, other, near, far, from_near, from_far, keep, send, near_out, far_out):
    halve(bit, x, other, keep, send)
    turn_body(near, far, from_near, from_far, near_out, far_out)


def add_body(x, other, out):
    out[...] = x[...] + other[...]


def add_sides_body(x, other, near, far, from_near, from_far, out, near_out, far_out):
    add_body(x, other, out)
    add_body(near, from_near, near_out)
    add_body(far, from_far, far_out)


def add_all_body(*refs):
    total = refs[0][...]
    for ref in refs[1:-1]:
        total = total + ref[...]
    refs[-1][...] = total


def reduce_all(keep, send, near, far):
    slab_count, cross_count = lax.axis_size("slab"), lax.axis_size("cross")
    group = (near.shape, f32)
    other = swap(send, "slab", 1)
    bit, step, received = 1, 0, None
    while bit < cross_count:
        half = ((keep.shape[0] // 2,) + keep.shape[1:], f32)
        if step == 0:
            keep, send, near, far = call(
                functools.partial(halve_hold_body, bit), [half, half, group, group], keep, other, near, far
            )
            received = neighbours_swap(near, far, "slab")
        elif step == 1:
            keep, send, near, far = call(
                functools.partial(halve_turn_body, bit), [half, half, group, group],
                keep, other, near, far, *received,
            )
            received = neighbours_swap(near, far, "cross")
        else:
            raise NotImplementedError
        other = swap(send, "cross", bit)
        bit, step = 2 * bit, step + 1
    x, other = keep[0], other[0]
    x, *sides = call(add_sides_body, [(x.shape, f32), group, group], x, other, near, far, *received)
    bits = [2**b for b in range(1, slab_count.bit_length()) if 2**b < slab_count]
    for i in range(0, len(bits), 2):
        pair = bits[i : i + 2]
        steps = pair + [sum(pair)] * (len(pair) - 1)
        (x,) = call(add_all_body, [(x.shape, f32)], x, *[swap(x, "slab", step) for step in steps])
    return x, swap(x, "slab", 1), sides


def device_step(
    positions, velocities, inverse_mass, species, type_table, neighbours, slot_count, atom_count,
    pair_bins, send_list, target, encoder, spreader, filters, rotator, reflector, combiner, splitter,
    readout, collector,
):
    lanes = positions.shape[1]
    slots = neighbours.shape[1]
    types, feat = type_table.shape
    bin_total = target.shape[0]
    slab_count, cross_count = lax.axis_size("slab"), lax.axis_size("cross")
    devices = slab_count * cross_count
    atoms_total = float(lanes * devices)
    depth = 1.6 * (lanes // 16)
    parts = cross_count
    row = lambda x: x.reshape(1, x.shape[0])
    i32 = jnp.int32
    vm, dma = pltpu.VMEM, pltpu.SemaphoreType.DMA
    narrow, wide = narrow_rows(feat).total, wide_rows(feat, types).total
    group = ((2, 8, lanes), f32)
    pool_shape = ((4, 8, lanes), f32)
    pair_scratch = vm((16 * slots, lanes), f32)
    near, far, own_rows, send = call(
        offer_body, [group, group, ((8, lanes), f32), ((8, lanes), i32)],
        *in_hbm(positions, velocities, row(inverse_mass), row(species), send_list),
        specs=[HB] * 5,
        scratch=[
            vm((3, lanes), f32), vm((3, lanes), f32), vm((1, lanes), f32), vm((1, lanes), i32),
            vm(send_list.shape, i32), vm((4, 8, lanes), f32), dma((5,)),
        ],
    )
    colmat, nh, nl, wh, wl, phi, slope, hidden_t, table_t, filt, spreader_in = call(
        weights_body,
        [
            ((feat, lanes), f32), ((narrow, feat), bf16), ((narrow, feat), bf16), ((wide, 2 * feat), bf16),
            ((wide, 2 * feat), bf16), ((types, 2 * feat), f32), ((types, feat), f32), ((feat, lanes), f32),
            ((feat, lanes), f32), ((STRIDE, 2 * feat), f32), (spreader.shape, f32),
        ],
        *in_hbm(
            type_table, encoder, spreader, filters, rotator, reflector, combiner, splitter, readout,
            row(collector),
        ),
        specs=[HB] * 10,
        scratch=[
            vm(type_table.shape, f32), vm(encoder.shape, f32), vm(filters.shape, f32), vm(rotator.shape, f32),
            vm(reflector.shape, f32), vm(combiner.shape, f32), vm(splitter.shape, f32), vm(readout.shape, f32),
            vm((1, feat), f32), dma((10,)),
        ],
    )
    index, masks, features, bins, goal = call(
        index_body,
        [
            ((slots + 8, lanes), i32), ((slots + 8, lanes), f32), ((feat, lanes), f32), ((slots, lanes), i32),
            ((1, bin_total), f32),
        ],
        *in_hbm(neighbours.T, row(slot_count), pair_bins.T, row(target)),
        atom_count, send, own_rows, table_t,
        specs=[HB] * 4 + [SM] + [VM] * 3,
        scratch=[vm((slots, lanes), i32), vm((1, lanes), i32), dma((4,))],
    )
    pieces = corner_sum(near, far)
    save_rows = saved_rows(feat, types, slots).total
    near, far, pool, save = call(
        functools.partial(force_body, types, depth),
        [group, group, pool_shape, ((save_rows, lanes), f32)],
        *pieces, own_rows, index, masks, features, colmat, nh, nl, wh, wl,
        scratch=[vm((4, 8, lanes), f32), pair_scratch],
    )
    pieces = corner_sum(near, far)
    next_positions, slopes, hist = call(
        functools.partial(hist_body, depth, bin_total),
        [((3, lanes), f32), ((3 * slots, lanes), f32), ((devices, bin_total), f32)],
        pool, *pieces, index, masks, bins,
        scratch=[vm((4, 8, lanes), f32), pair_scratch],
    )
    hists = lax.all_to_all(hist.reshape(devices, 1, bin_total), ("slab", "cross"), 0, 0)
    near, far = call(
        functools.partial(adjoint_body, atoms_total), [group, group],
        hists.reshape(devices, bin_total), goal, slopes, index, bins,
        scratch=[vm((4, 8, lanes), f32), pair_scratch],
    )
    pieces = corner_sum(near, far)
    half_grads = ((parts, feat, lanes), f32)
    keep, send, adjoint, after = call(
        functools.partial(grads_body, types),
        [half_grads, half_grads, pool_shape, ((4 * slots + 4 * feat, lanes), f32)],
        pool, *pieces, index, save, colmat, phi, filt, nh, nl, wh, wl,
        scratch=[vm((4 * STRIDE * types, lanes), f32), vm((parts, 2 * feat, lanes), f32)],
    )
    near, far = call(
        functools.partial(moves_body, types), [group, group], index, save, after, wh, wl,
        scratch=[vm((8 * slots, lanes), f32), vm((4, 8, lanes), f32), pair_scratch],
    )
    mine, other, sides = reduce_all(keep, send, near, far)
    share = feat // parts
    results = call(
        functools.partial(last_body, types, parts, atoms_total),
        [
            ((3, lanes), f32), ((3, lanes), f32), ((share, feat), f32), ((share, 2 * feat), f32),
            ((filters.shape[0], 2 * feat // parts), f32), ((share, feat), f32), ((share, feat), f32),
            ((2 * share, feat), f32), ((share, 2 * feat), f32), ((share, feat), f32), ((1, share), f32),
        ],
        mine, other, adjoint, *sides, index, slope, hidden_t, table_t, spreader_in, next_positions,
        scratch=[vm((2 * feat, lanes), f32)],
        keep=False,
    )
    return tuple(results[:10]) + (results[10].reshape(share),)


def solution(mesh):
    both = ("slab", "cross")
    in_specs = (
        P(None, both), P(None, both), P(both), P(both), P(), P(both, None), P(both), P(both), P(both, None),
        P("slab", "cross", None),
    ) + (P(),) * 10
    out_specs = (
        P(None, both), P(None, both), P("cross", None), P("cross", None), P(None, "cross"), P("cross", None),
        P("cross", None), P("cross", None), P("cross", None), P("cross", None), P("cross"),
    )
    return jax.shard_map(device_step, mesh=mesh, in_specs=in_specs, out_specs=out_specs, check_vma=False)
```

```python
import functools

import jax
import jax.numpy as jnp
from jax import lax
from jax.experimental import pallas as pl
from jax.experimental.pallas import tpu as pltpu
from jax.sharding import PartitionSpec as P


cutoff = 5.0
soften = 0.25
sigma_two = 0.18
slab_length = 10.0
cell_length = 10.0
time_step = 0.5
highest = lax.Precision.HIGHEST
f32 = jnp.float32
bf16 = jnp.bfloat16
pi = 3.141592653589793
omega = pi / cutoff

NN = ((1,), (0,))
NT = ((1,), (1,))
VM = pl.BlockSpec(memory_space=pltpu.VMEM)
SM = pl.BlockSpec(memory_space=pltpu.SMEM)
HB = pl.BlockSpec(memory_space=pltpu.HBM)


def call(body, outs, *args, specs=None, scratch=(), keep=True):
    return pl.pallas_call(
        body,
        out_shape=[(pltpu.VMEM if keep else jax.ShapeDtypeStruct)(s, d) for s, d in outs],
        in_specs=[VM] * len(args) if specs is None else specs,
        out_specs=[VM] * len(outs),
        scratch_shapes=list(scratch),
        compiler_params=pltpu.CompilerParams(vmem_limit_bytes=16 * 2**20),
    )(*args)


def in_hbm(*arrays):
    return [pltpu.with_memory_space_constraint(x, pltpu.HBM) for x in arrays]


def fetch(sources, targets, semaphores):
    copies = [
        pltpu.make_async_copy(source, target, semaphores.at[i])
        for i, (source, target) in enumerate(zip(sources, targets))
    ]
    for copy in copies:
        copy.start()
    for copy in copies:
        copy.wait()


def split(x):
    high = x.astype(bf16)
    return high, (x - high.astype(f32)).astype(bf16)


def dot1(a, b, dims):
    return lax.dot_general(a, b, (dims, ((), ())), preferred_element_type=f32)


def dot3(a, b, dims=NN):
    return dot1(
        jnp.concatenate([a[0], a[0], a[1]], dims[0][0]), jnp.concatenate([b[0], b[1], b[0]], dims[1][0]), dims
    )


def cat(parts, axis):
    return jnp.concatenate(parts, axis=axis)


def iota(shape, dim):
    return lax.broadcasted_iota(jnp.int32, shape, dim)


def lane_take(row, index):
    return jnp.take_along_axis(jnp.broadcast_to(row, index.shape), index, axis=1)


def own_lanes(group, lanes):
    quarter = lanes // 4
    start = 2 * quarter * (1 - group // 2) + quarter * (1 - group % 2)
    return start, quarter


def pool_offsets(group, lanes):
    place = iota((1, lanes), 1)
    up, right = group // 2, group % 2
    half, quarter = lanes // 2, lanes // 4
    first = (place >= half) if up else (place < half)
    second_bit = place % half >= quarter
    second = second_bit if right else jnp.logical_not(second_bit)
    sign_u, sign_r = 2.0 * up - 1.0, 2.0 * right - 1.0
    return (
        jnp.where(first, sign_u * slab_length, 0.0).astype(f32),
        jnp.where(second, sign_r * cell_length, 0.0).astype(f32),
        None,
    )


def from_pool(rows, code, lanes):
    group = code // lanes
    lane = code % lanes
    out = lane_take(rows[0], lane)
    for j in range(1, 4):
        out = jnp.where(group == j, lane_take(rows[j], lane), out)
    return out


def pool_deltas(pool_rows, own_rows, code, lanes, depth):
    deltas = []
    for c in range(3):
        d = from_pool([pool_rows(j, c) for j in range(4)], code, lanes) - own_rows(c)
        if c == 2:
            d = d - depth * jnp.floor(d / depth + 0.5)
        deltas.append(d)
    radius = jnp.sqrt(deltas[0] * deltas[0] + deltas[1] * deltas[1] + deltas[2] * deltas[2] + soften)
    return deltas, radius


def one_hot_rows(index, slots, count):
    lanes = index.shape[1]
    place = iota((count, lanes), 0)
    return cat(
        [(place == index[k : k + 1, :]).astype(f32).astype(bf16) for k in range(slots)], 1
    )


def scatter_lanes(values, index, scratch, count):
    shape = index.shape
    slots = shape[0]
    for row in range(16):
        value = values[row] if row < len(values) else None
        if value is None:
            value = jnp.zeros(shape, f32)
        scratch[pl.ds(row, slots, stride=16), :] = value
    highs, mids, lows = [], [], []
    for k in range(slots):
        x = scratch[16 * k : 16 * k + 16, :]
        high = x.astype(bf16)
        rest = x - high.astype(f32)
        mid = rest.astype(bf16)
        highs.append(high)
        mids.append(mid)
        lows.append((rest - mid.astype(f32)).astype(bf16))
    left = cat([cat(highs, 1), cat(mids, 1), cat(lows, 1)], 0)
    sums = dot1(left, one_hot_rows(index, slots, count), NT)
    return sums[0:16] + (sums[16:32] + sums[32:48])


def pool_partials(deltas_bar, code, send_index, outs, groups, scratch, lanes):
    group = code // lanes
    values = []
    for j in range(4):
        for c in range(3):
            values.append(jnp.where(group == j, deltas_bar[c], 0.0))
        values.append(None)
    sums = scatter_lanes(values, code % lanes, scratch, lanes)
    centres = [-jnp.sum(d, axis=0, keepdims=True) for d in deltas_bar]
    place = iota((1, lanes), 1)
    for j in range(4):
        start, width = own_lanes(j, lanes)
        own = jnp.logical_and(place >= start, place < start + width)
        groups[j, :, :] = jnp.zeros((8, lanes), f32)
        for c in range(3):
            mine = lane_take(jnp.broadcast_to(centres[c], (8, lanes)), jnp.broadcast_to(send_index(j), (8, lanes)))
            groups[j, c : c + 1, :] = sums[4 * j + c : 4 * j + c + 1, :] + jnp.where(
                own, mine[0:1, :], 0.0
            )
    by_side(groups[...], *outs)


def offer_body(
    pos, vel, mass, species, send_list, near, far, own_out, send_out,
    pos_v, vel_v, mass_v, species_v, list_v, groups, semaphores,
):
    fetch((pos, vel, mass, species, send_list), (pos_v, vel_v, mass_v, species_v, list_v), semaphores)
    lanes = pos.shape[1]
    own_out[0:3, :] = pos_v[...]
    own_out[3:6, :] = vel_v[...]
    own_out[6:7, :] = mass_v[...]
    own_out[7:8, :] = species_v[...].astype(f32)
    own_rows = own_out[...]
    place = iota((8, lanes), 1)
    send_out[...] = jnp.zeros((8, lanes), jnp.int32)
    for j in range(4):
        start, width = own_lanes(j, lanes)
        pieces = [list_v[j // 2, j % 2 : j % 2 + 1, :]]
        if start:
            pieces = [jnp.zeros((1, start), jnp.int32)] + pieces
        if start + width < lanes:
            pieces = pieces + [jnp.zeros((1, lanes - start - width), jnp.int32)]
        row = cat(pieces, 1)
        send_out[j : j + 1, :] = row
        own = jnp.logical_and(place >= start, place < start + width)
        taken = jnp.take_along_axis(own_rows, jnp.broadcast_to(row, (8, lanes)), axis=1)
        groups[j, :, :] = jnp.where(own, taken, 0.0)
    by_side(groups[...], near, far)


def parity(axis):
    return lax.axis_index(axis) % 2 == 1


def by_side(groups, near, far):
    odd = parity("slab")
    low, high = groups[0:2], groups[2:4]
    near[...] = jnp.where(odd, low, high)
    far[...] = jnp.where(odd, high, low)


def turn_body(near, far, from_near, from_far, near_out, far_out):
    odd = parity("slab")
    near_sum, far_sum = near[...] + from_near[...], far[...] + from_far[...]
    low, high = jnp.where(odd, near_sum, far_sum), jnp.where(odd, far_sum, near_sum)
    odd = parity("cross")
    for u, part in enumerate((low, high)):
        near_out[u, :, :] = jnp.where(odd, part[0], part[1])
        far_out[u, :, :] = jnp.where(odd, part[1], part[0])


def whole(pieces, j):
    u = j // 2
    near_sum, far_sum = pieces[0][u] + pieces[2][u], pieces[1][u] + pieces[3][u]
    odd = parity("cross")
    return jnp.where(odd, far_sum, near_sum) if j % 2 else jnp.where(odd, near_sum, far_sum)


class Rows:
    def __init__(self, sizes):
        self.at = {}
        self.total = 0
        for name, size in sizes:
            self.at[name] = (self.total, size)
            self.total += size

    def get(self, ref, name):
        start, size = self.at[name]
        return ref[start : start + size, :]

    def put(self, ref, name, value):
        start, size = self.at[name]
        ref[start : start + size, :] = value


STRIDE = 32
USED = 24


def narrow_rows(feat):
    return Rows((("RQT", 2 * feat), ("C", 2 * feat), ("ST", 2 * feat), ("RT", feat), ("R", feat)))


def wide_rows(feat, types):
    return Rows((("BT", 2 * feat), ("B", STRIDE * types), ("RQ", feat), ("CT", feat), ("S", feat)))


def weights_body(
    table_h, encoder_h, spreader_h, filters_h, rotator_h, reflector_h, combiner_h, splitter_h, readout_h,
    collector_h, col_out, nh, nl, wh, wl, phi_out, slope_out, hidden_t, table_t, filt_out, spreader,
    table, encoder, filters, rotator, reflector, combiner, splitter, readout, collector, semaphores,
):
    fetch(
        (table_h, encoder_h, spreader_h, filters_h, rotator_h, reflector_h, combiner_h, splitter_h, readout_h,
         collector_h),
        (table, encoder, spreader, filters, rotator, reflector, combiner, splitter, readout, collector),
        semaphores,
    )
    types, feat = table.shape
    lanes = hidden_t.shape[1]
    basis = filters.shape[0]
    pre = jnp.dot(table[...], encoder[...], precision=highest, preferred_element_type=f32)
    gate = lax.logistic(pre)
    hidden = pre * gate
    phi = jnp.dot(hidden, spreader[...], precision=highest, preferred_element_type=f32)
    phi_out[...] = phi
    slope_out[...] = gate * (1.0 + pre * (1.0 - gate))
    rest = [jnp.zeros((lanes - types, feat), f32)]
    hidden_t[...] = jnp.transpose(cat([hidden] + rest, 0))
    table_t[...] = jnp.transpose(cat([table[...]] + rest, 0))
    filt_out[...] = jnp.zeros(filt_out.shape, f32)
    filt_out[0:basis, :] = filters[...]
    filt = filt_out[...]
    col_out[...] = jnp.transpose(jnp.broadcast_to(collector[...], (lanes, feat)))
    narrow = narrow_rows(feat)
    wide = wide_rows(feat, types)

    def put(rows, high_ref, low_ref, name, value, row=0, col=0):
        high, low = split(value)
        start = rows.at[name][0] + row
        high_ref[start : start + value.shape[0], col : col + value.shape[1]] = high
        low_ref[start : start + value.shape[0], col : col + value.shape[1]] = low

    per_half = feat // STRIDE
    for half in range(2):
        cols = slice(half * feat, (half + 1) * feat)
        for chunk in range(types // per_half):
            block = cat(
                [
                    filt[:, cols] * phi[t : t + 1, cols]
                    for t in range(chunk * per_half, (chunk + 1) * per_half)
                ],
                0,
            )
            put(wide, wh, wl, "B", block, chunk * feat, half * feat)
            put(wide, wh, wl, "BT", jnp.transpose(block), half * feat, chunk * feat)
    put(wide, wh, wl, "RQ", rotator[...], 0, 0)
    put(wide, wh, wl, "RQ", reflector[...], 0, feat)
    put(narrow, nh, nl, "RQT", jnp.transpose(rotator[...]), 0)
    put(narrow, nh, nl, "RQT", jnp.transpose(reflector[...]), feat)
    put(narrow, nh, nl, "C", combiner[...])
    put(wide, wh, wl, "CT", jnp.transpose(combiner[0:feat, :]), 0, 0)
    put(wide, wh, wl, "CT", jnp.transpose(combiner[feat : 2 * feat, :]), 0, feat)
    put(wide, wh, wl, "S", splitter[...])
    put(narrow, nh, nl, "ST", jnp.transpose(splitter[:, 0:feat]), 0)
    put(narrow, nh, nl, "ST", jnp.transpose(splitter[:, feat : 2 * feat]), feat)
    put(narrow, nh, nl, "R", readout[...])
    put(narrow, nh, nl, "RT", jnp.transpose(readout[...]))


def index_body(
    near_h, count_h, bins_h, target_h, atom_count, send, own_rows, table_t,
    index, masks, feat_out, bins, target, near, slot_count, semaphores,
):
    fetch((near_h, count_h, bins_h, target_h), (near, slot_count, bins, target), semaphores)
    species = own_rows[7:8, :].astype(jnp.int32)
    slots, lanes = near.shape
    quarter = lanes // 4
    lane_row = iota((16, lanes), 1).astype(f32)
    row_id = iota((16, lanes), 0)
    lefts, rights = [], []
    place = iota((lanes, lanes), 1)
    for j in range(4):
        start, width = own_lanes(j, lanes)
        own = jnp.logical_and(place >= start, place < start + width)
        same = jnp.logical_and(own, iota((lanes, lanes), 0) == send[j : j + 1, :])
        rights.append(same.astype(f32).astype(bf16))
        lefts.append(
            jnp.where(row_id == 0, lane_row, jnp.where(row_id == 1, float(j), 0.0)).astype(bf16)
        )
    found = dot1(cat(lefts, 1), cat(rights, 1), NT)
    inverse = (found[0:1, :] + lanes * found[1:2, :] + 0.5).astype(jnp.int32)
    near_v = near[...]
    ghost = near_v - lanes
    block = ghost // quarter
    p, q, g = block // 4, block % 4, ghost % quarter
    ghost_code = (2 * (p // 2) + q // 2) * lanes + 2 * quarter * (p % 2) + quarter * (q % 2) + g
    own_code = lane_take(inverse, jnp.minimum(near_v, lanes - 1))
    index[...] = jnp.zeros(index.shape, jnp.int32)
    index[0:slots, :] = jnp.where(near_v < lanes, own_code, ghost_code)
    index[slots : slots + 4, :] = send[0:4, :]
    index[slots + 4 : slots + 5, :] = inverse
    masks[...] = jnp.zeros(masks.shape, f32)
    masks[0:slots, :] = (iota((slots, lanes), 0) < slot_count[...]).astype(f32)
    masks[slots : slots + 1, :] = (iota((1, lanes), 1) < atom_count[0]).astype(f32)
    feat_out[...] = jnp.take_along_axis(table_t[...], jnp.broadcast_to(species, table_t.shape), axis=1)


def saved_rows(feat, types, slots):
    k = STRIDE * types
    pair = ("e", "e1", "e2", "ir", "u0", "u1", "u2", "t")
    sizes = [("A%d" % q, k) for q in range(4)]
    sizes += [("%s%d" % (n, c), feat) for n in ("v", "vb") for c in range(3)]
    sizes += [("%s%d" % (n, c), 2 * feat) for n in ("uw", "uwb") for c in range(3)]
    sizes += [("joined", 2 * feat), ("ab", 2 * feat)]
    sizes += [
        (n, feat)
        for n in ("z", "dz", "d2z", "a2", "q", "n", "s2", "yb", "yc", "ldy", "s2b", "zb", "hb", "qb", "nbn", "s1b")
    ]
    sizes += [("sin", slots * USED), ("cos", slots * USED), ("mask", 8 * slots * types)]
    sizes += [(n, slots) for n in pair]
    sizes += [("%s%d" % (n, q), slots) for n in ("sa", "sb", "sd") for q in range(4)]
    return Rows(sizes)


def multiples(c1, s1, sin_ref, cos_ref, slots):
    lanes = c1.shape[1]
    powers = [(c1, s1)]
    for _ in range(4):
        c, s = powers[-1]
        powers.append((c * c - s * s, 2.0 * c * s))
    sub = iota((8, lanes), 0)
    bits = [(sub // 2**b) % 2 == 1 for b in range(3)]
    order = sub.astype(f32) + 1.0

    def times(x, y):
        return x[0] * y[0] - x[1] * y[1], x[0] * y[1] + x[1] * y[0]

    for k in range(slots):
        rows = [
            tuple(jnp.broadcast_to(part[k : k + 1, :], (8, lanes)) for part in power)
            for power in powers
        ]
        z = rows[0]
        for b in range(3):
            step = (jnp.where(bits[b], rows[b][0], 1.0), jnp.where(bits[b], rows[b][1], 0.0))
            z = times(z, step)
        for v in range(3):
            if v == 1:
                zv = times(z, rows[3])
            elif v == 2:
                zv = times(z, rows[4])
            else:
                zv = z
            start = k * USED + 8 * v
            sin_ref[start : start + 8, :] = zv[1]
            cos_ref[start : start + 8, :] = zv[0] * ((order + 8.0 * v) * omega)


def type_masks(kinds, types, put):
    slots, lanes = kinds.shape
    for k in range(slots):
        kind = jnp.broadcast_to(kinds[k : k + 1, :], (8, lanes))
        for t in range(types):
            put(k * types + t, jnp.where(kind == t, 1.0, 0.0))


def choose(options, bits):
    for bit in bits:
        options = [
            jnp.where(bit, options[i + 1], options[i]) if i + 1 < len(options) else options[i]
            for i in range(0, len(options), 2)
        ]
    return options[0]


def slot_sums(read_sin, read_cos, sin_coef, cos_coef, read_mask, slots, types, put):
    lanes = sin_coef[0].shape[1]
    tiles = USED // 8
    for q in range(4):
        sums = [[None] * tiles for _ in range(types)]
        for k in range(slots):
            value = read_sin(k) * sin_coef[q][k : k + 1, :]
            if cos_coef is not None:
                value = value + read_cos(k) * cos_coef[q][k : k + 1, :]
            for t in range(types):
                mask = read_mask(k * types + t)
                for v in range(tiles):
                    part = value[8 * v : 8 * v + 8] * mask
                    sums[t][v] = part if sums[t][v] is None else sums[t][v] + part
        rest = jnp.zeros((STRIDE - USED, lanes), f32)
        put(q, cat([x for t in range(types) for x in sums[t] + [rest]], 0))


def slot_reads(values, kinds, read_sin, read_cos, slots, types, put, with_square):
    lanes = kinds.shape[1]
    tiles = USED // 8
    whole_kinds = (kinds + 0.5).astype(jnp.int32)
    kind_bits = [((whole_kinds // 2**b) % 2).astype(f32) for b in range((types - 1).bit_length())]
    square = [((iota((8, lanes), 0).astype(f32) + (8.0 * v + 1.0)) * omega) ** 2 for v in range(tiles)]
    for q in range(4):
        value = values(q)
        tables = [
            [value[STRIDE * t + 8 * v : STRIDE * t + 8 * v + 8] for v in range(tiles)] for t in range(types)
        ]
        for k in range(slots):
            bits = [jnp.broadcast_to(part[k : k + 1, :], (8, lanes)) > 0.5 for part in kind_bits]
            picked = [choose([table[v] for table in tables], bits) for v in range(tiles)]
            sines, cosines = read_sin(k), read_cos(k)
            with_sin = [sines[8 * v : 8 * v + 8] * picked[v] for v in range(tiles)]
            put("sa", q, k, jnp.sum(sum(with_sin), axis=0, keepdims=True))
            with_cos = [cosines[8 * v : 8 * v + 8] * picked[v] for v in range(tiles)]
            put("sb", q, k, jnp.sum(sum(with_cos), axis=0, keepdims=True))
            if with_square:
                with_sin = [with_sin[v] * square[v] for v in range(tiles)]
                put("sd", q, k, jnp.sum(sum(with_sin), axis=0, keepdims=True))


def triple(rows, ref, name):
    return cat([rows.get(ref, "%s%d" % (name, c)) for c in range(3)], 1)


def thirds(value):
    n = value.shape[1] // 3
    return [value[:, c * n : (c + 1) * n] for c in range(3)]


def force_body(
    types, depth, near, far, from_near, from_far, own_rows, index, masks, features, colmat, nh, nl, wh, wl,
    near_out, far_out, pool, save, groups, scratch,
):
    lanes = own_rows.shape[1]
    for j in range(4):
        pool[j, :, :] = whole((near, far, from_near, from_far), j)
    slots = index.shape[0] - 8
    feat = features.shape[0]
    rows = saved_rows(feat, types, slots)
    narrow = narrow_rows(feat)
    wide = wide_rows(feat, types)
    code = index[0:slots, :]
    mask = masks[0:slots, :]
    live = masks[slots : slots + 1, :]

    def coords(j, c):
        shift = pool_offsets(j, lanes)[c]
        row = pool[j, c : c + 1, :]
        return row if shift is None else row + shift

    deltas, radius = pool_deltas(coords, lambda c: own_rows[c : c + 1, :], code, lanes, depth)
    kinds = from_pool([pool[j, 7:8, :] for j in range(4)], code, lanes)
    inside = jnp.where(radius < cutoff, mask, 0.0)
    theta = omega * jnp.minimum(radius, cutoff)
    c1, s1 = jnp.cos(theta), jnp.sin(theta)
    ir = 1.0 / radius
    env = 0.5 * (c1 + 1.0) * inside
    e = env * ir
    e1 = ((-0.5 * omega) * s1 * inside - e) * ir
    e2 = ((-0.5 * omega * omega) * c1 * inside - 2.0 * e1) * ir
    unit = [d * ir for d in deltas]
    for name, value in (("e", e), ("e1", e1), ("e2", e2), ("ir", ir), ("t", kinds)):
        rows.put(save, name, value)
    for c in range(3):
        rows.put(save, "u%d" % c, unit[c])
    sin_at, cos_at = rows.at["sin"][0], rows.at["cos"][0]
    multiples(c1, s1, save.at[sin_at : sin_at + slots * USED, :], save.at[cos_at : cos_at + slots * USED, :], slots)

    def read_sin(k):
        return save[sin_at + k * USED : sin_at + (k + 1) * USED, :]

    def read_cos(k):
        return save[cos_at + k * USED : cos_at + (k + 1) * USED, :]

    coefs = [e] + [e * u for u in unit]
    mask_at = rows.at["mask"][0]

    def put_mask(i, value):
        save[mask_at + 8 * i : mask_at + 8 * i + 8, :] = value

    type_masks(kinds, types, put_mask)

    def read_mask(i):
        return save[mask_at + 8 * i : mask_at + 8 * i + 8, :]

    slot_sums(read_sin, read_cos, coefs, None, read_mask, slots, types, lambda q, v: rows.put(save, "A%d" % q, v))

    def nw(name):
        return narrow.get(nh, name), narrow.get(nl, name)

    def wd(name, first=None, last=None, rsl=slice(None)):
        return tuple(wide.get(r, name)[rsl, first:last] for r in (wh, wl))

    a0 = split(rows.get(save, "A0"))
    av = split(cat([rows.get(save, "A%d" % q) for q in (1, 2, 3)], 1))
    s_one = features[...] + dot3(wd("BT", rsl=slice(0, feat)), a0)
    v = dot3(wd("BT", rsl=slice(feat, 2 * feat)), av)
    uw = dot3(nw("RQT"), split(v))
    turned, mirrored = thirds(uw[0:feat]), thirds(uw[feat : 2 * feat])
    q = turned[0] * mirrored[0] + turned[1] * mirrored[1] + turned[2] * mirrored[2]
    n = jnp.sqrt(mirrored[0] * mirrored[0] + mirrored[1] * mirrored[1] + mirrored[2] * mirrored[2] + 1.0)
    joined = cat([s_one, n], 0)
    h = dot3(wd("CT"), split(joined))
    gate = lax.logistic(h)
    z = h * gate
    dz = gate * (1.0 + h * (1.0 - gate))
    d2z = gate * (1.0 - gate) * (2.0 + h * (1.0 - 2.0 * gate))
    a = dot3(nw("ST"), split(z))
    a2 = a[feat : 2 * feat]
    s_two = s_one + a[0:feat] + a2 * q
    y = dot3(nw("RT"), split(s_two))
    gate = lax.logistic(y)
    dy = gate * (1.0 + y * (1.0 - gate))
    d2y = gate * (1.0 - gate) * (2.0 + y * (1.0 - 2.0 * gate))
    ldy = dy * live
    yb = colmat[...] * ldy
    s2b = dot3(nw("R"), split(yb))
    ab = cat([s2b, s2b * q], 0)
    qb = s2b * a2
    zb = dot3(wd("S"), split(ab))
    hb = zb * dz
    jb = dot3(nw("C"), split(hb))
    s1b = s2b + jb[0:feat]
    nbn = jb[feat : 2 * feat] / n
    uwb = cat(
        [
            cat([qb * mirrored[c] for c in range(3)], 1),
            cat([nbn * mirrored[c] + qb * turned[c] for c in range(3)], 1),
        ],
        0,
    )
    vb = dot3(wd("RQ"), split(uwb))
    for name, value in (
        ("joined", joined), ("ab", ab), ("z", z), ("dz", dz), ("d2z", d2z), ("a2", a2), ("q", q), ("n", n),
        ("s2", s_two), ("yb", yb), ("yc", colmat[...] * live * d2y), ("ldy", ldy), ("s2b", s2b), ("zb", zb),
        ("hb", hb), ("qb", qb), ("nbn", nbn), ("s1b", s1b),
    ):
        rows.put(save, name, value)
    for name, value in (("v", v), ("uw", uw), ("uwb", uwb), ("vb", vb)):
        for c, part in enumerate(thirds(value)):
            rows.put(save, "%s%d" % (name, c), part)
    ab0 = dot3(wd("B", 0, feat), split(s1b))
    abv = thirds(dot3(wd("B", feat, 2 * feat), split(vb)))

    def put(name, q, k, row):
        start = rows.at["%s%d" % (name, q)][0] + k
        save[start : start + 1, :] = row

    tables = [ab0] + abv
    slot_reads(lambda q: tables[q], kinds, read_sin, read_cos, slots, types, put, True)
    sa = [rows.get(save, "sa%d" % q) for q in range(4)]
    sb = [rows.get(save, "sb%d" % q) for q in range(4)]
    z_sum = unit[0] * sa[1] + unit[1] * sa[2] + unit[2] * sa[3]
    x_sum = sb[0] + unit[0] * sb[1] + unit[1] * sb[2] + unit[2] * sb[3]
    rb = e * x_sum + e1 * (sa[0] + z_sum) - ir * e * z_sum
    deltas_bar = [rb * unit[c] + e * ir * sa[c + 1] for c in range(3)]
    pool_partials(deltas_bar, code, lambda j: index[slots + j : slots + j + 1, :], (near_out, far_out), groups, scratch, lanes)


def centres_of(bins, bin_total):
    return 0.1 * jnp.sqrt(3600.0 * (bins.astype(f32) + 0.5) / bin_total)


def hist_body(
    depth, bin_total, pool, near, far, from_near, from_far, index, masks, bins,
    next_own, slopes, hist, moved, scratch,
):
    lanes = pool.shape[2]
    slots = index.shape[0] - 8
    code = index[0:slots, :]
    inverse = index[slots + 4 : slots + 5, :]
    mask = masks[0:slots, :]
    for j in range(4):
        kick = (0.5 * time_step * time_step) * pool[j, 6:7, :]
        force = whole((near, far, from_near, from_far), j)
        moved[j, 0:3, :] = pool[j, 0:3, :] + time_step * pool[j, 3:6, :] - kick * force[0:3, :]
    inverse8 = jnp.broadcast_to(inverse, (8, lanes))
    own = []
    for c in range(3):
        row = from_pool([moved[j, c : c + 1, :] for j in range(4)], inverse8, lanes)[0:1, :]
        next_own[c : c + 1, :] = row
        own.append(row)

    def coords(j, c):
        shift = pool_offsets(j, lanes)[c]
        row = moved[j, c : c + 1, :]
        return row if shift is None else row + shift

    deltas, radius = pool_deltas(coords, lambda c: own[c], code, lanes, depth)
    gap = radius - centres_of(bins[...], bin_total)
    kernel = jnp.exp(-gap * gap / sigma_two) * mask
    scale = kernel * gap * (-2.0 / sigma_two) / radius
    for c in range(3):
        slopes[c * slots : (c + 1) * slots, :] = scale * deltas[c]
    sums = scatter_lanes([kernel], bins[...], scratch, bin_total)
    hist[...] = jnp.broadcast_to(sums[0:1, :], hist.shape)


def adjoint_body(atoms_total, hists, target, slopes, index, bins, near, far, groups, scratch):
    lanes = bins.shape[1]
    slots = bins.shape[0]
    code = index[0:slots, :]
    total = jnp.sum(hists[...], axis=0, keepdims=True)
    weights = 2.0 * (total / atoms_total - target[...]) / atoms_total
    picked = lane_take(weights, bins[...])
    deltas_bar = [picked * slopes[c * slots : (c + 1) * slots, :] for c in range(3)]
    pool_partials(deltas_bar, code, lambda j: index[slots + j : slots + j + 1, :], (near, far), groups, scratch, lanes)


def grads_body(
    types, pool, near, far, from_near, from_far, index, save, colmat, phi, filt, nh, nl, wh, wl,
    keep, send, adjoint, after, tangents, grads,
):
    lanes = pool.shape[2]
    slots = index.shape[0] - 8
    feat = colmat.shape[0]
    rows = saved_rows(feat, types, slots)
    narrow = narrow_rows(feat)
    wide = wide_rows(feat, types)
    code = index[0:slots, :]
    inverse8 = jnp.broadcast_to(index[slots + 4 : slots + 5, :], (8, lanes))

    def get(name):
        return rows.get(save, name)

    for j in range(4):
        adjoint[j, :, :] = whole((near, far, from_near, from_far), j)
    probe = [
        [(0.5 * time_step * time_step) * pool[j, 6:7, :] * adjoint[j, c : c + 1, :] for j in range(4)]
        for c in range(3)
    ]
    moves = [
        from_pool(probe[c], code, lanes) - from_pool(probe[c], inverse8, lanes)[0:1, :] for c in range(3)
    ]
    e, e1, e2, ir, kinds = get("e"), get("e1"), get("e2"), get("ir"), get("t")
    unit = [get("u%d" % c) for c in range(3)]
    dr = unit[0] * moves[0] + unit[1] * moves[1] + unit[2] * moves[2]
    du = [(moves[c] - unit[c] * dr) * ir for c in range(3)]
    de = e1 * dr
    sin_at, cos_at = rows.at["sin"][0], rows.at["cos"][0]

    def read_sin(k):
        return save[sin_at + k * USED : sin_at + (k + 1) * USED, :]

    def read_cos(k):
        return save[cos_at + k * USED : cos_at + (k + 1) * USED, :]

    k_rows = STRIDE * types

    def put_sum(q, value):
        tangents[q * k_rows : (q + 1) * k_rows, :] = value

    sin_coef = [de] + [de * unit[c] + e * du[c] for c in range(3)]
    cos_coef = [e * dr] + [e * dr * unit[c] for c in range(3)]
    mask_at = rows.at["mask"][0]

    def read_mask(i):
        return save[mask_at + 8 * i : mask_at + 8 * i + 8, :]

    slot_sums(read_sin, read_cos, sin_coef, cos_coef, read_mask, slots, types, put_sum)

    def nw(name):
        return narrow.get(nh, name), narrow.get(nl, name)

    def wd(name, first=None, last=None, rsl=slice(None)):
        return tuple(wide.get(r, name)[rsl, first:last] for r in (wh, wl))

    da_zero = tangents[0:k_rows, :]
    da_vec = cat([tangents[q * k_rows : (q + 1) * k_rows, :] for q in (1, 2, 3)], 1)
    ds1 = dot3(wd("BT", rsl=slice(0, feat)), split(da_zero))
    dv = dot3(wd("BT", rsl=slice(feat, 2 * feat)), split(da_vec))
    duw = dot3(nw("RQT"), split(dv))
    d_turn, d_mirr = thirds(duw[0:feat]), thirds(duw[feat : 2 * feat])
    turned = [get("uw%d" % c)[0:feat] for c in range(3)]
    mirrored = [get("uw%d" % c)[feat : 2 * feat] for c in range(3)]
    q, n, a2, dz, d2z = get("q"), get("n"), get("a2"), get("dz"), get("d2z")
    s2b, zb, qb, nbn = get("s2b"), get("zb"), get("qb"), get("nbn")
    dq = sum(d_turn[c] * mirrored[c] + turned[c] * d_mirr[c] for c in range(3))
    dn = sum(mirrored[c] * d_mirr[c] for c in range(3)) / n
    dj = cat([ds1, dn], 0)
    dh = dot3(wd("CT"), split(dj))
    dzt = dz * dh
    da = dot3(nw("ST"), split(dzt))
    da2 = da[feat : 2 * feat]
    ds2 = ds1 + da[0:feat] + da2 * q + a2 * dq
    dyt = dot3(nw("RT"), split(ds2))
    dyb = get("yc") * dyt
    ds2b = dot3(nw("R"), split(dyb))
    dab = cat([ds2b, ds2b * q + s2b * dq], 0)
    dqb = ds2b * a2 + s2b * da2
    dzb = dot3(wd("S"), split(dab))
    dhb = dzb * dz + zb * (d2z * dh)
    djb = dot3(nw("C"), split(dhb))
    ds1b = ds2b + djb[0:feat]
    dnbn = (djb[feat : 2 * feat] - nbn * dn) / n
    duwb = cat(
        [
            cat([dqb * mirrored[c] + qb * d_mirr[c] for c in range(3)], 1),
            cat(
                [
                    dnbn * mirrored[c] + nbn * d_mirr[c] + dqb * turned[c] + qb * d_turn[c]
                    for c in range(3)
                ],
                1,
            ),
        ],
        0,
    )
    dvb = dot3(wd("RQ"), split(duwb))

    def both(first, second, third, fourth):
        return -dot3(split(cat([first, second], 1)), split(cat([third, fourth], 1)), NT)

    parts = grads.shape[0]
    share = feat // parts
    rq = both(dv, triple(rows, save, "v"), triple(rows, save, "uwb"), duwb)
    cg = both(dj, get("joined"), get("hb"), dhb)
    sg = both(dzt, get("z"), get("ab"), dab)
    rg = both(ds2, get("s2"), get("yb"), dyb)
    bs = both(da_zero, get("A0"), get("s1b"), ds1b)
    bv = both(da_vec, cat([get("A%d" % i) for i in (1, 2, 3)], 1), triple(rows, save, "vb"), dvb)
    low, high = split(get("ldy") * dyt)
    ones = jnp.ones((16, lanes), bf16)
    col = -(dot1(ones, low, NT) + dot1(ones, high, NT))
    fg, pg = [], []
    for half, value in enumerate((bs, bv)):
        cols = slice(half * feat, (half + 1) * feat)
        total = None
        for t in range(types):
            block = value[STRIDE * t : STRIDE * t + USED, :]
            term = block * phi[t : t + 1, cols]
            total = term if total is None else total + term
            pg.append((half, t, jnp.sum(block * filt[0:USED, cols], axis=0, keepdims=True)))
        fg.append(total)
    base = 7 * share
    place = iota((10, lanes), 1)
    for part in range(parts):
        mine = slice(part * share, (part + 1) * share)
        grads[part, 0:share, :] = rq[mine, 0:feat]
        grads[part, share : 2 * share, :] = rq[mine, feat : 2 * feat]
        grads[part, 2 * share : 4 * share, :] = cg[2 * part * share : 2 * (part + 1) * share, :]
        grads[part, 4 * share : 5 * share, :] = sg[mine, 0:feat]
        grads[part, 5 * share : 6 * share, :] = sg[mine, feat : 2 * feat]
        grads[part, 6 * share : 7 * share, :] = rg[mine, :]
        for half, t, row in pg:
            at = base + half * types + t
            grads[part, at : at + 1, :] = row
        chosen = fg[part // 2]
        rolled = pltpu.roll(chosen, feat // 2, 1)
        here, there = (chosen, rolled) if part % 2 == 0 else (rolled, chosen)
        at = base + 2 * types
        grads[part, at : at + 10, :] = jnp.where(place < feat // 2, here[0:10, :], there[10:20, :])
        grads[part, at + 10 : at + 11, :] = col[0:1, :]
        grads[part, at + 11 :, :] = jnp.zeros((grads.shape[1] - at - 11, lanes), f32)

    odd = lax.axis_index("slab") % 2
    half = grads.shape[1] // 2
    keep[...] = grads[:, pl.ds(pl.multiple_of(odd * half, half), half), :]
    send[...] = grads[:, pl.ds(pl.multiple_of((1 - odd) * half, half), half), :]
    for c in range(3):
        after[c * slots : (c + 1) * slots, :] = du[c]
        after[4 * slots + (c + 1) * feat : 4 * slots + (c + 2) * feat, :] = dvb[:, c * lanes : (c + 1) * lanes]
    after[3 * slots : 4 * slots, :] = dr
    after[4 * slots : 4 * slots + feat, :] = ds1b


def moves_body(types, index, save, after, wh, wl, near, far, sums, groups, scratch):
    lanes = index.shape[1]
    slots = index.shape[0] - 8
    feat = lanes
    rows = saved_rows(feat, types, slots)
    wide = wide_rows(feat, types)
    code = index[0:slots, :]

    def get(name):
        return rows.get(save, name)

    def wd(name, first, last):
        return tuple(wide.get(r, name)[:, first:last] for r in (wh, wl))

    e, e1, e2, ir, kinds = get("e"), get("e1"), get("e2"), get("ir"), get("t")
    unit = [get("u%d" % c) for c in range(3)]
    du = [after[c * slots : (c + 1) * slots, :] for c in range(3)]
    dr = after[3 * slots : 4 * slots, :]
    de, de1, dir_ = e1 * dr, e2 * dr, -ir * ir * dr
    sin_at, cos_at = rows.at["sin"][0], rows.at["cos"][0]

    def read_sin(k):
        return save[sin_at + k * USED : sin_at + (k + 1) * USED, :]

    def read_cos(k):
        return save[cos_at + k * USED : cos_at + (k + 1) * USED, :]

    ds1b = after[4 * slots : 4 * slots + feat, :]
    dvb = cat([after[4 * slots + (c + 1) * feat : 4 * slots + (c + 2) * feat, :] for c in range(3)], 1)
    dab0 = dot3(wd("B", 0, feat), split(ds1b))
    dabv = thirds(dot3(wd("B", feat, 2 * feat), split(dvb)))
    tables = [dab0] + dabv

    def put(name, q, k, row):
        start = (0 if name == "sa" else 4 * slots) + q * slots + k
        sums[start : start + 1, :] = row

    slot_reads(lambda q: tables[q], kinds, read_sin, read_cos, slots, types, put, False)
    sa = [get("sa%d" % q) for q in range(4)]
    sb = [get("sb%d" % q) for q in range(4)]
    sd = [get("sd%d" % q) for q in range(4)]
    dsa = [sb[q] * dr + sums[q * slots : (q + 1) * slots, :] for q in range(4)]
    dsb = [
        sums[(4 + q) * slots : (5 + q) * slots, :] - sd[q] * dr for q in range(4)
    ]
    z_sum = sum(unit[c] * sa[c + 1] for c in range(3))
    x_sum = sb[0] + sum(unit[c] * sb[c + 1] for c in range(3))
    dz_sum = sum(du[c] * sa[c + 1] + unit[c] * dsa[c + 1] for c in range(3))
    dx_sum = dsb[0] + sum(du[c] * sb[c + 1] + unit[c] * dsb[c + 1] for c in range(3))
    rb = e * x_sum + e1 * (sa[0] + z_sum) - ir * e * z_sum
    drb = (
        de * x_sum + e * dx_sum + de1 * (sa[0] + z_sum) + e1 * (dsa[0] + dz_sum)
        - (dir_ * e + ir * de) * z_sum - ir * e * dz_sum
    )
    deltas_bar = [
        drb * unit[c] + rb * du[c] + (de * ir + e * dir_) * sa[c + 1] + e * ir * dsa[c + 1]
        for c in range(3)
    ]
    pool_partials(deltas_bar, code, lambda j: index[slots + j : slots + j + 1, :], (near, far), groups, scratch, lanes)


def last_body(
    types, parts, atoms_total, mine, other, adjoint, near, far, index, slope, hidden_t, table_t, spreader, next_own,
    next_out, adj, enc, spr, fil, rot, ref, com, spl, rea, col, total,
):
    next_out[...] = next_own[...]
    odd = lax.axis_index("slab") % 2
    half = mine.shape[0]
    total[pl.ds(pl.multiple_of(odd * half, half), half), :] = mine[...]
    total[pl.ds(pl.multiple_of((1 - odd) * half, half), half), :] = other[...]
    lanes = adjoint.shape[2]
    slots = index.shape[0] - 8
    feat = lanes
    share = feat // parts
    inverse8 = jnp.broadcast_to(index[slots + 4 : slots + 5, :], (8, lanes))
    crossed = parity("cross")
    near_v, far_v = near[...], far[...]
    second = (jnp.where(crossed, near_v, far_v), jnp.where(crossed, far_v, near_v))
    for c in range(3):
        rows = [
            atoms_total * (adjoint[j, c : c + 1, :] - second[j % 2][j // 2, c : c + 1, :]) for j in range(4)
        ]
        adj[c : c + 1, :] = from_pool(rows, inverse8, lanes)[0:1, :]
    rot[...] = total[0:share, :]
    ref[...] = total[share : 2 * share, :]
    com[...] = total[2 * share : 4 * share, :]
    spl[:, 0:feat] = total[4 * share : 5 * share, :]
    spl[:, feat : 2 * feat] = total[5 * share : 6 * share, :]
    rea[...] = total[6 * share : 7 * share, :]
    base = 7 * share
    phib = cat([total[base : base + types, :], total[base + types : base + 2 * types, :]], 1)
    at = base + 2 * types
    block = total[at : at + 10, :]
    fil[0:10, :] = block[:, 0 : feat // 2]
    fil[10:20, :] = pltpu.roll(block, feat // 2, 1)[:, 0 : feat // 2]
    col_row = total[at + 10 : at + 11, :]
    spare = jnp.zeros((types, 2 * feat), f32)
    pre_bar = dot3(split(cat([phib, spare], 0)), split(spreader[...]), NT)[0:types] * slope[...]
    here = pl.ds(pl.multiple_of(lax.axis_index("cross") * share, share), share)
    rest = jnp.zeros((lanes - types, feat), f32)
    spr[...] = dot3(split(hidden_t[here, :]), split(cat([phib, cat([rest, rest], 1)], 0)))
    enc[...] = dot3(split(table_t[here, :]), split(cat([pre_bar, rest], 0)))
    for part in range(parts):
        @pl.when(lax.axis_index("cross") == part)
        def _():
            col[...] = col_row[:, part * share : (part + 1) * share]


def neighbours_swap(near, far, axis):
    count = lax.axis_size(axis)
    forward = [(i, (i + 1) % count) for i in range(count)]
    pairs = [[p for a, b in forward if a % 2 == side for p in ((a, b), (b, a))] for side in (0, 1)]
    from_far = lax.ppermute(far, axis, pairs[1])
    from_near = lax.ppermute(near, axis, pairs[0])
    return from_near, from_far


def corner_sum(near, far):
    near, far = call(turn_body, [(near.shape, f32)] * 2, near, far, *neighbours_swap(near, far, "slab"))
    return (near, far) + neighbours_swap(near, far, "cross")


def swap(x, axis, bit):
    return lax.ppermute(x, axis, [(i, i ^ bit) for i in range(lax.axis_size(axis))])


def add_body(x, other, out):
    out[...] = x[...] + other[...]


def add_all_body(*refs):
    total = refs[0][...]
    for ref in refs[1:-1]:
        total = total + ref[...]
    refs[-1][...] = total


def spread_body(x, other, near, far, *outs):
    me = lax.axis_index("cross")
    for step, ref in enumerate(outs[:-2]):
        part = pl.ds(me ^ step, 1)
        ref[...] = (x[part] + other[part]).reshape(ref.shape)
    outs[-2][...] = near[...]
    outs[-1][...] = far[...]


def gather_turn_body(near, far, from_near, from_far, *refs):
    add_all_body(*refs[:-2])
    turn_body(near, far, from_near, from_far, refs[-2], refs[-1])


def gather_sides_body(near, far, from_near, from_far, *refs):
    add_all_body(*refs[:-2])
    add_body(near, from_near, refs[-2])
    add_body(far, from_far, refs[-1])


def reduce_all(keep, send, near, far):
    slab_count, cross_count = lax.axis_size("slab"), lax.axis_size("cross")
    group, part = (near.shape, f32), (keep.shape[1:], f32)
    *shares, near, far = call(
        spread_body, [part] * cross_count + [group] * 2, keep, swap(send, "slab", 1), near, far
    )
    got = [swap(shares[step], "cross", step) for step in range(1, cross_count)]
    received = neighbours_swap(near, far, "slab")
    x, near, far = call(gather_turn_body, [part, group, group], near, far, *received, shares[0], *got)
    received = neighbours_swap(near, far, "cross")
    bits = [2**b for b in range(1, slab_count.bit_length()) if 2**b < slab_count]
    sides = None
    for i in range(0, len(bits), 2):
        pair = bits[i : i + 2]
        steps = pair + [sum(pair)] * (len(pair) - 1)
        parts = [x] + [swap(x, "slab", step) for step in steps]
        if sides is None:
            x, *sides = call(gather_sides_body, [part, group, group], near, far, *received, *parts)
        else:
            (x,) = call(add_all_body, [part], *parts)
    return x, swap(x, "slab", 1), sides


def device_step(
    positions, velocities, inverse_mass, species, type_table, neighbours, slot_count, atom_count,
    pair_bins, send_list, target, encoder, spreader, filters, rotator, reflector, combiner, splitter,
    readout, collector,
):
    lanes = positions.shape[1]
    slots = neighbours.shape[1]
    types, feat = type_table.shape
    bin_total = target.shape[0]
    slab_count, cross_count = lax.axis_size("slab"), lax.axis_size("cross")
    devices = slab_count * cross_count
    atoms_total = float(lanes * devices)
    depth = 1.6 * (lanes // 16)
    parts = cross_count
    row = lambda x: x.reshape(1, x.shape[0])
    i32 = jnp.int32
    vm, dma = pltpu.VMEM, pltpu.SemaphoreType.DMA
    narrow, wide = narrow_rows(feat).total, wide_rows(feat, types).total
    group = ((2, 8, lanes), f32)
    pool_shape = ((4, 8, lanes), f32)
    pair_scratch = vm((16 * slots, lanes), f32)
    near, far, own_rows, send = call(
        offer_body, [group, group, ((8, lanes), f32), ((8, lanes), i32)],
        *in_hbm(positions, velocities, row(inverse_mass), row(species), send_list),
        specs=[HB] * 5,
        scratch=[
            vm((3, lanes), f32), vm((3, lanes), f32), vm((1, lanes), f32), vm((1, lanes), i32),
            vm(send_list.shape, i32), vm((4, 8, lanes), f32), dma((5,)),
        ],
    )
    colmat, nh, nl, wh, wl, phi, slope, hidden_t, table_t, filt, spreader_in = call(
        weights_body,
        [
            ((feat, lanes), f32), ((narrow, feat), bf16), ((narrow, feat), bf16), ((wide, 2 * feat), bf16),
            ((wide, 2 * feat), bf16), ((types, 2 * feat), f32), ((types, feat), f32), ((feat, lanes), f32),
            ((feat, lanes), f32), ((STRIDE, 2 * feat), f32), (spreader.shape, f32),
        ],
        *in_hbm(
            type_table, encoder, spreader, filters, rotator, reflector, combiner, splitter, readout,
            row(collector),
        ),
        specs=[HB] * 10,
        scratch=[
            vm(type_table.shape, f32), vm(encoder.shape, f32), vm(filters.shape, f32), vm(rotator.shape, f32),
            vm(reflector.shape, f32), vm(combiner.shape, f32), vm(splitter.shape, f32), vm(readout.shape, f32),
            vm((1, feat), f32), dma((10,)),
        ],
    )
    index, masks, features, bins, goal = call(
        index_body,
        [
            ((slots + 8, lanes), i32), ((slots + 8, lanes), f32), ((feat, lanes), f32), ((slots, lanes), i32),
            ((1, bin_total), f32),
        ],
        *in_hbm(neighbours.T, row(slot_count), pair_bins.T, row(target)),
        atom_count, send, own_rows, table_t,
        specs=[HB] * 4 + [SM] + [VM] * 3,
        scratch=[vm((slots, lanes), i32), vm((1, lanes), i32), dma((4,))],
    )
    pieces = corner_sum(near, far)
    save_rows = saved_rows(feat, types, slots).total
    near, far, pool, save = call(
        functools.partial(force_body, types, depth),
        [group, group, pool_shape, ((save_rows, lanes), f32)],
        *pieces, own_rows, index, masks, features, colmat, nh, nl, wh, wl,
        scratch=[vm((4, 8, lanes), f32), pair_scratch],
    )
    pieces = corner_sum(near, far)
    next_positions, slopes, hist = call(
        functools.partial(hist_body, depth, bin_total),
        [((3, lanes), f32), ((3 * slots, lanes), f32), ((devices, bin_total), f32)],
        pool, *pieces, index, masks, bins,
        scratch=[vm((4, 8, lanes), f32), pair_scratch],
    )
    hists = lax.all_to_all(hist.reshape(devices, 1, bin_total), ("slab", "cross"), 0, 0)
    near, far = call(
        functools.partial(adjoint_body, atoms_total), [group, group],
        hists.reshape(devices, bin_total), goal, slopes, index, bins,
        scratch=[vm((4, 8, lanes), f32), pair_scratch],
    )
    pieces = corner_sum(near, far)
    half_grads = ((parts, feat, lanes), f32)
    keep, send, adjoint, after = call(
        functools.partial(grads_body, types),
        [half_grads, half_grads, pool_shape, ((4 * slots + 4 * feat, lanes), f32)],
        pool, *pieces, index, save, colmat, phi, filt, nh, nl, wh, wl,
        scratch=[vm((4 * STRIDE * types, lanes), f32), vm((parts, 2 * feat, lanes), f32)],
    )
    near, far = call(
        functools.partial(moves_body, types), [group, group], index, save, after, wh, wl,
        scratch=[vm((8 * slots, lanes), f32), vm((4, 8, lanes), f32), pair_scratch],
    )
    mine, other, sides = reduce_all(keep, send, near, far)
    share = feat // parts
    results = call(
        functools.partial(last_body, types, parts, atoms_total),
        [
            ((3, lanes), f32), ((3, lanes), f32), ((share, feat), f32), ((share, 2 * feat), f32),
            ((filters.shape[0], 2 * feat // parts), f32), ((share, feat), f32), ((share, feat), f32),
            ((2 * share, feat), f32), ((share, 2 * feat), f32), ((share, feat), f32), ((1, share), f32),
        ],
        mine, other, adjoint, *sides, index, slope, hidden_t, table_t, spreader_in, next_positions,
        scratch=[vm((2 * feat, lanes), f32)],
        keep=False,
    )
    return tuple(results[:10]) + (results[10].reshape(share),)


def solution(mesh):
    both = ("slab", "cross")
    in_specs = (
        P(None, both), P(None, both), P(both), P(both), P(), P(both, None), P(both), P(both), P(both, None),
        P("slab", "cross", None),
    ) + (P(),) * 10
    out_specs = (
        P(None, both), P(None, both), P("cross", None), P("cross", None), P(None, "cross"), P("cross", None),
        P("cross", None), P("cross", None), P("cross", None), P("cross", None), P("cross"),
    )
    return jax.shard_map(device_step, mesh=mesh, in_specs=in_specs, out_specs=out_specs, check_vma=False)
```
